32 devices in a mesh: region: 4 (over x, core), sector: 8 (over z, y).
Axes of the slice: x: 2, y: 2, z: 4, core: 2. Of those that a mesh axis runs over, the one named last changes fastest.
Arguments:
- env_left: bfloat16 [4, 8, 2048, 2048], P('region', None, 'sector'), may hold values from -6 to 6
- site_tensor: bfloat16 [4, 2048, 2, 2048], P('region', 'sector'), may hold values from -0.125 to 0.125
- mpo_tensor: float32 [4, 8, 8, 2, 2], P('region'), may hold values from -1 to 1
- env_right: bfloat16 [4, 8, 2048, 2048], P('region', None, 'sector'), may hold values from -0.046875 to 0.046875
- bond_tensor: bfloat16 [4, 2048, 2048], P('region'), may hold values from -0.125 to 0.125
Outputs:
- env_next: bfloat16 [4, 8, 2048, 2048], P('region', None, 'sector')
- bond_image: bfloat16 [4, 2048, 2048], P('region', 'sector')
The draws below stay inside these ranges and needn't reach their ends.
All inputs are finite; a program needn't handle non-finite values.
Results may differ from the reference program's by a relative error of at most 0.0065.
Values may be sent and summed in bfloat16 or wider, within the bound.
A program may use at most 192 MiB of HBM per device.

```python
import jax
import jax.numpy as jnp
from jax import lax

CHI = 2048
W = 8
D_PHYS = 2
NREG = 4
N_REGION = 4


def level_of(own_key, dims, split, least, top_value):
    def one(position, shards_of):
        steps = jax.random.uniform(jax.random.fold_in(jax.random.fold_in(own_key, 6), position), (shards_of,), jnp.float32, least / len(split), top_value / len(split))
        return jnp.repeat(jnp.exp(steps), dims[position] // shards_of).reshape((-1,) + (1,) * (len(dims) - position - 1))

    factor_of = one(*split[0])
    for cut in split[1:]:
        factor_of = factor_of * one(*cut)
    return factor_of


def gaussian(rng, dims, scale, most, shards=(), dtype=jnp.bfloat16):
    values = jax.random.normal(rng, dims, jnp.float32) * scale
    if len(shards) > 0:
        values = level_of(rng, dims, shards, -0.22, 0.18) * values
    return jnp.clip(values, min=-most, max=most).astype(dtype)


def setup_inputs(seed: int = 0) -> dict:
    arg_keys = jax.random.split(jax.random.key(seed), 6)
    env_left = gaussian(arg_keys[0], (NREG, W, CHI, CHI), 1.0, 6.0, ((0, 4), (2, 8)))
    site_tensor = gaussian(arg_keys[1], (NREG, CHI, D_PHYS, CHI), CHI ** -0.5, 0.125, ((0, 4), (1, 8)))
    mpo_tensor = gaussian(arg_keys[2], (NREG, W, W, D_PHYS, D_PHYS), (W * D_PHYS * D_PHYS) ** -0.5, 1.0, ((0, 4),), jnp.float32)
    env_right = gaussian(arg_keys[3], (NREG, W, CHI, CHI), (CHI * W) ** -0.5, 0.046875, ((0, 4), (2, 8)))
    bond_tensor = gaussian(arg_keys[4], (NREG, CHI, CHI), CHI ** -0.5, 0.125, ((0, 4),))
    return dict(env_left=env_left, site_tensor=site_tensor, mpo_tensor=mpo_tensor, env_right=env_right, bond_tensor=bond_tensor)


def reference(env_left, site_tensor, mpo_tensor, env_right, bond_tensor):
    env_list = []
    image_list = []
    for region_id in range(N_REGION):
        site_whole = site_tensor[region_id].astype(jnp.float32)
        half_done = jnp.einsum("wak,ksc->wasc", env_left[region_id].astype(jnp.float32), site_whole)
        carried = jnp.einsum("vwst,vatc->wsac", mpo_tensor[region_id], half_done, precision=lax.Precision.HIGHEST).astype(jnp.bfloat16)
        env_new = jnp.einsum("wsac,asb->wcb", carried.astype(jnp.float32), site_whole).astype(jnp.bfloat16)
        right_next = env_right[(region_id + 1) % N_REGION].astype(jnp.float32)
        bond_right = jnp.einsum("wbc,kc->wbk", right_next, bond_tensor[region_id].astype(jnp.float32)).astype(jnp.bfloat16)
        image_new = jnp.einsum("wka,wbk->ab", env_new.astype(jnp.float32), bond_right.astype(jnp.float32)).astype(jnp.bfloat16)
        env_list.append(env_new)
        image_list.append(image_new)
    return jnp.stack(env_list), jnp.stack(image_list)
```

```python
import functools

import jax
import jax.numpy as jnp
from jax import lax
from jax.experimental import pallas as pl
from jax.experimental.pallas import tpu as pltpu
from jax.sharding import PartitionSpec as P


GROUP = 16
LANES = 128
CHUNKS = 2
SHIFTS = 4
VMEM_LIMIT = 60 * 1024 * 1024


def shifted(block, axis, distance):
    devices = range(lax.axis_size(axis))
    route = [((i - distance) % len(devices), i) for i in devices]
    return lax.ppermute(block, axis, route)


def swap(blocks):
    return lax.all_to_all(blocks, "sector", split_axis=0, concat_axis=0, tiled=True)


MESH = pl.DeviceIdType.MESH


def carried_body(mix_ref, env_ref, site_ref, *out_refs):
    width, rows, bond = env_ref.shape
    _, states, _, columns = site_ref.shape
    mix = mix_ref[...]
    mix_high = mix.astype(jnp.bfloat16)
    mix_low = (mix - mix_high.astype(jnp.float32)).astype(jnp.bfloat16)
    env = env_ref[...].reshape(width * rows, bond)
    half_done = [
        jnp.dot(env, site_ref[:, t].reshape(bond, columns), preferred_element_type=jnp.float32)
        .reshape(width, rows, columns)
        for t in range(states)
    ]
    dot = functools.partial(jnp.dot, preferred_element_type=jnp.float32)
    for g in range(rows // GROUP):
        span = slice(g * GROUP, (g + 1) * GROUP)
        x = jnp.concatenate(
            [h[:, span].reshape(width * GROUP, columns) for h in half_done], axis=0
        )
        high = x.astype(jnp.bfloat16)
        low = (x - high.astype(jnp.float32)).astype(jnp.bfloat16)
        y = dot(mix_high, high) + dot(mix_high, low) + dot(mix_low, high)
        y = y.astype(jnp.bfloat16).reshape(width, states, GROUP, columns)
        step = width // len(out_refs)
        for i, out_ref in enumerate(out_refs):
            out_ref[0, :, :, span, :] = y[i * step : (i + 1) * step]


def head_kernel(
    mix_ref, right_hbm, site_hbm, bond_hbm, left_hbm,
    gathered, moved, *rest,
):
    carried = rest[:CHUNKS]
    (right, bond_ref, blocks, own_site, shift_send, shift_recv, site_send, site_recv,
     block_send, block_recv, local_sem) = rest[CHUNKS:]
    parts, states, depth, bond = gathered.shape
    width, rows, _ = right_hbm.shape
    columns = bond // parts
    line = parts // 2
    me = lax.axis_index("sector")
    z, y = me // 2, lax.rem(me, 2)
    regions = lax.axis_size("region")
    region = lax.axis_index("region")
    before = lax.rem(region + regions - 1, regions)
    after = lax.rem(region + 1, regions)
    part_rows = rows // SHIFTS
    twin = 2 * z + 1 - y

    barrier = pltpu.get_barrier_semaphore()
    for d in range(1, parts):
        pl.semaphore_signal(
            barrier, inc=1, device_id={"sector": lax.rem(me + d, parts)}, device_id_type=MESH
        )
    for other in (before, after):
        pl.semaphore_signal(barrier, inc=1, device_id={"region": other}, device_id_type=MESH)
    pl.semaphore_wait(barrier, parts + 1)

    def shift(q):
        span = pl.ds(q * part_rows, part_rows)
        return pltpu.make_async_remote_copy(
            src_ref=right_hbm.at[:, span],
            dst_ref=right.at[:, span],
            send_sem=shift_send.at[q],
            recv_sem=shift_recv.at[q],
            device_id={"region": before},
            device_id_type=MESH,
        )

    def hop(way, source, piece, target, first=False):
        return pltpu.make_async_remote_copy(
            src_ref=site_hbm.at[piece] if first else gathered.at[source, piece],
            dst_ref=gathered.at[source, piece],
            send_sem=site_send.at[way, source, piece],
            recv_sem=site_recv.at[source, piece],
            device_id={"sector": target},
            device_id_type=MESH,
        )

    def outward(source, piece, first, ways, act):
        for way in ways:
            there = {0: me + 2, 1: me - 2, 2: twin}[way]
            if way == 2:
                act(hop(way, source, piece, there, first))
            else:
                inside = z + 1 < line if way == 0 else z >= 1

                @pl.when(inside)
                def _():
                    act(hop(way, source, piece, there, first))

    def block(q, d):
        return pltpu.make_async_remote_copy(
            src_ref=blocks.at[q, d],
            dst_ref=moved.at[me, :, pl.ds(q * part_rows, part_rows)],
            send_sem=block_send.at[q, d],
            recv_sem=block_recv.at[q, me],
            device_id={"sector": lax.rem(me + 1 + d, parts)},
            device_id_type=MESH,
        )

    def own_block(q):
        return pltpu.make_async_copy(
            blocks.at[q, parts - 1],
            moved.at[me, :, pl.ds(q * part_rows, part_rows)],
            block_send.at[q, parts - 1],
        )

    def start(copy):
        copy.start()

    for q in range(SHIFTS):
        shift(q).start()
    for piece in range(states):
        outward(me, piece, True, (0, 1, 2), start)
    load_bond = pltpu.make_async_copy(bond_hbm, bond_ref, local_sem.at[0])
    load_bond.start()
    load_site = pltpu.make_async_copy(site_hbm, own_site, local_sem.at[1])
    load_site.start()
    load_site.wait()
    keep_site = pltpu.make_async_copy(own_site, gathered.at[me], local_sem.at[1])
    keep_site.start()
    load_bond.wait()

    def product(q):
        shift(q).wait_recv()
        span = pl.ds(q * part_rows, part_rows)
        x = right[:, span].reshape(width * part_rows, bond)

        def step(d, carry):
            j = lax.rem(me + 1 + d, parts)
            out = lax.dot_general(
                x,
                bond_ref[pl.ds(pl.multiple_of(j * columns, columns), columns), :],
                (((1,), (1,)), ((), ())),
                preferred_element_type=jnp.float32,
            )
            blocks[q, d] = out.astype(jnp.bfloat16).reshape(width, part_rows, columns)

            @pl.when(d > 0)
            def _():
                block(q, d - 1).start()

            return carry

        lax.fori_loop(0, parts, step, 0)
        own_block(q).start()

    def relay(distance, piece):
        for way, source in ((0, me - 2 * distance), (1, me + 2 * distance)):
            there = z >= distance if way == 0 else z + distance < line

            @pl.when(there)
            def _():
                hop(way, source, piece, twin).wait_recv()
                outward(source, piece, False, (way, 2), start)

    ticks = [(distance, piece) for distance in range(1, line) for piece in range(states)]
    for i, (distance, piece) in enumerate(ticks):
        relay(distance, piece)
        if i < SHIFTS:
            product(i)
    for q in range(len(ticks), SHIFTS):
        product(q)
    for other in range(line):
        for piece in range(states):
            hop(2, 2 * other + 1 - y, piece, twin).wait_recv()
    keep_site.wait()

    tile = min(rows, LANES)
    pltpu.emit_pipeline(
        functools.partial(carried_body, mix_ref),
        grid=(rows // tile, parts),
        in_specs=[
            pl.BlockSpec((width, tile, bond), lambda i, j: (0, i, 0)),
            pl.BlockSpec((parts, states, depth, columns), lambda i, j: (0, 0, 0, j)),
        ],
        out_specs=[
            pl.BlockSpec((1, width // CHUNKS, states, tile, columns), lambda i, j: (j, 0, 0, i, 0))
        ] * CHUNKS,
    )(left_hbm, gathered, *carried)

    for q in range(SHIFTS):
        shift(q).wait_send()
    for piece in range(states):
        outward(me, piece, True, (0, 1, 2), lambda copy: copy.wait_send())
    for distance, piece in ticks:
        for way, source in ((0, me - 2 * distance), (1, me + 2 * distance)):
            there = z >= distance if way == 0 else z + distance < line

            @pl.when(there)
            def _():
                outward(source, piece, False, (way, 2), lambda copy: copy.wait_send())
    for q in range(SHIFTS):
        own_block(q).wait()

        def finish(d, carry):
            block(q, d).wait_send()
            source = lax.rem(me + 1 + d, parts)
            pltpu.make_async_remote_copy(
                src_ref=blocks.at[q, d],
                dst_ref=moved.at[source, :, pl.ds(q * part_rows, part_rows)],
                send_sem=block_send.at[q, d],
                recv_sem=block_recv.at[q, source],
                device_id={"sector": source},
                device_id_type=MESH,
            ).wait_recv()
            return carry

        lax.fori_loop(0, parts - 1, finish, 0)


def head(env_left, site, mpo, env_right, bond_tensor, parts):
    width, rows, bond = env_left.shape
    states, depth, _ = site.shape
    columns = bond // parts
    eye = jnp.eye(GROUP, dtype=jnp.float32)
    side = width * states * GROUP
    mix = jnp.einsum("vwst,ij->wsitvj", mpo, eye, precision=lax.Precision.HIGHEST).reshape(side, side)
    part_rows = rows // SHIFTS
    carried = jax.ShapeDtypeStruct((parts, width // CHUNKS, states, rows, columns), jnp.bfloat16)
    anywhere = pl.BlockSpec(memory_space=pl.ANY)
    dma = pltpu.SemaphoreType.DMA
    return pl.pallas_call(
        head_kernel,
        in_specs=[pl.BlockSpec(memory_space=pltpu.VMEM)] + [anywhere] * 4,
        out_specs=[anywhere] * (2 + CHUNKS),
        out_shape=[
            jax.ShapeDtypeStruct((parts, states, depth, bond), jnp.bfloat16),
            jax.ShapeDtypeStruct((parts, width, rows, columns), jnp.bfloat16),
        ] + [carried] * CHUNKS,
        scratch_shapes=[
            pltpu.VMEM((width, rows, bond), jnp.bfloat16),
            pltpu.VMEM((bond, bond), jnp.bfloat16),
            pltpu.VMEM((SHIFTS, parts, width, part_rows, columns), jnp.bfloat16),
            pltpu.VMEM((states, depth, bond), jnp.bfloat16),
            dma((SHIFTS,)),
            dma((SHIFTS,)),
            dma((3, parts, states)),
            dma((parts, states)),
            dma((SHIFTS, parts)),
            dma((SHIFTS, parts)),
            dma((2,)),
        ],
        compiler_params=pltpu.CompilerParams(
            vmem_limit_bytes=VMEM_LIMIT, collective_id=0, has_side_effects=True
        ),
        cost_estimate=pl.CostEstimate(
            flops=3 * width * rows * bond * bond * states,
            bytes_accessed=128 * 1024 * 1024,
            transcendentals=0,
        ),
    )(mix, env_right, site, bond_tensor, env_left)


def env_kernel(x_ref, site_ref, *rest):
    out_ref, turned = rest[-2:]
    parts, count, states, depth, columns = x_ref.shape

    @pl.when(pl.program_id(0) == 0)
    def _():
        for n in range(parts):
            for s in range(states):
                at = (n * states + s) * depth
                for v in range(count):
                    turned[v * columns : (v + 1) * columns, at : at + depth] = x_ref[n, v, s].T

    site = site_ref[...].reshape(parts * states * depth, site_ref.shape[-1])
    total = jnp.dot(turned[...], site, preferred_element_type=jnp.float32)
    out_ref[...] = total.astype(jnp.bfloat16).reshape(out_ref.shape)


def env_chunk(moved, gathered, previous, chunk, width, tile):
    parts, count, states, depth, columns = moved.shape
    bond = gathered.shape[-1]
    operands = (moved, gathered) + (() if previous is None else (previous,))
    specs = [
        pl.BlockSpec(moved.shape, lambda j: (0, 0, 0, 0, 0), pipeline_mode=pl.Buffered(1)),
        pl.BlockSpec((parts, states, depth, tile), lambda j: (0, 0, 0, j)),
    ]
    if previous is not None:
        specs.append(pl.BlockSpec(memory_space=pl.ANY))
    return pl.pallas_call(
        env_kernel,
        grid=(bond // tile,),
        in_specs=specs,
        out_specs=pl.BlockSpec((count, columns, tile), lambda j: (chunk, 0, j)),
        out_shape=jax.ShapeDtypeStruct((width, columns, bond), jnp.bfloat16),
        scratch_shapes=[pltpu.VMEM((count * columns, parts * states * depth), jnp.bfloat16)],
        input_output_aliases={} if previous is None else {2: 0},
        compiler_params=pltpu.CompilerParams(vmem_limit_bytes=VMEM_LIMIT),
        cost_estimate=pl.CostEstimate(
            flops=2 * count * columns * parts * states * depth * bond,
            bytes_accessed=32 * 1024 * 1024,
            transcendentals=0,
        ),
    )(*operands)


def local(env_left, site_tensor, mpo_tensor, env_right, bond_tensor):
    parts = lax.axis_size("sector")
    width, rows, bond = env_left.shape[1:]
    columns = bond // parts
    half = rows // CHUNKS
    gathered, bond_moved, *carried = head(
        env_left[0], site_tensor[0].transpose(1, 0, 2), mpo_tensor[0],
        env_right[0], bond_tensor[0], parts,
    )
    moved = []
    for i in range(CHUNKS):
        moved.append(swap(carried[i]))
    env_new = None
    for i in range(CHUNKS):
        env_new = env_chunk(moved[i], gathered, env_new, i, width, 2 * LANES)
    image_rows = []
    for i in range(CHUNKS):
        image = jnp.einsum(
            "wkda,nwbk->dnba",
            env_new.reshape(width, columns, parts, columns),
            bond_moved[:, :, i * half : (i + 1) * half],
            preferred_element_type=jnp.float32,
        ).astype(jnp.bfloat16).reshape(parts, parts * half, columns)
        image_rows.append(lax.psum_scatter(image, "sector", scatter_dimension=0, tiled=False))
    image_rows = jnp.stack(
        [x.reshape(parts, half, columns) for x in image_rows], axis=1
    ).reshape(bond, columns).T
    return (env_new[None], image_rows[None])


def plain_local(env_left, site_tensor, mpo_tensor, env_right, bond_tensor):
    width = env_left.shape[1]
    states = site_tensor.shape[2]
    gathered = lax.all_gather(site_tensor, "sector", axis=1, tiled=True)[0]
    half_done = jnp.einsum(
        "wak,ksc->wasc", env_left[0], gathered, preferred_element_type=jnp.float32
    )
    carried = jnp.einsum(
        "vwst,vatc->wsac", mpo_tensor[0], half_done, precision=lax.Precision.HIGHEST
    ).astype(jnp.bfloat16)
    carried = carried.reshape((width * states,) + carried.shape[2:])
    right_next = shifted(env_right, "region", -1)[0]
    bond_right = jnp.einsum(
        "wbc,kc->wbk", right_next, bond_tensor[0], preferred_element_type=jnp.float32
    ).astype(jnp.bfloat16)
    carried_moved = lax.all_to_all(carried, "sector", split_axis=2, concat_axis=1, tiled=True)
    bond_moved = lax.all_to_all(bond_right, "sector", split_axis=2, concat_axis=1, tiled=True)
    carried_moved = carried_moved.reshape((width, states) + carried_moved.shape[1:])
    env_new = jnp.einsum(
        "wsac,asb->wcb", carried_moved, gathered, preferred_element_type=jnp.float32
    ).astype(jnp.bfloat16)
    image_rows = lax.psum_scatter(
        jnp.einsum("wka,wbk->ab", env_new, bond_moved, preferred_element_type=jnp.float32),
        "sector",
        scatter_dimension=0,
        tiled=True,
    )
    return (env_new[None], image_rows.astype(jnp.bfloat16)[None])


def solution(mesh):
    def body(env_left, site_tensor, mpo_tensor, env_right, bond_tensor):
        width, rows, bond = env_left.shape[1:]
        columns = bond // mesh.shape["sector"]
        tiled = rows % LANES == 0 and columns % LANES == 0 and width % CHUNKS == 0 and rows % (16 * SHIFTS) == 0
        tiled = tiled and mesh.shape["sector"] % 2 == 0 and mesh.shape["region"] > 2
        step = local if tiled else plain_local
        return step(env_left, site_tensor, mpo_tensor, env_right, bond_tensor)

    return jax.shard_map(
        body,
        mesh=mesh,
        in_specs=(
            P("region", None, "sector", None),
            P("region", "sector", None, None),
            P("region", None, None, None, None),
            P("region", None, "sector", None),
            P("region", None, None),
        ),
        out_specs=(P("region", None, "sector", None), P("region", "sector", None)),
        check_vma=False,
    )
```

```python
import functools

import jax
import jax.numpy as jnp
from jax import lax
from jax.experimental import pallas as pl
from jax.experimental.pallas import tpu as pltpu
from jax.sharding import PartitionSpec as P

GROUP = 16
LANES = 128
CHUNKS = 4
SHIFTS = 4
EARLY = 2
HOLD = (0, 5)
AHEAD = 2
VMEM_LIMIT = 60 * 1024 * 1024


def shifted(block, axis, distance):
    devices = range(lax.axis_size(axis))
    route = [((i - distance) % len(devices), i) for i in devices]
    return lax.ppermute(block, axis, route)


MESH = pl.DeviceIdType.MESH


def carried_body(mix_ref, env_ref, site_ref, *out_refs):
    width, rows, bond = env_ref.shape
    _, states, _, columns = site_ref.shape
    mix = mix_ref[...]
    mix_high = mix.astype(jnp.bfloat16)
    mix_low = (mix - mix_high.astype(jnp.float32)).astype(jnp.bfloat16)
    env = env_ref[...].reshape(width * rows, bond)
    half_done = [
        jnp.dot(env, site_ref[:, t].reshape(bond, columns), preferred_element_type=jnp.float32)
        .reshape(width, rows, columns)
        for t in range(states)
    ]
    dot = functools.partial(jnp.dot, preferred_element_type=jnp.float32)
    for g in range(rows // GROUP):
        span = slice(g * GROUP, (g + 1) * GROUP)
        x = jnp.concatenate(
            [h[:, span].reshape(width * GROUP, columns) for h in half_done], axis=0
        )
        high = x.astype(jnp.bfloat16)
        low = (x - high.astype(jnp.float32)).astype(jnp.bfloat16)
        y = dot(mix_high, high) + dot(mix_high, low) + dot(mix_low, high)
        y = y.astype(jnp.bfloat16).reshape(width, states, GROUP, columns)
        step = width // len(out_refs)
        for i, out_ref in enumerate(out_refs):
            out_ref[0, :, :, span, :] = y[i * step : (i + 1) * step]


def head_kernel(
    mix_ref, right_hbm, site_hbm, bond_hbm, left_hbm,
    gathered, moved, late, *rest,
):
    carried = rest[:CHUNKS]
    (right, bond_ref, blocks, own_site, shift_send, shift_recv, site_send, site_recv,
     block_send, block_recv, local_sem) = rest[CHUNKS:]
    parts, states, depth, bond = gathered.shape
    width, rows, _ = right_hbm.shape
    columns = bond // parts
    line = parts // 2
    me = lax.axis_index("sector")
    z, y = me // 2, lax.rem(me, 2)
    regions = lax.axis_size("region")
    region = lax.axis_index("region")
    before = lax.rem(region + regions - 1, regions)
    after = lax.rem(region + 1, regions)
    part_rows = rows // SHIFTS
    twin = 2 * z + 1 - y

    barrier = pltpu.get_barrier_semaphore()
    for d in range(1, parts):
        pl.semaphore_signal(
            barrier, inc=1, device_id={"sector": lax.rem(me + d, parts)}, device_id_type=MESH
        )
    for other in (before, after):
        pl.semaphore_signal(barrier, inc=1, device_id={"region": other}, device_id_type=MESH)
    pl.semaphore_wait(barrier, parts + 1)

    def shift(q):
        span = pl.ds(q * part_rows, part_rows)
        return pltpu.make_async_remote_copy(
            src_ref=right_hbm.at[:, span],
            dst_ref=right.at[:, span],
            send_sem=shift_send.at[q],
            recv_sem=shift_recv.at[q],
            device_id={"region": before},
            device_id_type=MESH,
        )

    def hop(way, source, piece, target, first=False):
        return pltpu.make_async_remote_copy(
            src_ref=site_hbm.at[piece] if first else gathered.at[source, piece],
            dst_ref=gathered.at[source, piece],
            send_sem=site_send.at[way, source, piece],
            recv_sem=site_recv.at[source, piece],
            device_id={"sector": target},
            device_id_type=MESH,
        )

    def outward(source, piece, first, ways, act):
        for way in ways:
            there = {0: me + 2, 1: me - 2, 2: twin}[way]
            if way == 2:
                act(hop(way, source, piece, there, first))
            else:
                inside = z + 1 < line if way == 0 else z >= 1

                @pl.when(inside)
                def _():
                    act(hop(way, source, piece, there, first))

    def block(q, d):
        return pltpu.make_async_remote_copy(
            src_ref=blocks.at[q, d],
            dst_ref=moved.at[q, me],
            send_sem=block_send.at[q, d],
            recv_sem=block_recv.at[q, me],
            device_id={"sector": lax.rem(me + 1 + d, parts)},
            device_id_type=MESH,
        )

    def stored(q, d):
        j = lax.rem(me + 1 + d, parts)
        return pltpu.make_async_copy(
            blocks.at[q, d],
            moved.at[q, j] if q < EARLY else late.at[q - EARLY, j],
            block_send.at[q, d],
        )

    def start(copy):
        copy.start()

    for q in range(SHIFTS):
        shift(q).start()
    for piece in range(states):
        outward(me, piece, True, (0, 1, 2), start)
    load_bond = pltpu.make_async_copy(bond_hbm, bond_ref, local_sem.at[0])
    load_bond.start()
    load_site = pltpu.make_async_copy(site_hbm, own_site, local_sem.at[1])
    load_site.start()
    load_site.wait()
    keep_site = pltpu.make_async_copy(own_site, gathered.at[me], local_sem.at[1])
    keep_site.start()
    load_bond.wait()

    def product(q):
        shift(q).wait_recv()
        span = pl.ds(q * part_rows, part_rows)
        x = right[:, span].reshape(width * part_rows, bond)

        def step(d, carry):
            j = lax.rem(me + 1 + d, parts)
            out = lax.dot_general(
                x,
                bond_ref[pl.ds(pl.multiple_of(j * columns, columns), columns), :],
                (((1,), (1,)), ((), ())),
                preferred_element_type=jnp.float32,
            )
            blocks[q, d] = out.astype(jnp.bfloat16).reshape(width, part_rows, columns)
            return carry

        lax.fori_loop(0, parts, step, 0)

    def dispatch(q):
        if q < EARLY:
            for d in range(parts - 1):
                block(q, d).start()
            stored(q, parts - 1).start()
        else:
            for d in range(parts):
                stored(q, d).start()

    def relay(distance, piece):
        for way, source in ((0, me - 2 * distance), (1, me + 2 * distance)):
            there = z >= distance if way == 0 else z + distance < line

            @pl.when(there)
            def _():
                hop(way, source, piece, twin).wait_recv()
                outward(source, piece, False, (way, 2), start)

    ticks = [(distance, piece) for distance in range(1, line) for piece in range(states)]
    for i, (distance, piece) in enumerate(ticks):
        relay(distance, piece)
        if i < SHIFTS:
            product(i)
            if i >= EARLY:
                dispatch(i)
        for q in range(EARLY):
            if HOLD[q] == i:
                dispatch(q)
    for other in range(line):
        for piece in range(states):
            hop(2, 2 * other + 1 - y, piece, twin).wait_recv()
    keep_site.wait()

    tile = min(rows, LANES)
    pltpu.emit_pipeline(
        functools.partial(carried_body, mix_ref),
        grid=(rows // tile, parts),
        in_specs=[
            pl.BlockSpec((width, tile, bond), lambda i, j: (0, i, 0)),
            pl.BlockSpec((parts, states, depth, columns), lambda i, j: (0, 0, 0, j)),
        ],
        out_specs=[
            pl.BlockSpec((1, width // CHUNKS, states, tile, columns), lambda i, j: (j, 0, 0, i, 0))
        ] * CHUNKS,
    )(left_hbm, gathered, *carried)

    for q in range(SHIFTS):
        shift(q).wait_send()
    for piece in range(states):
        outward(me, piece, True, (0, 1, 2), lambda copy: copy.wait_send())
    for distance, piece in ticks:
        for way, source in ((0, me - 2 * distance), (1, me + 2 * distance)):
            there = z >= distance if way == 0 else z + distance < line

            @pl.when(there)
            def _():
                outward(source, piece, False, (way, 2), lambda copy: copy.wait_send())
    for q in range(EARLY, SHIFTS):
        for d in range(parts):
            stored(q, d).wait()
    for q in range(EARLY):
        stored(q, parts - 1).wait()

        def finish(d, carry):
            block(q, d).wait_send()
            source = lax.rem(me + 1 + d, parts)
            pltpu.make_async_remote_copy(
                src_ref=blocks.at[q, d],
                dst_ref=moved.at[q, source],
                send_sem=block_send.at[q, d],
                recv_sem=block_recv.at[q, source],
                device_id={"sector": source},
                device_id_type=MESH,
            ).wait_recv()
            return carry

        lax.fori_loop(0, parts - 1, finish, 0)


def head(env_left, site, mpo, env_right, bond_tensor, parts):
    width, rows, bond = env_left.shape
    states, depth, _ = site.shape
    columns = bond // parts
    eye = jnp.eye(GROUP, dtype=jnp.float32)
    side = width * states * GROUP
    mix = jnp.einsum("vwst,ij->wsitvj", mpo, eye, precision=lax.Precision.HIGHEST).reshape(side, side)
    part_rows = rows // SHIFTS
    carried = jax.ShapeDtypeStruct((parts, width // CHUNKS, states, rows, columns), jnp.bfloat16)
    anywhere = pl.BlockSpec(memory_space=pl.ANY)
    dma = pltpu.SemaphoreType.DMA
    return pl.pallas_call(
        head_kernel,
        in_specs=[pl.BlockSpec(memory_space=pltpu.VMEM)] + [anywhere] * 4,
        out_specs=[anywhere] * (3 + CHUNKS),
        out_shape=[
            jax.ShapeDtypeStruct((parts, states, depth, bond), jnp.bfloat16),
            jax.ShapeDtypeStruct((EARLY, parts, width, part_rows, columns), jnp.bfloat16),
            jax.ShapeDtypeStruct((SHIFTS - EARLY, parts, width, part_rows, columns), jnp.bfloat16),
        ] + [carried] * CHUNKS,
        scratch_shapes=[
            pltpu.VMEM((width, rows, bond), jnp.bfloat16),
            pltpu.VMEM((bond, bond), jnp.bfloat16),
            pltpu.VMEM((SHIFTS, parts, width, part_rows, columns), jnp.bfloat16),
            pltpu.VMEM((states, depth, bond), jnp.bfloat16),
            dma((SHIFTS,)),
            dma((SHIFTS,)),
            dma((3, parts, states)),
            dma((parts, states)),
            dma((SHIFTS, parts)),
            dma((SHIFTS, parts)),
            dma((2,)),
        ],
        compiler_params=pltpu.CompilerParams(
            vmem_limit_bytes=VMEM_LIMIT, collective_id=0, has_side_effects=True
        ),
        cost_estimate=pl.CostEstimate(
            flops=3 * width * rows * bond * bond * states,
            bytes_accessed=128 * 1024 * 1024,
            transcendentals=0,
        ),
    )(mix, env_right, site, bond_tensor, env_left)


def rest_kernel(gathered, moved, late, *refs):
    carried = refs[:CHUNKS]
    env_out, image_out, late_moved = refs[CHUNKS : CHUNKS + 3]
    landed = refs[CHUNKS + 3 : 2 * CHUNKS + 3]
    (x, turned, env, bond_in, keep, pair_out, pair_in, line_out, line_in, done,
     swap_send, swap_recv, late_send, late_recv, pair_send, pair_recv, line_send, line_recv,
     load_sem, env_sem, out_sem) = refs[2 * CHUNKS + 3 :]
    parts, states, depth, bond = gathered.shape
    _, count, _, _, columns = landed[0].shape
    width = count * CHUNKS
    part_rows = moved.shape[3]
    line = parts // 2
    group = line
    steps = SHIFTS * 2
    me = lax.axis_index("sector")
    z, y = me // 2, lax.rem(me, 2)
    twin = 2 * z + 1 - y

    barrier = pltpu.get_barrier_semaphore()
    for d in range(1, parts):
        pl.semaphore_signal(
            barrier, inc=1, device_id={"sector": lax.rem(me + d, parts)}, device_id_type=MESH
        )
    pl.semaphore_wait(barrier, parts - 1)

    def remote(src, dst, send, recv, target):
        return pltpu.make_async_remote_copy(
            src_ref=src, dst_ref=dst, send_sem=send, recv_sem=recv,
            device_id={"sector": target}, device_id_type=MESH,
        )

    def batch_copy(b, d, receiving=False):
        j = lax.rem(me + 1 + d, parts)
        owner = j if receiving else me
        if b < CHUNKS:
            return remote(
                carried[b].at[j], landed[b].at[owner],
                swap_send.at[b, d], swap_recv.at[b, owner], j,
            )
        q = b - CHUNKS
        return remote(
            late.at[q, j], late_moved.at[q, owner],
            late_send.at[q, d], late_recv.at[q, owner], j,
        )

    batches = CHUNKS + SHIFTS - EARLY

    def dispatch(b):
        if b < batches:
            for d in range(parts - 1):
                batch_copy(b, d).start()

    def collect(b):
        for d in range(parts - 1):
            batch_copy(b, d, True).wait_recv()
        dispatch(b + AHEAD)

    for b in range(AHEAD):
        dispatch(b)

    def fill(b):
        own = pltpu.make_async_copy(carried[b].at[me], x.at[me], load_sem.at[parts - 1])
        own.start()
        copies = [own]
        for d in range(parts - 1):
            n = lax.rem(me + 1 + d, parts)
            copies.append(pltpu.make_async_copy(landed[b].at[n], x.at[n], load_sem.at[d]))
            copies[-1].start()
        for copy in copies:
            copy.wait()

    def turn(n, carry):
        for s in range(states):
            at = pl.multiple_of((n * states + s) * depth, depth)
            for v in range(count):
                turned[v * columns : (v + 1) * columns, pl.ds(at, depth)] = x[n, v, s].T
        return carry

    def env_body(site_ref, out_ref):
        site = site_ref[...].reshape(parts * states * depth, site_ref.shape[-1])
        total = jnp.dot(turned[...], site, preferred_element_type=jnp.float32)
        out_ref[...] = total.astype(jnp.bfloat16).reshape(out_ref.shape)

    def reload(b):
        span = pl.ds(b * count, count)
        return pltpu.make_async_copy(env_out.at[span], env.at[span], env_sem.at[b])

    tile = 2 * LANES
    for b in range(CHUNKS):
        collect(b)
        fill(b)
        lax.fori_loop(0, parts, turn, 0)
        pltpu.emit_pipeline(
            env_body,
            grid=(bond // tile,),
            in_specs=[pl.BlockSpec((parts, states, depth, tile), lambda j: (0, 0, 0, j))],
            out_specs=[pl.BlockSpec((count, columns, tile), lambda j: (0, 0, j))],
        )(gathered, env_out.at[pl.ds(b * count, count)])
        reload(b).start()
    for b in range(CHUNKS):
        reload(b).wait()

    def pair_copy(u):
        return remote(pair_out.at[u], pair_in.at[u], pair_send.at[u], pair_recv.at[u], twin)

    def line_copy(u, t, way):
        slot = t + 1 if way == 0 else t
        return remote(
            line_out.at[u, t], line_in.at[u, slot], line_send.at[u, t], line_recv.at[u, slot],
            me + 2 if way == 0 else me - 2,
        )

    def dot(a, b):
        return jnp.dot(a, b, preferred_element_type=jnp.float32)

    def image(u):
        q, part = u // 2, u % 2
        for i in range(group):
            n = part * group + i
            if q < EARLY:
                pltpu.make_async_copy(moved.at[q, n], bond_in.at[i], load_sem.at[i]).start()
            else:
                mine = n == me

                @pl.when(mine)
                def _():
                    pltpu.make_async_copy(
                        late.at[q - EARLY, n], bond_in.at[i], load_sem.at[i]
                    ).start()

                @pl.when(jnp.logical_not(mine))
                def _():
                    pltpu.make_async_copy(
                        late_moved.at[q - EARLY, n], bond_in.at[i], load_sem.at[i]
                    ).start()

        for i in range(group):
            pltpu.make_async_copy(moved.at[0, 0], bond_in.at[i], load_sem.at[i]).wait()
        left = jnp.concatenate(
            [bond_in[:, w].reshape(group * part_rows, columns) for w in range(width)], axis=1
        )
        for t in range(line):
            at = pl.multiple_of((2 * t + 1 - y) * columns, columns)
            pair_out[u, t] = dot(
                left, env[:, :, pl.ds(at, columns)].reshape(width * columns, columns)
            ).astype(jnp.bfloat16)
        for t in range(line):
            at = pl.multiple_of((2 * t + y) * columns, columns)
            keep[u, t] = dot(left, env[:, :, pl.ds(at, columns)].reshape(width * columns, columns))
        pair_copy(u).start()

    def paired(u):
        pair_copy(u).wait_recv()
        keep[u] = keep[u] + pair_in[u].astype(jnp.float32)

    def relay(s, way):
        first = z if way == 0 else line - 1 - z
        u = s - 1 - first
        live = jnp.logical_and(u >= 0, u < steps)
        for t in range(line):
            sends = jnp.logical_and(live, t > z if way == 0 else t < z)

            @pl.when(jnp.logical_and(sends, first == 0))
            def _():
                line_out[u, t] = keep[u, t].astype(jnp.bfloat16)

            @pl.when(jnp.logical_and(sends, first > 0))
            def _():
                slot = t + 1 if way == 0 else t
                line_copy(u, t, way).wait_recv()
                line_out[u, t] = (
                    keep[u, t] + line_in[u, slot].astype(jnp.float32)
                ).astype(jnp.bfloat16)

    def send_on(s, way):
        first = z if way == 0 else line - 1 - z
        u = s - 1 - first
        live = jnp.logical_and(u >= 0, u < steps)
        for t in range(line):

            @pl.when(jnp.logical_and(live, t > z if way == 0 else t < z))
            def _():
                line_copy(u, t, way).start()

    def result(u):
        return pltpu.make_async_copy(done.at[u], image_out.at[u], out_sem.at[u])

    def total(u):
        @pl.when(z > 0)
        def _():
            line_copy(u, z, 0).wait_recv()
            keep[u, z] = keep[u, z] + line_in[u, z + 1].astype(jnp.float32)

        @pl.when(z < line - 1)
        def _():
            line_copy(u, z, 1).wait_recv()
            keep[u, z] = keep[u, z] + line_in[u, z].astype(jnp.float32)

        done[u] = keep[u, z].astype(jnp.bfloat16)

    for s in range(steps + line):
        if s < steps:
            if s % 2 == 0 and s // 2 >= EARLY:
                collect(CHUNKS + s // 2 - EARLY)
            image(s)
        if 1 <= s <= steps:
            paired(s - 1)
        relay(s, 0)
        relay(s, 1)
        if s >= line:
            total(s - line)
        send_on(s, 0)
        send_on(s, 1)
        if s >= line:
            result(s - line).start()

    for b in range(batches):
        for d in range(parts - 1):
            batch_copy(b, d).wait_send()
    for u in range(steps):
        pair_copy(u).wait_send()
        result(u).wait()
        for t in range(line):
            @pl.when(t > z)
            def _():
                line_copy(u, t, 0).wait_send()

            @pl.when(t < z)
            def _():
                line_copy(u, t, 1).wait_send()


def rest_of(gathered, moved, late, carried):
    parts, states, depth, bond = gathered.shape
    _, count, _, _, columns = carried[0].shape
    width = count * CHUNKS
    part_rows = moved.shape[3]
    line = parts // 2
    steps = SHIFTS * 2
    block = (line * part_rows, columns)
    anywhere = pl.BlockSpec(memory_space=pl.ANY)
    dma = pltpu.SemaphoreType.DMA
    bf16 = jnp.bfloat16
    return pl.pallas_call(
        rest_kernel,
        in_specs=[anywhere] * (3 + CHUNKS),
        out_specs=[anywhere] * (3 + CHUNKS),
        out_shape=[
            jax.ShapeDtypeStruct((width, columns, bond), bf16),
            jax.ShapeDtypeStruct((steps,) + block, bf16),
            jax.ShapeDtypeStruct(late.shape, bf16),
        ] + [jax.ShapeDtypeStruct(c.shape, bf16) for c in carried],
        scratch_shapes=[
            pltpu.VMEM(carried[0].shape, bf16),
            pltpu.VMEM((count * columns, parts * states * depth), bf16),
            pltpu.VMEM((width, columns, bond), bf16),
            pltpu.VMEM((line, width, part_rows, columns), bf16),
            pltpu.VMEM((steps, line) + block, jnp.float32),
            pltpu.VMEM((steps, line) + block, bf16),
            pltpu.VMEM((steps, line) + block, bf16),
            pltpu.VMEM((steps, line) + block, bf16),
            pltpu.VMEM((steps, line + 1) + block, bf16),
            pltpu.VMEM((steps,) + block, bf16),
            dma((CHUNKS, parts)),
            dma((CHUNKS, parts)),
            dma((SHIFTS - EARLY, parts)),
            dma((SHIFTS - EARLY, parts)),
            dma((steps,)),
            dma((steps,)),
            dma((steps, line)),
            dma((steps, line + 1)),
            dma((parts,)),
            dma((CHUNKS,)),
            dma((steps,)),
        ],
        compiler_params=pltpu.CompilerParams(
            vmem_limit_bytes=VMEM_LIMIT, collective_id=1, has_side_effects=True
        ),
        cost_estimate=pl.CostEstimate(
            flops=3 * width * columns * parts * states * depth * bond,
            bytes_accessed=128 * 1024 * 1024,
            transcendentals=0,
        ),
    )(gathered, moved, late, *carried)


def local(env_left, site_tensor, mpo_tensor, env_right, bond_tensor):
    parts = lax.axis_size("sector")
    _, rows, bond = env_left.shape[1:]
    columns = bond // parts
    gathered, moved, late, *carried = head(
        env_left[0], site_tensor[0].transpose(1, 0, 2), mpo_tensor[0],
        env_right[0], bond_tensor[0], parts,
    )
    env_new, image, *_ = rest_of(gathered, moved, late, carried)
    image_rows = (
        image.reshape(SHIFTS, parts, rows // SHIFTS, columns)
        .transpose(3, 1, 0, 2)
        .reshape(columns, bond)
    )
    return (env_new[None], image_rows[None])


def plain_local(env_left, site_tensor, mpo_tensor, env_right, bond_tensor):
    width = env_left.shape[1]
    states = site_tensor.shape[2]
    gathered = lax.all_gather(site_tensor, "sector", axis=1, tiled=True)[0]
    half_done = jnp.einsum(
        "wak,ksc->wasc", env_left[0], gathered, preferred_element_type=jnp.float32
    )
    carried = jnp.einsum(
        "vwst,vatc->wsac", mpo_tensor[0], half_done, precision=lax.Precision.HIGHEST
    ).astype(jnp.bfloat16)
    carried = carried.reshape((width * states,) + carried.shape[2:])
    right_next = shifted(env_right, "region", -1)[0]
    bond_right = jnp.einsum(
        "wbc,kc->wbk", right_next, bond_tensor[0], preferred_element_type=jnp.float32
    ).astype(jnp.bfloat16)
    carried_moved = lax.all_to_all(carried, "sector", split_axis=2, concat_axis=1, tiled=True)
    bond_moved = lax.all_to_all(bond_right, "sector", split_axis=2, concat_axis=1, tiled=True)
    carried_moved = carried_moved.reshape((width, states) + carried_moved.shape[1:])
    env_new = jnp.einsum(
        "wsac,asb->wcb", carried_moved, gathered, preferred_element_type=jnp.float32
    ).astype(jnp.bfloat16)
    image_rows = lax.psum_scatter(
        jnp.einsum("wka,wbk->ab", env_new, bond_moved, preferred_element_type=jnp.float32),
        "sector",
        scatter_dimension=0,
        tiled=True,
    )
    return (env_new[None], image_rows.astype(jnp.bfloat16)[None])


def solution(mesh):
    def body(env_left, site_tensor, mpo_tensor, env_right, bond_tensor):
        width, rows, bond = env_left.shape[1:]
        columns = bond // mesh.shape["sector"]
        tiled = rows % LANES == 0 and columns % LANES == 0 and width % CHUNKS == 0 and rows % (16 * SHIFTS) == 0
        tiled = tiled and mesh.shape["sector"] % 2 == 0 and mesh.shape["region"] > 2
        step = local if tiled else plain_local
        return step(env_left, site_tensor, mpo_tensor, env_right, bond_tensor)

    return jax.shard_map(
        body,
        mesh=mesh,
        in_specs=(
            P("region", None, "sector", None),
            P("region", "sector", None, None),
            P("region", None, None, None, None),
            P("region", None, "sector", None),
            P("region", None, None),
        ),
        out_specs=(P("region", None, "sector", None), P("region", "sector", None)),
        check_vma=False,
    )
```

```python
import functools

import jax
import jax.numpy as jnp
from jax import lax
from jax.experimental import pallas as pl
from jax.experimental.pallas import tpu as pltpu
from jax.sharding import PartitionSpec as P

GROUP = 16
LANES = 128
CHUNKS = 4
SHIFTS = 4
PIECES = 4
CROSS = (3, 5, 7, 9)
PRODUCT = (0, 2, 4, 6)
AHEAD = 2
SPLIT = 4
VMEM_LIMIT = 60 * 1024 * 1024


def shifted(block, axis, distance):
    devices = range(lax.axis_size(axis))
    route = [((i - distance) % len(devices), i) for i in devices]
    return lax.ppermute(block, axis, route)


MESH = pl.DeviceIdType.MESH


def carried_body(mix_ref, env_ref, site_ref, out_ref):
    width, rows, bond = env_ref.shape
    _, states, _, columns = site_ref.shape
    mix = mix_ref[...]
    mix_high = mix.astype(jnp.bfloat16)
    mix_low = (mix - mix_high.astype(jnp.float32)).astype(jnp.bfloat16)
    env = env_ref[...].reshape(width * rows, bond)
    half_done = [
        jnp.dot(env, site_ref[:, t].reshape(bond, columns), preferred_element_type=jnp.float32)
        .reshape(width, rows, columns)
        for t in range(states)
    ]
    dot = functools.partial(jnp.dot, preferred_element_type=jnp.float32)
    step = width // CHUNKS
    for g in range(rows // GROUP):
        span = slice(g * GROUP, (g + 1) * GROUP)
        x = jnp.concatenate(
            [h[:, span].reshape(width * GROUP, columns) for h in half_done], axis=0
        )
        high = x.astype(jnp.bfloat16)
        low = (x - high.astype(jnp.float32)).astype(jnp.bfloat16)
        y = dot(mix_high, high) + dot(mix_high, low) + dot(mix_low, high)
        y = y.astype(jnp.bfloat16).reshape(width, states, GROUP, columns)
        for i in range(CHUNKS):
            out_ref[i, 0, :, :, span, :] = y[i * step : (i + 1) * step]


def greet(parts):
    me = lax.axis_index("sector")
    barrier = pltpu.get_barrier_semaphore()
    for d in range(1, parts):
        pl.semaphore_signal(
            barrier, inc=1, device_id={"sector": lax.rem(me + d, parts)}, device_id_type=MESH
        )
    return barrier


def remote(src, dst, send, recv, target):
    return pltpu.make_async_remote_copy(
        src_ref=src, dst_ref=dst, send_sem=send, recv_sem=recv,
        device_id=target, device_id_type=MESH,
    )


def head_kernel(
    mix_ref, right_hbm, site_hbm, bond_hbm, left_hbm,
    gathered, moved, carried,
    right, bond_ref, blocks, own_site, shift_send, shift_recv, site_send, site_recv,
    block_send, block_recv, local_sem,
):
    parts, states, depth, bond = gathered.shape
    width, rows, _ = right_hbm.shape
    columns = bond // parts
    line = parts // 2
    me = lax.axis_index("sector")
    z, y = me // 2, lax.rem(me, 2)
    regions = lax.axis_size("region")
    region = lax.axis_index("region")
    before = lax.rem(region + regions - 1, regions)
    after = lax.rem(region + 1, regions)
    part_rows = rows // SHIFTS
    piece_columns = bond // PIECES
    twin = 2 * z + 1 - y

    barrier = greet(parts)
    for other in (before, after):
        pl.semaphore_signal(barrier, inc=1, device_id={"region": other}, device_id_type=MESH)
    pl.semaphore_wait(barrier, parts + 1)

    def shift(q):
        span = pl.ds(q * part_rows, part_rows)
        return remote(
            right_hbm.at[:, span], right.at[:, span], shift_send.at[q], shift_recv.at[q],
            {"region": before},
        )

    def cut(piece):
        return pl.ds(pl.multiple_of(piece * piece_columns, piece_columns), piece_columns)

    def hop(way, source, piece, target, first=False):
        there = gathered.at[source, :, :, cut(piece)]
        return remote(
            site_hbm.at[:, :, cut(piece)] if first else there, there,
            site_send.at[way, source, piece], site_recv.at[source, piece], {"sector": target},
        )

    def outward(source, piece, first, ways, act):
        for way in ways:
            there = {0: me + 2, 1: me - 2, 2: twin}[way]
            if way == 2:
                act(hop(way, source, piece, there, first))
            else:
                inside = z + 1 < line if way == 0 else z >= 1

                @pl.when(inside)
                def _():
                    act(hop(way, source, piece, there, first))

    def target_of(d):
        return lax.rem(me + 1 + d, parts)

    def block(q, d):
        return remote(
            blocks.at[q, d], moved.at[q, me], block_send.at[q, d], block_recv.at[q, me],
            {"sector": target_of(d)},
        )

    def block_in(q, d):
        source = target_of(d)
        return remote(
            blocks.at[q, d], moved.at[q, source], block_send.at[q, d], block_recv.at[q, source],
            {"sector": source},
        )

    def own_block(q):
        return pltpu.make_async_copy(
            blocks.at[q, parts - 1], moved.at[q, me], block_send.at[q, parts - 1]
        )

    def start(copy):
        copy.start()

    for q in range(SHIFTS):
        shift(q).start()
    for piece in range(PIECES):
        outward(me, piece, True, (0, 1, 2), start)
    load_bond = pltpu.make_async_copy(bond_hbm, bond_ref, local_sem.at[0])
    load_bond.start()
    load_site = pltpu.make_async_copy(site_hbm, own_site, local_sem.at[1])
    load_site.start()
    load_site.wait()
    keep_site = pltpu.make_async_copy(own_site, gathered.at[me], local_sem.at[1])
    keep_site.start()
    load_bond.wait()

    def product(q):
        shift(q).wait_recv()
        span = pl.ds(q * part_rows, part_rows)
        x = right[:, span].reshape(width * part_rows, bond)

        def step(d, carry):
            j = target_of(d)
            out = lax.dot_general(
                x,
                bond_ref[pl.ds(pl.multiple_of(j * columns, columns), columns), :],
                (((1,), (1,)), ((), ())),
                preferred_element_type=jnp.float32,
            )
            blocks[q, d] = out.astype(jnp.bfloat16).reshape(width, part_rows, columns)
            return carry

        lax.fori_loop(0, parts, step, 0)

    def dispatch(q, cross):
        def step(d, carry):
            same = lax.rem(target_of(d), 2) == y

            @pl.when(jnp.logical_not(same) if cross else same)
            def _():
                block(q, d).start()

            return carry

        lax.fori_loop(0, parts - 1, step, 0)
        if not cross:
            own_block(q).start()

    def relay(distance, piece):
        for way, source in ((0, me - 2 * distance), (1, me + 2 * distance)):
            there = z >= distance if way == 0 else z + distance < line

            @pl.when(there)
            def _():
                hop(way, source, piece, twin).wait_recv()
                outward(source, piece, False, (way, 2), start)

    def tick(i, carry):
        relay(i // PIECES + 1, lax.rem(i, PIECES))
        for q in range(SHIFTS):

            @pl.when(i == PRODUCT[q])
            def _():
                product(q)
                dispatch(q, False)

            @pl.when(i == CROSS[q])
            def _():
                dispatch(q, True)

        return carry

    ticks = (line - 1) * PIECES
    lax.fori_loop(0, ticks, tick, 0)
    keep_site.wait()
    tile = min(rows, LANES)
    per = parts // PIECES

    def absorb(piece, carry):
        for other in range(line):
            hop(2, 2 * other + 1 - y, piece, twin).wait_recv()
        pltpu.emit_pipeline(
            functools.partial(carried_body, mix_ref),
            grid=(rows // tile, per),
            in_specs=[
                pl.BlockSpec((width, tile, bond), lambda i, j: (0, i, 0)),
                pl.BlockSpec((parts, states, depth, columns), lambda i, j: (0, 0, 0, j)),
            ],
            out_specs=[
                pl.BlockSpec(
                    (CHUNKS, 1, width // CHUNKS, states, tile, columns),
                    lambda i, j: (0, j, 0, 0, i, 0),
                )
            ],
        )(
            left_hbm,
            gathered.at[:, :, :, cut(piece)],
            carried.at[:, pl.ds(piece * per, per)],
        )
        return carry

    lax.fori_loop(0, PIECES, absorb, 0)

    def settle(copy):
        copy.wait_send()

    for q in range(SHIFTS):
        shift(q).wait_send()

    def sent(piece, carry):
        outward(me, piece, True, (0, 1, 2), settle)
        return carry

    lax.fori_loop(0, PIECES, sent, 0)

    def relayed(i, carry):
        distance, piece = i // PIECES + 1, lax.rem(i, PIECES)
        for way, source in ((0, me - 2 * distance), (1, me + 2 * distance)):
            there = z >= distance if way == 0 else z + distance < line

            @pl.when(there)
            def _():
                outward(source, piece, False, (way, 2), settle)

        return carry

    lax.fori_loop(0, ticks, relayed, 0)

    def finish(i, carry):
        q, d = i // (parts - 1), lax.rem(i, parts - 1)
        block(q, d).wait_send()
        block_in(q, d).wait_recv()
        return carry

    lax.fori_loop(0, SHIFTS * (parts - 1), finish, 0)
    for q in range(SHIFTS):
        own_block(q).wait()


def head(env_left, site, mpo, env_right, bond_tensor, parts):
    width, rows, bond = env_left.shape
    states, depth, _ = site.shape
    columns = bond // parts
    eye = jnp.eye(GROUP, dtype=jnp.float32)
    side = width * states * GROUP
    mix = jnp.einsum("vwst,ij->wsitvj", mpo, eye, precision=lax.Precision.HIGHEST).reshape(side, side)
    part_rows = rows // SHIFTS
    bf16 = jnp.bfloat16
    anywhere = pl.BlockSpec(memory_space=pl.ANY)
    dma = pltpu.SemaphoreType.DMA
    return pl.pallas_call(
        head_kernel,
        in_specs=[pl.BlockSpec(memory_space=pltpu.VMEM)] + [anywhere] * 4,
        out_specs=[anywhere] * 3,
        out_shape=[
            jax.ShapeDtypeStruct((parts, states, depth, bond), bf16),
            jax.ShapeDtypeStruct((SHIFTS, parts, width, part_rows, columns), bf16),
            jax.ShapeDtypeStruct((CHUNKS, parts, width // CHUNKS, states, rows, columns), bf16),
        ],
        scratch_shapes=[
            pltpu.VMEM((width, rows, bond), bf16),
            pltpu.VMEM((bond, bond), bf16),
            pltpu.VMEM((SHIFTS, parts, width, part_rows, columns), bf16),
            pltpu.VMEM((states, depth, bond), bf16),
            dma((SHIFTS,)),
            dma((SHIFTS,)),
            dma((3, parts, PIECES)),
            dma((parts, PIECES)),
            dma((SHIFTS, parts)),
            dma((SHIFTS, parts)),
            dma((2,)),
        ],
        compiler_params=pltpu.CompilerParams(
            vmem_limit_bytes=VMEM_LIMIT, collective_id=0, has_side_effects=True
        ),
        cost_estimate=pl.CostEstimate(
            flops=3 * width * rows * bond * bond * states,
            bytes_accessed=128 * 1024 * 1024,
            transcendentals=0,
        ),
    )(mix, env_right, site, bond_tensor, env_left)


def rest_kernel(
    gathered, moved, carried,
    env_out, image_out, landed,
    x, turned, env, bond_in, keep, pair_out, pair_in, line_out, line_in, done,
    swap_send, swap_recv, pair_send, pair_recv, line_send, line_recv,
    load_sem, env_sem, out_sem,
):
    parts, states, depth, bond = gathered.shape
    _, _, count, _, _, columns = landed.shape
    width = count * CHUNKS
    part_rows = moved.shape[3]
    line = parts // 2
    group = bond_in.shape[0]
    splits = parts // group
    steps = SHIFTS * splits
    me = lax.axis_index("sector")
    z, y = me // 2, lax.rem(me, 2)
    twin = 2 * z + 1 - y

    pl.semaphore_wait(greet(parts), parts - 1)

    def swap(b, d, receiving=False):
        j = lax.rem(me + 1 + d, parts)
        owner = j if receiving else me
        return remote(
            carried.at[b, j], landed.at[b, owner], swap_send.at[b, d], swap_recv.at[b, owner],
            {"sector": j},
        )

    def dispatch(b):
        def step(d, carry):
            swap(b, d).start()
            return carry

        lax.fori_loop(0, parts - 1, step, 0)

    def fill(b, d):
        n = lax.rem(me + 1 + d, parts)
        return pltpu.make_async_copy(landed.at[b, n], x.at[n], load_sem.at[d])

    def fill_own(b):
        return pltpu.make_async_copy(carried.at[b, me], x.at[me], load_sem.at[parts - 1])

    def turn(n, carry):
        for s in range(states):
            at = pl.multiple_of((n * states + s) * depth, depth)
            for v in range(count):
                turned[v * columns : (v + 1) * columns, pl.ds(at, depth)] = x[n, v, s].T
        return carry

    def env_body(site_ref, out_ref):
        site = site_ref[...].reshape(parts * states * depth, site_ref.shape[-1])
        total = jnp.dot(turned[...], site, preferred_element_type=jnp.float32)
        out_ref[...] = total.astype(jnp.bfloat16).reshape(out_ref.shape)

    def reload(b):
        span = pl.ds(b * count, count)
        return pltpu.make_async_copy(env_out.at[span], env.at[span], env_sem.at[b])

    tile = 2 * LANES
    for b in range(AHEAD):
        dispatch(b)

    def advance(b, carry):
        fill_own(b).start()

        def collect(d, carry):
            swap(b, d, True).wait_recv()
            fill(b, d).start()
            return carry

        lax.fori_loop(0, parts - 1, collect, 0)

        @pl.when(b + AHEAD < CHUNKS)
        def _():
            dispatch(b + AHEAD)

        def filled(d, carry):
            fill(b, d).wait()
            return carry

        lax.fori_loop(0, parts - 1, filled, 0)
        fill_own(b).wait()
        lax.fori_loop(0, parts, turn, 0)
        pltpu.emit_pipeline(
            env_body,
            grid=(bond // tile,),
            in_specs=[pl.BlockSpec((parts, states, depth, tile), lambda j: (0, 0, 0, j))],
            out_specs=[pl.BlockSpec((count, columns, tile), lambda j: (0, 0, j))],
        )(gathered, env_out.at[pl.ds(b * count, count)])
        reload(b).start()
        return carry

    lax.fori_loop(0, CHUNKS, advance, 0)
    for b in range(CHUNKS):
        reload(b).wait()

    def pair_copy(u):
        return remote(
            pair_out.at[u], pair_in.at[u], pair_send.at[u], pair_recv.at[u], {"sector": twin}
        )

    def line_copy(u, t, way):
        slot = t + 1 if way == 0 else t
        return remote(
            line_out.at[u, t], line_in.at[u, slot], line_send.at[u, t], line_recv.at[u, slot],
            {"sector": me + 2 if way == 0 else me - 2},
        )

    def dot(a, b):
        return jnp.dot(a, b, preferred_element_type=jnp.float32)

    def take(u, i):
        q, n = u // splits, lax.rem(u, splits) * group + i
        return pltpu.make_async_copy(
            moved.at[q, n], bond_in.at[i], load_sem.at[i]
        )

    def image(u):
        for i in range(group):
            take(u, i).start()
        for i in range(group):
            take(u, i).wait()
        left = jnp.concatenate(
            [bond_in[:, w].reshape(group * part_rows, columns) for w in range(width)], axis=1
        )

        def right(j):
            at = pl.multiple_of(j * columns, columns)
            return env[:, :, pl.ds(at, columns)].reshape(width * columns, columns)

        for t in range(line):
            pair_out[u, t] = dot(left, right(2 * t + 1 - y)).astype(jnp.bfloat16)
        for t in range(line):
            keep[u, t] = dot(left, right(2 * t + y))
        pair_copy(u).start()

    def paired(u):
        pair_copy(u).wait_recv()
        keep[u] = keep[u] + pair_in[u].astype(jnp.float32)

    def relay(s, way):
        first = z if way == 0 else line - 1 - z
        u = s - 1 - first
        live = jnp.logical_and(u >= 0, u < steps)
        for t in range(line):
            sends = jnp.logical_and(live, t > z if way == 0 else t < z)

            @pl.when(jnp.logical_and(sends, first == 0))
            def _():
                line_out[u, t] = keep[u, t].astype(jnp.bfloat16)

            @pl.when(jnp.logical_and(sends, first > 0))
            def _():
                slot = t + 1 if way == 0 else t
                line_copy(u, t, way).wait_recv()
                line_out[u, t] = (
                    keep[u, t] + line_in[u, slot].astype(jnp.float32)
                ).astype(jnp.bfloat16)

    def send_on(s, way):
        first = z if way == 0 else line - 1 - z
        u = s - 1 - first
        live = jnp.logical_and(u >= 0, u < steps)
        for t in range(line):

            @pl.when(jnp.logical_and(live, t > z if way == 0 else t < z))
            def _():
                line_copy(u, t, way).start()

    def result(u):
        return pltpu.make_async_copy(done.at[u], image_out.at[u], out_sem.at[u])

    def total(u):
        @pl.when(z > 0)
        def _():
            line_copy(u, z, 0).wait_recv()
            keep[u, z] = keep[u, z] + line_in[u, z + 1].astype(jnp.float32)

        @pl.when(z < line - 1)
        def _():
            line_copy(u, z, 1).wait_recv()
            keep[u, z] = keep[u, z] + line_in[u, z].astype(jnp.float32)

        done[u] = keep[u, z].astype(jnp.bfloat16)

    def pass_on(s, carry):
        @pl.when(s < steps)
        def _():
            image(s)

        @pl.when(jnp.logical_and(s >= 1, s <= steps))
        def _():
            paired(s - 1)

        relay(s, 0)
        relay(s, 1)

        @pl.when(s >= line)
        def _():
            total(s - line)

        send_on(s, 0)
        send_on(s, 1)

        @pl.when(s >= line)
        def _():
            result(s - line).start()

        return carry

    lax.fori_loop(0, steps + line, pass_on, 0)

    def sent(b, carry):
        def step(d, carry):
            swap(b, d).wait_send()
            return carry

        return lax.fori_loop(0, parts - 1, step, carry)

    lax.fori_loop(0, CHUNKS, sent, 0)

    def ended(u, carry):
        pair_copy(u).wait_send()
        result(u).wait()
        for t in range(line):
            @pl.when(t > z)
            def _():
                line_copy(u, t, 0).wait_send()

            @pl.when(t < z)
            def _():
                line_copy(u, t, 1).wait_send()

        return carry

    lax.fori_loop(0, steps, ended, 0)


def rest_of(gathered, moved, carried):
    parts, states, depth, bond = gathered.shape
    _, _, count, _, _, columns = carried.shape
    width = count * CHUNKS
    part_rows = moved.shape[3]
    line = parts // 2
    group = max(parts // SPLIT, 1)
    steps = SHIFTS * (parts // group)
    block = (group * part_rows, columns)
    anywhere = pl.BlockSpec(memory_space=pl.ANY)
    dma = pltpu.SemaphoreType.DMA
    bf16 = jnp.bfloat16
    return pl.pallas_call(
        rest_kernel,
        in_specs=[anywhere] * 3,
        out_specs=[anywhere] * 3,
        out_shape=[
            jax.ShapeDtypeStruct((width, columns, bond), bf16),
            jax.ShapeDtypeStruct((steps,) + block, bf16),
            jax.ShapeDtypeStruct(carried.shape, bf16),
        ],
        scratch_shapes=[
            pltpu.VMEM(carried.shape[1:], bf16),
            pltpu.VMEM((count * columns, parts * states * depth), bf16),
            pltpu.VMEM((width, columns, bond), bf16),
            pltpu.VMEM((group, width, part_rows, columns), bf16),
            pltpu.VMEM((steps, line) + block, jnp.float32),
            pltpu.VMEM((steps, line) + block, bf16),
            pltpu.VMEM((steps, line) + block, bf16),
            pltpu.VMEM((steps, line) + block, bf16),
            pltpu.VMEM((steps, line + 1) + block, bf16),
            pltpu.VMEM((steps,) + block, bf16),
            dma((CHUNKS, parts)),
            dma((CHUNKS, parts)),
            dma((steps,)),
            dma((steps,)),
            dma((steps, line)),
            dma((steps, line + 1)),
            dma((parts,)),
            dma((CHUNKS,)),
            dma((steps,)),
        ],
        compiler_params=pltpu.CompilerParams(
            vmem_limit_bytes=VMEM_LIMIT, collective_id=1, has_side_effects=True
        ),
        cost_estimate=pl.CostEstimate(
            flops=3 * width * columns * parts * states * depth * bond,
            bytes_accessed=128 * 1024 * 1024,
            transcendentals=0,
        ),
    )(gathered, moved, carried)


def local(env_left, site_tensor, mpo_tensor, env_right, bond_tensor):
    parts = lax.axis_size("sector")
    _, rows, bond = env_left.shape[1:]
    columns = bond // parts
    gathered, moved, carried = head(
        env_left[0], site_tensor[0].transpose(1, 0, 2), mpo_tensor[0],
        env_right[0], bond_tensor[0], parts,
    )
    env_new, image, _ = rest_of(gathered, moved, carried)
    image_rows = (
        image.reshape(SHIFTS, parts, rows // SHIFTS, columns)
        .transpose(3, 1, 0, 2)
        .reshape(columns, bond)
    )
    return (env_new[None], image_rows[None])


def plain_local(env_left, site_tensor, mpo_tensor, env_right, bond_tensor):
    width = env_left.shape[1]
    states = site_tensor.shape[2]
    gathered = lax.all_gather(site_tensor, "sector", axis=1, tiled=True)[0]
    half_done = jnp.einsum(
        "wak,ksc->wasc", env_left[0], gathered, preferred_element_type=jnp.float32
    )
    carried = jnp.einsum(
        "vwst,vatc->wsac", mpo_tensor[0], half_done, precision=lax.Precision.HIGHEST
    ).astype(jnp.bfloat16)
    carried = carried.reshape((width * states,) + carried.shape[2:])
    right_next = shifted(env_right, "region", -1)[0]
    bond_right = jnp.einsum(
        "wbc,kc->wbk", right_next, bond_tensor[0], preferred_element_type=jnp.float32
    ).astype(jnp.bfloat16)
    carried_moved = lax.all_to_all(carried, "sector", split_axis=2, concat_axis=1, tiled=True)
    bond_moved = lax.all_to_all(bond_right, "sector", split_axis=2, concat_axis=1, tiled=True)
    carried_moved = carried_moved.reshape((width, states) + carried_moved.shape[1:])
    env_new = jnp.einsum(
        "wsac,asb->wcb", carried_moved, gathered, preferred_element_type=jnp.float32
    ).astype(jnp.bfloat16)
    image_rows = lax.psum_scatter(
        jnp.einsum("wka,wbk->ab", env_new, bond_moved, preferred_element_type=jnp.float32),
        "sector",
        scatter_dimension=0,
        tiled=True,
    )
    return (env_new[None], image_rows.astype(jnp.bfloat16)[None])


def solution(mesh):
    def body(env_left, site_tensor, mpo_tensor, env_right, bond_tensor):
        width, rows, bond = env_left.shape[1:]
        columns = bond // mesh.shape["sector"]
        tiled = rows % LANES == 0 and columns % LANES == 0 and width % CHUNKS == 0 and rows % (16 * SHIFTS) == 0
        tiled = tiled and mesh.shape["sector"] % 2 == 0 and mesh.shape["region"] > 2
        step = local if tiled else plain_local
        return step(env_left, site_tensor, mpo_tensor, env_right, bond_tensor)

    return jax.shard_map(
        body,
        mesh=mesh,
        in_specs=(
            P("region", None, "sector", None),
            P("region", "sector", None, None),
            P("region", None, None, None, None),
            P("region", None, "sector", None),
            P("region", None, None),
        ),
        out_specs=(P("region", None, "sector", None), P("region", "sector", None)),
        check_vma=False,
    )
```

```python
import functools

import jax
import jax.numpy as jnp
from jax import lax
from jax.experimental import pallas as pl
from jax.experimental.pallas import tpu as pltpu
from jax.sharding import PartitionSpec as P

GROUP = 16
LANES = 128
HALVES = 2
CHUNKS = 2
SHIFTS = 4
CROSS = (4, 6, 11, 12)
PRODUCT = (0, 1, 2, 3)
OWN_LATER = 2
ABSORB = 7
SPLIT = 4
VMEM_LIMIT = 60 * 1024 * 1024


def shifted(block, axis, distance):
    devices = range(lax.axis_size(axis))
    route = [((i - distance) % len(devices), i) for i in devices]
    return lax.ppermute(block, axis, route)


MESH = pl.DeviceIdType.MESH


def carried_into(mix_ref, env_ref, site_ref, out_ref):
    width, rows, bond = env_ref.shape
    _, states, _, columns = site_ref.shape
    sub = columns // 2
    tile = min(rows, LANES)
    mix = mix_ref[...]
    mix_high = mix.astype(jnp.bfloat16)
    mix_low = (mix - mix_high.astype(jnp.float32)).astype(jnp.bfloat16)
    dot = functools.partial(jnp.dot, preferred_element_type=jnp.float32)
    step = width // CHUNKS

    def rows_of(i, carry):
        top = pl.multiple_of(i * tile, tile)
        env = env_ref[:, pl.ds(top, tile)].reshape(width * tile, bond)
        half_done = [
            dot(env, site_ref[:, t].reshape(bond, columns)).reshape(width, tile, columns)
            for t in range(states)
        ]
        for g in range(tile // GROUP):
            span = slice(g * GROUP, (g + 1) * GROUP)
            x = jnp.concatenate(
                [h[:, span].reshape(width * GROUP, columns) for h in half_done], axis=0
            )
            high = x.astype(jnp.bfloat16)
            low = (x - high.astype(jnp.float32)).astype(jnp.bfloat16)
            y = dot(mix_high, high) + dot(mix_high, low) + dot(mix_low, high)
            y = y.astype(jnp.bfloat16).reshape(width, states, GROUP, columns)
            for i in range(CHUNKS):
                for j in range(2):
                    out_ref[i, j, :, :, pl.ds(top + g * GROUP, GROUP), :] = y[
                        i * step : (i + 1) * step, :, :, j * sub : (j + 1) * sub
                    ]
        return carry

    lax.fori_loop(0, rows // tile, rows_of, 0)


def greet(parts):
    me = lax.axis_index("sector")
    barrier = pltpu.get_barrier_semaphore()
    for d in range(1, parts):
        pl.semaphore_signal(
            barrier, inc=1, device_id={"sector": lax.rem(me + d, parts)}, device_id_type=MESH
        )
    return barrier


def remote(src, dst, send, recv, target):
    return pltpu.make_async_remote_copy(
        src_ref=src, dst_ref=dst, send_sem=send, recv_sem=recv,
        device_id=target, device_id_type=MESH,
    )


def head_kernel(
    mix_ref, right_hbm, site_hbm, bond_hbm, left_hbm,
    gathered, moved, landed, carried,
    right, bond_ref, blocks, left, tiles, outs,
    shift_send, shift_recv, site_send, site_recv,
    block_send, block_recv, swap_send, swap_recv, out_sem, tile_sem, local_sem,
):
    _, parts, states, _, _ = gathered.shape
    width, rows, bond = right_hbm.shape
    columns = bond // parts
    line = parts // 2
    me = lax.axis_index("sector")
    z, y = me // 2, lax.rem(me, 2)
    regions = lax.axis_size("region")
    region = lax.axis_index("region")
    before = lax.rem(region + regions - 1, regions)
    after = lax.rem(region + 1, regions)
    part_rows = rows // SHIFTS
    twin = 2 * z + 1 - y

    barrier = greet(parts)
    for other in (before, after):
        pl.semaphore_signal(barrier, inc=1, device_id={"region": other}, device_id_type=MESH)
    pl.semaphore_wait(barrier, parts + 1)

    def shift(q):
        span = pl.ds(q * part_rows, part_rows)
        return remote(
            right_hbm.at[:, span], right.at[:, span], shift_send.at[q], shift_recv.at[q],
            {"region": before},
        )

    def hop(way, source, p, t, target, first=False):
        there = gathered.at[p, source, t]
        return remote(
            site_hbm.at[p, t] if first else there, there,
            site_send.at[way, p, source, t], site_recv.at[p, source, t], {"sector": target},
        )

    def outward(source, p, t, first, ways, act):
        for way in ways:
            there = {0: me + 2, 1: me - 2, 2: twin}[way]
            if way == 2:
                act(hop(way, source, p, t, there, first))
            else:
                inside = z + 1 < line if way == 0 else z >= 1

                @pl.when(inside)
                def _():
                    act(hop(way, source, p, t, there, first))

    def target_of(d):
        return lax.rem(me + 1 + d, parts)

    def block(q, d):
        return remote(
            blocks.at[q, d], moved.at[q, me], block_send.at[q, d], block_recv.at[q, me],
            {"sector": target_of(d)},
        )

    def block_in(q, d):
        source = target_of(d)
        return remote(
            blocks.at[q, d], moved.at[q, source], block_send.at[q, d], block_recv.at[q, source],
            {"sector": source},
        )

    def own_block(q):
        return pltpu.make_async_copy(
            blocks.at[q, parts - 1], moved.at[q, me], block_send.at[q, parts - 1]
        )

    def start(copy):
        copy.start()

    def settle(copy):
        copy.wait_send()

    for q in range(SHIFTS):
        shift(q).start()
    for t in range(states):
        outward(me, 0, t, True, (0, 1, 2), start)
    load_bond = pltpu.make_async_copy(bond_hbm, bond_ref, local_sem.at[0])
    load_bond.start()
    load_left = pltpu.make_async_copy(left_hbm, left, local_sem.at[1])
    load_left.start()
    keep_site = [
        pltpu.make_async_copy(site_hbm.at[p], gathered.at[p, me], local_sem.at[2 + p])
        for p in range(HALVES)
    ]
    for copy in keep_site:
        copy.start()
    load_bond.wait()

    def product(q):
        shift(q).wait_recv()
        span = pl.ds(q * part_rows, part_rows)
        x = right[:, span].reshape(width * part_rows, bond)

        def step(d, carry):
            j = target_of(d)
            out = lax.dot_general(
                x,
                bond_ref[pl.ds(pl.multiple_of(j * columns, columns), columns), :],
                (((1,), (1,)), ((), ())),
                preferred_element_type=jnp.float32,
            )
            blocks[q, d] = out.astype(jnp.bfloat16).reshape(width, part_rows, columns)
            return carry

        lax.fori_loop(0, parts, step, 0)

    def dispatch(q, cross):
        def step(d, carry):
            same = lax.rem(target_of(d), 2) == y

            @pl.when(jnp.logical_not(same) if cross else same)
            def _():
                block(q, d).start()

            return carry

        lax.fori_loop(0, parts - 1, step, 0)
        if not cross:
            own_block(q).start()

    hops = (line - 1) * states
    ticks = HALVES * hops

    def relayed(i, act, receive):
        p, distance, t = i // hops, lax.rem(i, hops) // states + 1, lax.rem(i, states)
        for way, source in ((0, me - 2 * distance), (1, me + 2 * distance)):
            there = z >= distance if way == 0 else z + distance < line

            @pl.when(there)
            def _():
                if receive:
                    hop(way, source, p, t, twin).wait_recv()
                outward(source, p, t, False, (way, 2), act)

    def tile_copies(a):
        p, slot = a // line, lax.rem(a, 2)
        m = lax.rem(z + 1 + a, line)
        span = pl.ds(pl.multiple_of(m * columns, columns), columns)
        mine = pltpu.make_async_copy(
            site_hbm.at[p, :, :, span], tiles.at[slot, me], tile_sem.at[slot, parts - 1]
        )
        return mine, lambda d: pltpu.make_async_copy(
            gathered.at[p, target_of(d), :, :, span], tiles.at[slot, target_of(d)],
            tile_sem.at[slot, d],
        )

    def each(count, act):
        def step(d, carry):
            act(d)
            return carry

        lax.fori_loop(0, count, step, 0)

    def load_tile(a):
        mine, other = tile_copies(a)
        mine.start()
        each(parts - 1, lambda d: other(d).start())

    def have_tile(a):
        mine, other = tile_copies(a)
        mine.wait()
        each(parts - 1, lambda d: other(d).wait())

    def swap(a, i, j):
        to = 2 * lax.rem(z + 1 + a, line) + j
        return to, remote(
            outs.at[a, i, j], landed.at[i, me], swap_send.at[i, to], swap_recv.at[i, me],
            {"sector": to},
        ), pltpu.make_async_copy(outs.at[a, i, j], landed.at[i, me], swap_send.at[i, to])

    def store(a, i, j):
        to = 2 * lax.rem(z + 1 + a, line) + j
        slot = lax.rem(a, 2)
        return pltpu.make_async_copy(
            outs.at[line + slot, i, j], carried.at[i, to], out_sem.at[slot, i, j]
        )

    def absorb(a):
        p = a // line

        @pl.when(lax.rem(a, line) == 0)
        def _():
            for other in range(line):
                for t in range(states):
                    hop(2, 2 * other + 1 - y, p, t, twin).wait_recv()
            load_tile(a)

        have_tile(a)

        @pl.when(lax.rem(a, line) < line - 1)
        def _():
            load_tile(a + 1)

        @pl.when(a >= line + 2)
        def _():
            for i in range(CHUNKS):
                for j in range(2):
                    store(a - 2, i, j).wait()

        slot = jnp.where(p == 0, a, line + lax.rem(a, 2))
        carried_into(mix_ref, left, tiles.at[lax.rem(a, 2)], outs.at[slot])
        for i in range(CHUNKS):
            for j in range(2):

                @pl.when(p == 0)
                def _():
                    to, far, near = swap(a, i, j)

                    @pl.when(to == me)
                    def _():
                        near.start()

                    @pl.when(to != me)
                    def _():
                        far.start()

                @pl.when(p > 0)
                def _():
                    store(a, i, j).start()

    def tick(i, carry):
        @pl.when(i < ticks)
        def _():
            relayed(i, start, True)

        @pl.when(i == OWN_LATER)
        def _():
            for p in range(1, HALVES):
                for t in range(states):
                    outward(me, p, t, True, (0, 1, 2), start)

        for q in range(SHIFTS):

            @pl.when(i == PRODUCT[q])
            def _():
                product(q)
                dispatch(q, False)

            @pl.when(i == CROSS[q])
            def _():
                dispatch(q, True)

        @pl.when(i == ABSORB)
        def _():
            load_left.wait()

        early = jnp.logical_and(i >= ABSORB, i < ABSORB + line)

        @pl.when(jnp.logical_or(early, i >= ticks))
        def _():
            absorb(jnp.where(i >= ticks, i - ticks + line, i - ABSORB))

        return carry

    lax.fori_loop(0, ticks + line, tick, 0)

    for copy in keep_site:
        copy.wait()
    for q in range(SHIFTS):
        shift(q).wait_send()
    for p in range(HALVES):
        for t in range(states):
            outward(me, p, t, True, (0, 1, 2), settle)
    each(ticks, lambda i: relayed(i, settle, False))

    def finish(i):
        q, d = i // (parts - 1), lax.rem(i, parts - 1)
        block(q, d).wait_send()
        block_in(q, d).wait_recv()

    each(SHIFTS * (parts - 1), finish)
    for q in range(SHIFTS):
        own_block(q).wait()

    def swapped(a):
        for i in range(CHUNKS):
            for j in range(2):
                to, far, near = swap(a, i, j)

                @pl.when(to == me)
                def _():
                    near.wait()

                @pl.when(to != me)
                def _():
                    far.wait_send()
                    remote(
                        outs.at[a, i, j], landed.at[i, to], swap_send.at[i, to],
                        swap_recv.at[i, to], {"sector": to},
                    ).wait_recv()

    each(line, swapped)
    for a in range(2 * line - 2, 2 * line):
        for i in range(CHUNKS):
            for j in range(2):
                store(a, i, j).wait()


def head(env_left, site, mpo, env_right, bond_tensor, parts):
    width, rows, bond = env_left.shape
    _, states, depth, _ = site.shape
    columns = bond // parts
    eye = jnp.eye(GROUP, dtype=jnp.float32)
    side = width * states * GROUP
    mix = jnp.einsum("vwst,ij->wsitvj", mpo, eye, precision=lax.Precision.HIGHEST).reshape(side, side)
    part_rows = rows // SHIFTS
    carried = (width // CHUNKS, states, rows, columns // HALVES)
    bf16 = jnp.bfloat16
    anywhere = pl.BlockSpec(memory_space=pl.ANY)
    dma = pltpu.SemaphoreType.DMA
    return pl.pallas_call(
        head_kernel,
        in_specs=[pl.BlockSpec(memory_space=pltpu.VMEM)] + [anywhere] * 4,
        out_specs=[anywhere] * 4,
        out_shape=[
            jax.ShapeDtypeStruct((HALVES, parts, states, depth, bond // HALVES), bf16),
            jax.ShapeDtypeStruct((SHIFTS, parts, width, part_rows, columns), bf16),
            jax.ShapeDtypeStruct((CHUNKS, parts) + carried, bf16),
            jax.ShapeDtypeStruct((CHUNKS, parts) + carried, bf16),
        ],
        scratch_shapes=[
            pltpu.VMEM((width, rows, bond), bf16),
            pltpu.VMEM((bond, bond), bf16),
            pltpu.VMEM((SHIFTS, parts, width, part_rows, columns), bf16),
            pltpu.VMEM((width, rows, bond), bf16),
            pltpu.VMEM((2, parts, states, depth, columns), bf16),
            pltpu.VMEM((parts // 2 + 2, CHUNKS, 2) + carried, bf16),
            dma((SHIFTS,)),
            dma((SHIFTS,)),
            dma((3, HALVES, parts, states)),
            dma((HALVES, parts, states)),
            dma((SHIFTS, parts)),
            dma((SHIFTS, parts)),
            dma((CHUNKS, parts)),
            dma((CHUNKS, parts)),
            dma((2, CHUNKS, 2)),
            dma((2, parts)),
            dma((2 + HALVES,)),
        ],
        compiler_params=pltpu.CompilerParams(
            vmem_limit_bytes=VMEM_LIMIT, collective_id=0, has_side_effects=True
        ),
        cost_estimate=pl.CostEstimate(
            flops=3 * width * rows * bond * bond * states,
            bytes_accessed=128 * 1024 * 1024,
            transcendentals=0,
        ),
    )(mix, env_right, site, bond_tensor, env_left)


def rest_kernel(
    gathered, moved, landed_first, carried,
    env_out, image_out, landed,
    x, turned, env, bond_in, keep, pair_out, pair_in, line_out, line_in, done,
    swap_send, swap_recv, pair_send, pair_recv, line_send, line_recv,
    load_sem, env_sem, out_sem,
):
    _, parts, states, depth, _ = gathered.shape
    _, _, count, _, _, sub = landed.shape
    width, columns, bond = env_out.shape
    part_rows = moved.shape[3]
    line = parts // 2
    group = bond_in.shape[0]
    splits = parts // group
    steps = SHIFTS * splits
    me = lax.axis_index("sector")
    z, y = me // 2, lax.rem(me, 2)
    twin = 2 * z + 1 - y

    pl.semaphore_wait(greet(parts), parts - 1)

    def swap(b, d, receiving=False):
        j = lax.rem(me + 1 + d, parts)
        owner = j if receiving else me
        return remote(
            carried.at[b, j], landed.at[b, owner], swap_send.at[b, d], swap_recv.at[b, owner],
            {"sector": j},
        )

    def dispatch(b):
        def step(d, carry):
            swap(b, d).start()
            return carry

        lax.fori_loop(0, parts - 1, step, 0)

    def fill(b, d, first):
        n = lax.rem(me + 1 + d, parts)
        origin = landed_first if first else landed
        return pltpu.make_async_copy(origin.at[b, n], x.at[n], load_sem.at[d])

    def fill_own(b, first):
        origin = landed_first if first else carried
        return pltpu.make_async_copy(origin.at[b, me], x.at[me], load_sem.at[parts - 1])

    def turn(n, carry):
        for s in range(states):
            at = pl.multiple_of((n * states + s) * depth, depth)
            for v in range(count):
                turned[v * sub : (v + 1) * sub, pl.ds(at, depth)] = x[n, v, s].T
        return carry

    def env_body(*refs):
        out_ref = refs[-1]
        tile = out_ref.shape[-1]
        totals = []
        for site_ref in refs[:-1]:
            site = site_ref[0].reshape(parts * states * depth, site_ref.shape[-1])
            totals.append(
                jnp.dot(turned[...], site, preferred_element_type=jnp.float32)
                .astype(jnp.bfloat16)
                .reshape(count, sub, site_ref.shape[-1])
            )
        for k in range(tile // sub):
            piece = slice(k // HALVES * sub, (k // HALVES + 1) * sub)
            out_ref[:, :, k * sub : (k + 1) * sub] = totals[k % HALVES][:, :, piece]

    def spot(ref, i):
        p, b = i // CHUNKS, lax.rem(i, CHUNKS)
        return ref.at[
            pl.ds(b * count, count), pl.ds(pl.multiple_of(p * sub, sub), sub)
        ]

    def reload(i):
        return pltpu.make_async_copy(spot(env_out, i), spot(env, i), env_sem.at[i])

    tile = 2 * LANES
    for b in range(CHUNKS):
        dispatch(b)

    def advance(i, carry):
        b = lax.rem(i, CHUNKS)
        for first in (True, False):

            @pl.when(i < CHUNKS if first else i >= CHUNKS)
            def _():
                fill_own(b, first).start()

                def collect(d, carry):
                    if not first:
                        swap(b, d, True).wait_recv()
                    fill(b, d, first).start()
                    return carry

                lax.fori_loop(0, parts - 1, collect, 0)

        def filled(d, carry):
            fill(b, d, True).wait()
            return carry

        lax.fori_loop(0, parts - 1, filled, 0)
        fill_own(b, True).wait()
        lax.fori_loop(0, parts, turn, 0)
        pltpu.emit_pipeline(
            env_body,
            grid=(bond // (tile * HALVES),),
            in_specs=[
                pl.BlockSpec(
                    (1, parts, states, depth, tile),
                    functools.partial(lambda p, j: (p, 0, 0, 0, j), p),
                )
                for p in range(HALVES)
            ],
            out_specs=[pl.BlockSpec((count, sub, tile * HALVES), lambda j: (0, 0, j))],
        )(*[gathered] * HALVES, spot(env_out, i))
        reload(i).start()
        return carry

    lax.fori_loop(0, HALVES * CHUNKS, advance, 0)
    for i in range(HALVES * CHUNKS):
        reload(i).wait()

    def pair_copy(u):
        return remote(
            pair_out.at[u], pair_in.at[u], pair_send.at[u], pair_recv.at[u], {"sector": twin}
        )

    def line_copy(u, t, way):
        slot = t + 1 if way == 0 else t
        return remote(
            line_out.at[u, t], line_in.at[u, slot], line_send.at[u, t], line_recv.at[u, slot],
            {"sector": me + 2 if way == 0 else me - 2},
        )

    def dot(a, b):
        return jnp.dot(a, b, preferred_element_type=jnp.float32)

    def take(u, i):
        q, n = u // splits, lax.rem(u, splits) * group + i
        return pltpu.make_async_copy(
            moved.at[q, n], bond_in.at[i], load_sem.at[i]
        )

    def image(u):
        for i in range(group):
            take(u, i).start()
        for i in range(group):
            take(u, i).wait()
        left = jnp.concatenate(
            [bond_in[:, w].reshape(group * part_rows, columns) for w in range(width)], axis=1
        )

        def right(j):
            at = pl.multiple_of(j * columns, columns)
            return env[:, :, pl.ds(at, columns)].reshape(width * columns, columns)

        for t in range(line):
            pair_out[u, t] = dot(left, right(2 * t + 1 - y)).astype(jnp.bfloat16)
        for t in range(line):
            keep[u, t] = dot(left, right(2 * t + y))
        pair_copy(u).start()

    def paired(u):
        pair_copy(u).wait_recv()
        keep[u] = keep[u] + pair_in[u].astype(jnp.float32)

    def relay(s, way):
        first = z if way == 0 else line - 1 - z
        u = s - 1 - first
        live = jnp.logical_and(u >= 0, u < steps)
        for t in range(line):
            sends = jnp.logical_and(live, t > z if way == 0 else t < z)

            @pl.when(jnp.logical_and(sends, first == 0))
            def _():
                line_out[u, t] = keep[u, t].astype(jnp.bfloat16)

            @pl.when(jnp.logical_and(sends, first > 0))
            def _():
                slot = t + 1 if way == 0 else t
                line_copy(u, t, way).wait_recv()
                line_out[u, t] = (
                    keep[u, t] + line_in[u, slot].astype(jnp.float32)
                ).astype(jnp.bfloat16)

    def send_on(s, way):
        first = z if way == 0 else line - 1 - z
        u = s - 1 - first
        live = jnp.logical_and(u >= 0, u < steps)
        for t in range(line):

            @pl.when(jnp.logical_and(live, t > z if way == 0 else t < z))
            def _():
                line_copy(u, t, way).start()

    def result(u):
        return pltpu.make_async_copy(done.at[u], image_out.at[u], out_sem.at[u])

    def total(u):
        @pl.when(z > 0)
        def _():
            line_copy(u, z, 0).wait_recv()
            keep[u, z] = keep[u, z] + line_in[u, z + 1].astype(jnp.float32)

        @pl.when(z < line - 1)
        def _():
            line_copy(u, z, 1).wait_recv()
            keep[u, z] = keep[u, z] + line_in[u, z].astype(jnp.float32)

        done[u] = keep[u, z].astype(jnp.bfloat16)

    def pass_on(s, carry):
        @pl.when(s < steps)
        def _():
            image(s)

        @pl.when(jnp.logical_and(s >= 1, s <= steps))
        def _():
            paired(s - 1)

        relay(s, 0)
        relay(s, 1)

        @pl.when(s >= line)
        def _():
            total(s - line)

        send_on(s, 0)
        send_on(s, 1)

        @pl.when(s >= line)
        def _():
            result(s - line).start()

        return carry

    lax.fori_loop(0, steps + line, pass_on, 0)

    def sent(b, carry):
        def step(d, carry):
            swap(b, d).wait_send()
            return carry

        return lax.fori_loop(0, parts - 1, step, carry)

    lax.fori_loop(0, CHUNKS, sent, 0)

    def ended(u, carry):
        pair_copy(u).wait_send()
        result(u).wait()
        for t in range(line):
            @pl.when(t > z)
            def _():
                line_copy(u, t, 0).wait_send()

            @pl.when(t < z)
            def _():
                line_copy(u, t, 1).wait_send()

        return carry

    lax.fori_loop(0, steps, ended, 0)


def rest_of(gathered, moved, landed, carried):
    _, parts, states, depth, _ = gathered.shape
    _, _, count, _, _, sub = carried.shape
    width, columns = count * CHUNKS, sub * HALVES
    bond = parts * columns
    part_rows = moved.shape[3]
    line = parts // 2
    group = max(parts // SPLIT, 1)
    steps = SHIFTS * (parts // group)
    block = (group * part_rows, columns)
    anywhere = pl.BlockSpec(memory_space=pl.ANY)
    dma = pltpu.SemaphoreType.DMA
    bf16 = jnp.bfloat16
    return pl.pallas_call(
        rest_kernel,
        in_specs=[anywhere] * 4,
        out_specs=[anywhere] * 3,
        out_shape=[
            jax.ShapeDtypeStruct((width, columns, bond), bf16),
            jax.ShapeDtypeStruct((steps,) + block, bf16),
            jax.ShapeDtypeStruct(carried.shape, bf16),
        ],
        scratch_shapes=[
            pltpu.VMEM(carried.shape[1:], bf16),
            pltpu.VMEM((count * sub, parts * states * depth), bf16),
            pltpu.VMEM((width, columns, bond), bf16),
            pltpu.VMEM((group, width, part_rows, columns), bf16),
            pltpu.VMEM((steps, line) + block, jnp.float32),
            pltpu.VMEM((steps, line) + block, bf16),
            pltpu.VMEM((steps, line) + block, bf16),
            pltpu.VMEM((steps, line) + block, bf16),
            pltpu.VMEM((steps, line + 1) + block, bf16),
            pltpu.VMEM((steps,) + block, bf16),
            dma((CHUNKS, parts)),
            dma((CHUNKS, parts)),
            dma((steps,)),
            dma((steps,)),
            dma((steps, line)),
            dma((steps, line + 1)),
            dma((parts,)),
            dma((HALVES * CHUNKS,)),
            dma((steps,)),
        ],
        compiler_params=pltpu.CompilerParams(
            vmem_limit_bytes=VMEM_LIMIT, collective_id=1, has_side_effects=True
        ),
        cost_estimate=pl.CostEstimate(
            flops=3 * width * columns * parts * states * depth * bond,
            bytes_accessed=128 * 1024 * 1024,
            transcendentals=0,
        ),
    )(gathered, moved, landed, carried)


def local(env_left, site_tensor, mpo_tensor, env_right, bond_tensor):
    parts = lax.axis_size("sector")
    _, rows, bond = env_left.shape[1:]
    columns = bond // parts
    site = site_tensor[0].reshape(rows, -1, parts, HALVES, columns // HALVES)
    site = site.transpose(3, 1, 0, 2, 4).reshape(HALVES, -1, rows, bond // HALVES)
    gathered, moved, landed, carried = head(
        env_left[0], site, mpo_tensor[0], env_right[0], bond_tensor[0], parts,
    )
    env_new, image, _ = rest_of(gathered, moved, landed, carried)
    image_rows = (
        image.reshape(SHIFTS, parts, rows // SHIFTS, columns)
        .transpose(3, 1, 0, 2)
        .reshape(columns, bond)
    )
    return (env_new[None], image_rows[None])


def plain_local(env_left, site_tensor, mpo_tensor, env_right, bond_tensor):
    width = env_left.shape[1]
    states = site_tensor.shape[2]
    gathered = lax.all_gather(site_tensor, "sector", axis=1, tiled=True)[0]
    half_done = jnp.einsum(
        "wak,ksc->wasc", env_left[0], gathered, preferred_element_type=jnp.float32
    )
    carried = jnp.einsum(
        "vwst,vatc->wsac", mpo_tensor[0], half_done, precision=lax.Precision.HIGHEST
    ).astype(jnp.bfloat16)
    carried = carried.reshape((width * states,) + carried.shape[2:])
    right_next = shifted(env_right, "region", -1)[0]
    bond_right = jnp.einsum(
        "wbc,kc->wbk", right_next, bond_tensor[0], preferred_element_type=jnp.float32
    ).astype(jnp.bfloat16)
    carried_moved = lax.all_to_all(carried, "sector", split_axis=2, concat_axis=1, tiled=True)
    bond_moved = lax.all_to_all(bond_right, "sector", split_axis=2, concat_axis=1, tiled=True)
    carried_moved = carried_moved.reshape((width, states) + carried_moved.shape[1:])
    env_new = jnp.einsum(
        "wsac,asb->wcb", carried_moved, gathered, preferred_element_type=jnp.float32
    ).astype(jnp.bfloat16)
    image_rows = lax.psum_scatter(
        jnp.einsum("wka,wbk->ab", env_new, bond_moved, preferred_element_type=jnp.float32),
        "sector",
        scatter_dimension=0,
        tiled=True,
    )
    return (env_new[None], image_rows.astype(jnp.bfloat16)[None])


def solution(mesh):
    def body(env_left, site_tensor, mpo_tensor, env_right, bond_tensor):
        width, rows, bond = env_left.shape[1:]
        columns = bond // mesh.shape["sector"]
        tiled = rows % LANES == 0 and columns % (HALVES * LANES) == 0 and width % CHUNKS == 0 and rows % (16 * SHIFTS) == 0
        tiled = tiled and mesh.shape["sector"] % 2 == 0 and mesh.shape["region"] > 2
        step = local if tiled else plain_local
        return step(env_left, site_tensor, mpo_tensor, env_right, bond_tensor)

    return jax.shard_map(
        body,
        mesh=mesh,
        in_specs=(
            P("region", None, "sector", None),
            P("region", "sector", None, None),
            P("region", None, None, None, None),
            P("region", None, "sector", None),
            P("region", None, None),
        ),
        out_specs=(P("region", None, "sector", None), P("region", "sector", None)),
        check_vma=False,
    )
```

```python
import functools

import jax
import jax.numpy as jnp
from jax import lax
from jax.experimental import pallas as pl
from jax.experimental.pallas import tpu as pltpu
from jax.sharding import PartitionSpec as P

GROUP = 16
LANES = 128
HALVES = 2
CHUNKS = 4
LATE_FROM = 0
AHEAD = 4
LATE_AFTER = 5
SHIFTS = 4
CROSS = (4, 6, 11, 12)
PRODUCT = (0, 1, 2, 3)
OWN_LATER = 2
ABSORB = 7
SPLIT = 4
VMEM_LIMIT = 60 * 1024 * 1024


def shifted(block, axis, distance):
    devices = range(lax.axis_size(axis))
    route = [((i - distance) % len(devices), i) for i in devices]
    return lax.ppermute(block, axis, route)


MESH = pl.DeviceIdType.MESH


def carried_into(mix_ref, env_ref, site_ref, out_ref):
    width, rows, bond = env_ref.shape
    _, states, _, columns = site_ref.shape
    sub = columns // 2
    tile = min(rows, LANES)
    mix = mix_ref[...]
    mix_high = mix.astype(jnp.bfloat16)
    mix_low = (mix - mix_high.astype(jnp.float32)).astype(jnp.bfloat16)
    dot = functools.partial(jnp.dot, preferred_element_type=jnp.float32)
    step = width // CHUNKS

    def rows_of(i, carry):
        top = pl.multiple_of(i * tile, tile)
        env = env_ref[:, pl.ds(top, tile)].reshape(width * tile, bond)
        half_done = [
            dot(env, site_ref[:, t].reshape(bond, columns)).reshape(width, tile, columns)
            for t in range(states)
        ]
        for g in range(tile // GROUP):
            span = slice(g * GROUP, (g + 1) * GROUP)
            x = jnp.concatenate(
                [h[:, span].reshape(width * GROUP, columns) for h in half_done], axis=0
            )
            high = x.astype(jnp.bfloat16)
            low = (x - high.astype(jnp.float32)).astype(jnp.bfloat16)
            y = dot(mix_high, high) + dot(mix_high, low) + dot(mix_low, high)
            y = y.astype(jnp.bfloat16).reshape(width, states, GROUP, columns)
            for i in range(CHUNKS):
                for j in range(2):
                    out_ref[i, j, :, :, pl.ds(top + g * GROUP, GROUP), :] = y[
                        i * step : (i + 1) * step, :, :, j * sub : (j + 1) * sub
                    ]
        return carry

    lax.fori_loop(0, rows // tile, rows_of, 0)


def inner(parts, device):
    z = device // 2
    return jnp.logical_and(z > 0, z < parts // 2 - 1)


def waits(parts, source, target, q):
    same = lax.rem(source + target, 2) == 0
    return jnp.logical_and(jnp.logical_and(same, inner(parts, source)), q >= LATE_FROM)


def greet(parts):
    me = lax.axis_index("sector")
    barrier = pltpu.get_barrier_semaphore()
    for d in range(1, parts):
        pl.semaphore_signal(
            barrier, inc=1, device_id={"sector": lax.rem(me + d, parts)}, device_id_type=MESH
        )
    return barrier


def remote(src, dst, send, recv, target):
    return pltpu.make_async_remote_copy(
        src_ref=src, dst_ref=dst, send_sem=send, recv_sem=recv,
        device_id=target, device_id_type=MESH,
    )


def head_kernel(
    mix_ref, right_hbm, site_hbm, bond_hbm, left_hbm,
    gathered, moved, landed, carried, late,
    right, bond_ref, blocks, left, tiles, outs,
    shift_send, shift_recv, site_send, site_recv,
    block_send, block_recv, swap_send, swap_recv, out_sem, tile_sem, local_sem,
):

    _, parts, states, _, _ = gathered.shape
    width, rows, bond = right_hbm.shape
    columns = bond // parts
    line = parts // 2
    me = lax.axis_index("sector")
    z, y = me // 2, lax.rem(me, 2)
    regions = lax.axis_size("region")
    region = lax.axis_index("region")
    before = lax.rem(region + regions - 1, regions)
    after = lax.rem(region + 1, regions)
    part_rows = rows // SHIFTS
    twin = 2 * z + 1 - y

    barrier = greet(parts)
    for other in (before, after):
        pl.semaphore_signal(barrier, inc=1, device_id={"region": other}, device_id_type=MESH)
    pl.semaphore_wait(barrier, parts + 1)

    def shift(q):
        span = pl.ds(q * part_rows, part_rows)
        return remote(
            right_hbm.at[:, span], right.at[:, span], shift_send.at[q], shift_recv.at[q],
            {"region": before},
        )

    def hop(way, source, p, t, target, first=False):
        there = gathered.at[p, source, t]
        return remote(
            site_hbm.at[p, t] if first else there, there,
            site_send.at[way, p, source, t], site_recv.at[p, source, t], {"sector": target},
        )

    def outward(source, p, t, first, ways, act):
        for way in ways:
            there = {0: me + 2, 1: me - 2, 2: twin}[way]
            if way == 2:
                act(hop(way, source, p, t, there, first))
            else:
                inside = z + 1 < line if way == 0 else z >= 1

                @pl.when(inside)
                def _():
                    act(hop(way, source, p, t, there, first))

    def target_of(d):
        return lax.rem(me + 1 + d, parts)

    def block(q, d):
        return remote(
            blocks.at[q, d], moved.at[q, me], block_send.at[q, d], block_recv.at[q, me],
            {"sector": target_of(d)},
        )

    def block_in(q, d):
        source = target_of(d)
        return remote(
            blocks.at[q, d], moved.at[q, source], block_send.at[q, d], block_recv.at[q, source],
            {"sector": source},
        )

    def held(q, d):
        return waits(parts, me, target_of(d), q)

    def put_off(q, d):
        return pltpu.make_async_copy(
            blocks.at[q, d], late.at[q, target_of(d) // 2], block_send.at[q, d]
        )

    def own_block(q):
        return pltpu.make_async_copy(
            blocks.at[q, parts - 1], moved.at[q, me], block_send.at[q, parts - 1]
        )

    def start(copy):
        copy.start()

    def settle(copy):
        copy.wait_send()

    for q in range(SHIFTS):
        shift(q).start()
    for t in range(states):
        outward(me, 0, t, True, (0, 1, 2), start)
    load_bond = pltpu.make_async_copy(bond_hbm, bond_ref, local_sem.at[0])
    load_bond.start()
    load_left = pltpu.make_async_copy(left_hbm, left, local_sem.at[1])
    load_left.start()
    keep_site = [
        pltpu.make_async_copy(site_hbm.at[p], gathered.at[p, me], local_sem.at[2 + p])
        for p in range(HALVES)
    ]
    for copy in keep_site:
        copy.start()
    load_bond.wait()

    def product(q):
        shift(q).wait_recv()
        span = pl.ds(q * part_rows, part_rows)
        x = right[:, span].reshape(width * part_rows, bond)

        def step(d, carry):
            j = target_of(d)
            out = lax.dot_general(
                x,
                bond_ref[pl.ds(pl.multiple_of(j * columns, columns), columns), :],
                (((1,), (1,)), ((), ())),
                preferred_element_type=jnp.float32,
            )
            blocks[q, d] = out.astype(jnp.bfloat16).reshape(width, part_rows, columns)
            return carry

        lax.fori_loop(0, parts, step, 0)

    def dispatch(q, cross):
        def step(d, carry):
            same = lax.rem(target_of(d), 2) == y

            @pl.when(jnp.logical_not(same) if cross else jnp.logical_and(same, jnp.logical_not(held(q, d))))
            def _():
                block(q, d).start()

            if not cross:

                @pl.when(held(q, d))
                def _():
                    put_off(q, d).start()

            return carry

        lax.fori_loop(0, parts - 1, step, 0)
        if not cross:
            own_block(q).start()

    hops = (line - 1) * states
    ticks = HALVES * hops

    def relayed(i, act, receive):
        p, distance, t = i // hops, lax.rem(i, hops) // states + 1, lax.rem(i, states)
        for way, source in ((0, me - 2 * distance), (1, me + 2 * distance)):
            there = z >= distance if way == 0 else z + distance < line

            @pl.when(there)
            def _():
                if receive:
                    hop(way, source, p, t, twin).wait_recv()
                outward(source, p, t, False, (way, 2), act)

    def tile_copies(a):
        p, slot = a // line, lax.rem(a, 2)
        m = lax.rem(z + 1 + a, line)
        span = pl.ds(pl.multiple_of(m * columns, columns), columns)
        mine = pltpu.make_async_copy(
            site_hbm.at[p, :, :, span], tiles.at[slot, me], tile_sem.at[slot, parts - 1]
        )
        return mine, lambda d: pltpu.make_async_copy(
            gathered.at[p, target_of(d), :, :, span], tiles.at[slot, target_of(d)],
            tile_sem.at[slot, d],
        )

    def each(count, act):
        def step(d, carry):
            act(d)
            return carry

        lax.fori_loop(0, count, step, 0)

    def load_tile(a):
        mine, other = tile_copies(a)
        mine.start()
        each(parts - 1, lambda d: other(d).start())

    def have_tile(a):
        mine, other = tile_copies(a)
        mine.wait()
        each(parts - 1, lambda d: other(d).wait())

    def swap(a, i, j):
        to = 2 * lax.rem(z + 1 + a, line) + j
        return to, remote(
            outs.at[a, i, j], landed.at[i, me], swap_send.at[i, to], swap_recv.at[i, me],
            {"sector": to},
        ), pltpu.make_async_copy(outs.at[a, i, j], landed.at[i, me], swap_send.at[i, to])

    def store(a, i, j):
        to = 2 * lax.rem(z + 1 + a, line) + j
        slot = lax.rem(a, 2)
        return pltpu.make_async_copy(
            outs.at[line + slot, i, j], carried.at[i, to], out_sem.at[slot, i, j]
        )

    def absorb(a):
        p = a // line

        @pl.when(lax.rem(a, line) == 0)
        def _():
            for other in range(line):
                for t in range(states):
                    hop(2, 2 * other + 1 - y, p, t, twin).wait_recv()
            load_tile(a)

        have_tile(a)

        @pl.when(lax.rem(a, line) < line - 1)
        def _():
            load_tile(a + 1)

        @pl.when(a >= line + 2)
        def _():
            for i in range(CHUNKS):
                for j in range(2):
                    store(a - 2, i, j).wait()

        slot = jnp.where(p == 0, a, line + lax.rem(a, 2))
        carried_into(mix_ref, left, tiles.at[lax.rem(a, 2)], outs.at[slot])
        for i in range(CHUNKS):
            for j in range(2):

                @pl.when(p == 0)
                def _():
                    to, far, near = swap(a, i, j)

                    @pl.when(to == me)
                    def _():
                        near.start()

                    @pl.when(to != me)
                    def _():
                        far.start()

                @pl.when(p > 0)
                def _():
                    store(a, i, j).start()

    def tick(i, carry):
        @pl.when(i < ticks)
        def _():
            relayed(i, start, True)

        @pl.when(i == OWN_LATER)
        def _():
            for p in range(1, HALVES):
                for t in range(states):
                    outward(me, p, t, True, (0, 1, 2), start)

        for q in range(SHIFTS):

            @pl.when(i == PRODUCT[q])
            def _():
                product(q)
                dispatch(q, False)

            @pl.when(i == CROSS[q])
            def _():
                dispatch(q, True)

        @pl.when(i == ABSORB)
        def _():
            load_left.wait()

        early = jnp.logical_and(i >= ABSORB, i < ABSORB + line)

        @pl.when(jnp.logical_or(early, i >= ticks))
        def _():
            absorb(jnp.where(i >= ticks, i - ticks + line, i - ABSORB))

        return carry

    lax.fori_loop(0, ticks + line, tick, 0)

    for copy in keep_site:
        copy.wait()
    for q in range(SHIFTS):
        shift(q).wait_send()
    for p in range(HALVES):
        for t in range(states):
            outward(me, p, t, True, (0, 1, 2), settle)
    each(ticks, lambda i: relayed(i, settle, False))

    def finish(i):
        q, d = i // (parts - 1), lax.rem(i, parts - 1)

        @pl.when(held(q, d))
        def _():
            put_off(q, d).wait()

        @pl.when(jnp.logical_not(held(q, d)))
        def _():
            block(q, d).wait_send()

        @pl.when(jnp.logical_not(waits(parts, target_of(d), me, q)))
        def _():
            block_in(q, d).wait_recv()

    each(SHIFTS * (parts - 1), finish)
    for q in range(SHIFTS):
        own_block(q).wait()

    def swapped(a):
        for i in range(CHUNKS):
            for j in range(2):
                to, far, near = swap(a, i, j)

                @pl.when(to == me)
                def _():
                    near.wait()

                @pl.when(to != me)
                def _():
                    far.wait_send()
                    remote(
                        outs.at[a, i, j], landed.at[i, to], swap_send.at[i, to],
                        swap_recv.at[i, to], {"sector": to},
                    ).wait_recv()

    each(line, swapped)
    for a in range(2 * line - 2, 2 * line):
        for i in range(CHUNKS):
            for j in range(2):
                store(a, i, j).wait()


def head(env_left, site, mpo, env_right, bond_tensor, parts):
    width, rows, bond = env_left.shape
    _, states, depth, _ = site.shape
    columns = bond // parts
    eye = jnp.eye(GROUP, dtype=jnp.float32)
    side = width * states * GROUP
    mix = jnp.einsum("vwst,ij->wsitvj", mpo, eye, precision=lax.Precision.HIGHEST).reshape(side, side)
    part_rows = rows // SHIFTS
    carried = (width // CHUNKS, states, rows, columns // HALVES)
    bf16 = jnp.bfloat16
    anywhere = pl.BlockSpec(memory_space=pl.ANY)
    dma = pltpu.SemaphoreType.DMA
    return pl.pallas_call(
        head_kernel,
        in_specs=[pl.BlockSpec(memory_space=pltpu.VMEM)] + [anywhere] * 4,
        out_specs=[anywhere] * 5,
        out_shape=[
            jax.ShapeDtypeStruct((HALVES, parts, states, depth, bond // HALVES), bf16),
            jax.ShapeDtypeStruct((SHIFTS, parts, width, part_rows, columns), bf16),
            jax.ShapeDtypeStruct((CHUNKS, parts) + carried, bf16),
            jax.ShapeDtypeStruct((CHUNKS, parts) + carried, bf16),
            jax.ShapeDtypeStruct((SHIFTS, parts // 2, width, part_rows, columns), bf16),
        ],
        scratch_shapes=[
            pltpu.VMEM((width, rows, bond), bf16),
            pltpu.VMEM((bond, bond), bf16),
            pltpu.VMEM((SHIFTS, parts, width, part_rows, columns), bf16),
            pltpu.VMEM((width, rows, bond), bf16),
            pltpu.VMEM((2, parts, states, depth, columns), bf16),
            pltpu.VMEM((parts // 2 + 2, CHUNKS, 2) + carried, bf16),
            dma((SHIFTS,)),
            dma((SHIFTS,)),
            dma((3, HALVES, parts, states)),
            dma((HALVES, parts, states)),
            dma((SHIFTS, parts)),
            dma((SHIFTS, parts)),
            dma((CHUNKS, parts)),
            dma((CHUNKS, parts)),
            dma((2, CHUNKS, 2)),
            dma((2, parts)),
            dma((2 + HALVES,)),
        ],
        compiler_params=pltpu.CompilerParams(
            vmem_limit_bytes=VMEM_LIMIT, collective_id=0, has_side_effects=True
        ),
        cost_estimate=pl.CostEstimate(
            flops=3 * width * rows * bond * bond * states,
            bytes_accessed=128 * 1024 * 1024,
            transcendentals=0,
        ),
    )(mix, env_right, site, bond_tensor, env_left)


def rest_kernel(
    gathered, moved_before, landed_first, carried, late,
    env_out, image_out, landed, moved,
    x, turned, env, bond_in, keep, pair_out, pair_in, line_out, line_in, done,
    swap_send, swap_recv, late_send, late_recv, pair_send, pair_recv, line_send, line_recv,
    load_sem, env_sem, out_sem,
):
    _, parts, states, depth, _ = gathered.shape
    _, _, count, _, _, sub = landed.shape
    width, columns, bond = env_out.shape
    part_rows = moved.shape[3]
    line = parts // 2
    group = bond_in.shape[0]
    splits = parts // group
    steps = SHIFTS * splits
    me = lax.axis_index("sector")
    z, y = me // 2, lax.rem(me, 2)
    twin = 2 * z + 1 - y

    pl.semaphore_wait(greet(parts), parts - 1)

    def swap(b, d, receiving=False):
        j = lax.rem(me + 1 + d, parts)
        owner = j if receiving else me
        return remote(
            carried.at[b, j], landed.at[b, owner], swap_send.at[b, d], swap_recv.at[b, owner],
            {"sector": j},
        )

    def dispatch(b):
        def step(d, carry):
            swap(b, d).start()
            return carry

        lax.fori_loop(0, parts - 1, step, 0)

    def fill(b, d, first):
        n = lax.rem(me + 1 + d, parts)
        origin = landed_first if first else landed
        return pltpu.make_async_copy(origin.at[b, n], x.at[n], load_sem.at[d])

    def fill_own(b, first):
        origin = landed_first if first else carried
        return pltpu.make_async_copy(origin.at[b, me], x.at[me], load_sem.at[parts - 1])

    def turn(n, carry):
        for s in range(states):
            at = pl.multiple_of((n * states + s) * depth, depth)
            for v in range(count):
                turned[v * sub : (v + 1) * sub, pl.ds(at, depth)] = x[n, v, s].T
        return carry

    def env_body(*refs):
        out_ref = refs[-1]
        tile = out_ref.shape[-1]
        totals = []
        for site_ref in refs[:-1]:
            site = site_ref[0].reshape(parts * states * depth, site_ref.shape[-1])
            totals.append(
                jnp.dot(turned[...], site, preferred_element_type=jnp.float32)
                .astype(jnp.bfloat16)
                .reshape(count, sub, site_ref.shape[-1])
            )
        for k in range(tile // sub):
            piece = slice(k // HALVES * sub, (k // HALVES + 1) * sub)
            out_ref[:, :, k * sub : (k + 1) * sub] = totals[k % HALVES][:, :, piece]

    def spot(ref, i):
        p, b = i // CHUNKS, lax.rem(i, CHUNKS)
        return ref.at[
            pl.ds(b * count, count), pl.ds(pl.multiple_of(p * sub, sub), sub)
        ]

    def reload(i):
        return pltpu.make_async_copy(spot(env_out, i), spot(env, i), env_sem.at[i])

    def late_block(q, k, receiving=False):
        to = lax.rem(z + 1 + k, line)
        other = 2 * to + y
        owner = other if receiving else me
        return remote(
            late.at[q, to], moved.at[q, owner], late_send.at[q, k],
            late_recv.at[q, owner // 2], {"sector": other},
        )

    def late_blocks(q, act, receiving=False):
        for k in range(line - 1):
            other = 2 * lax.rem(z + 1 + k, line) + y

            @pl.when(waits(parts, other, me, q) if receiving else waits(parts, me, other, q))
            def _():
                act(late_block(q, k, receiving))

    tile = 2 * LANES
    for b in range(min(AHEAD, CHUNKS)):
        dispatch(b)

    def advance(i, carry):
        b = lax.rem(i, CHUNKS)
        for first in (True, False):

            @pl.when(i < CHUNKS if first else i >= CHUNKS)
            def _():
                fill_own(b, first).start()

                def collect(d, carry):
                    if not first:
                        swap(b, d, True).wait_recv()
                    fill(b, d, first).start()
                    return carry

                lax.fori_loop(0, parts - 1, collect, 0)

        @pl.when(jnp.logical_and(i >= CHUNKS, b + AHEAD < CHUNKS))
        def _():
            dispatch(b + AHEAD)

        @pl.when(i == LATE_AFTER)
        def _():
            for q in range(SHIFTS):
                late_blocks(q, lambda copy: copy.start())

        def filled(d, carry):
            fill(b, d, True).wait()
            return carry

        lax.fori_loop(0, parts - 1, filled, 0)
        fill_own(b, True).wait()
        lax.fori_loop(0, parts, turn, 0)
        pltpu.emit_pipeline(
            env_body,
            grid=(bond // (tile * HALVES),),
            in_specs=[
                pl.BlockSpec(
                    (1, parts, states, depth, tile),
                    functools.partial(lambda p, j: (p, 0, 0, 0, j), p),
                )
                for p in range(HALVES)
            ],
            out_specs=[pl.BlockSpec((count, sub, tile * HALVES), lambda j: (0, 0, j))],
        )(*[gathered] * HALVES, spot(env_out, i))
        reload(i).start()
        return carry

    lax.fori_loop(0, HALVES * CHUNKS, advance, 0)
    for i in range(HALVES * CHUNKS):
        reload(i).wait()

    def pair_copy(u):
        return remote(
            pair_out.at[u], pair_in.at[u], pair_send.at[u], pair_recv.at[u], {"sector": twin}
        )

    def line_copy(u, t, way):
        slot = t + 1 if way == 0 else t
        return remote(
            line_out.at[u, t], line_in.at[u, slot], line_send.at[u, t], line_recv.at[u, slot],
            {"sector": me + 2 if way == 0 else me - 2},
        )

    def dot(a, b):
        return jnp.dot(a, b, preferred_element_type=jnp.float32)

    def take(u, i):
        q, n = u // splits, lax.rem(u, splits) * group + i
        return pltpu.make_async_copy(
            moved.at[q, n], bond_in.at[i], load_sem.at[i]
        )

    def image(u):
        for i in range(group):
            take(u, i).start()
        for i in range(group):
            take(u, i).wait()
        left = jnp.concatenate(
            [bond_in[:, w].reshape(group * part_rows, columns) for w in range(width)], axis=1
        )

        def right(j):
            at = pl.multiple_of(j * columns, columns)
            return env[:, :, pl.ds(at, columns)].reshape(width * columns, columns)

        for t in range(line):
            pair_out[u, t] = dot(left, right(2 * t + 1 - y)).astype(jnp.bfloat16)
        for t in range(line):
            keep[u, t] = dot(left, right(2 * t + y))
        pair_copy(u).start()

    def paired(u):
        pair_copy(u).wait_recv()
        keep[u] = keep[u] + pair_in[u].astype(jnp.float32)

    def relay(s, way):
        first = z if way == 0 else line - 1 - z
        u = s - 1 - first
        live = jnp.logical_and(u >= 0, u < steps)
        for t in range(line):
            sends = jnp.logical_and(live, t > z if way == 0 else t < z)

            @pl.when(jnp.logical_and(sends, first == 0))
            def _():
                line_out[u, t] = keep[u, t].astype(jnp.bfloat16)

            @pl.when(jnp.logical_and(sends, first > 0))
            def _():
                slot = t + 1 if way == 0 else t
                line_copy(u, t, way).wait_recv()
                line_out[u, t] = (
                    keep[u, t] + line_in[u, slot].astype(jnp.float32)
                ).astype(jnp.bfloat16)

    def send_on(s, way):
        first = z if way == 0 else line - 1 - z
        u = s - 1 - first
        live = jnp.logical_and(u >= 0, u < steps)
        for t in range(line):

            @pl.when(jnp.logical_and(live, t > z if way == 0 else t < z))
            def _():
                line_copy(u, t, way).start()

    def result(u):
        return pltpu.make_async_copy(done.at[u], image_out.at[u], out_sem.at[u])

    def total(u):
        @pl.when(z > 0)
        def _():
            line_copy(u, z, 0).wait_recv()
            keep[u, z] = keep[u, z] + line_in[u, z + 1].astype(jnp.float32)

        @pl.when(z < line - 1)
        def _():
            line_copy(u, z, 1).wait_recv()
            keep[u, z] = keep[u, z] + line_in[u, z].astype(jnp.float32)

        done[u] = keep[u, z].astype(jnp.bfloat16)

    def pass_on(s, carry):
        @pl.when(s < steps)
        def _():
            @pl.when(lax.rem(s, splits) == 0)
            def _():
                late_blocks(s // splits, lambda copy: copy.wait_recv(), True)

            image(s)

        @pl.when(jnp.logical_and(s >= 1, s <= steps))
        def _():
            paired(s - 1)

        relay(s, 0)
        relay(s, 1)

        @pl.when(s >= line)
        def _():
            total(s - line)

        send_on(s, 0)
        send_on(s, 1)

        @pl.when(s >= line)
        def _():
            result(s - line).start()

        return carry

    lax.fori_loop(0, steps + line, pass_on, 0)

    def sent(b, carry):
        def step(d, carry):
            swap(b, d).wait_send()
            return carry

        return lax.fori_loop(0, parts - 1, step, carry)

    lax.fori_loop(0, CHUNKS, sent, 0)

    for q in range(SHIFTS):
        late_blocks(q, lambda copy: copy.wait_send())

    def ended(u, carry):
        pair_copy(u).wait_send()
        result(u).wait()
        for t in range(line):
            @pl.when(t > z)
            def _():
                line_copy(u, t, 0).wait_send()

            @pl.when(t < z)
            def _():
                line_copy(u, t, 1).wait_send()

        return carry

    lax.fori_loop(0, steps, ended, 0)


def rest_of(gathered, moved, landed, carried, late):
    _, parts, states, depth, _ = gathered.shape
    _, _, count, _, _, sub = carried.shape
    width, columns = count * CHUNKS, sub * HALVES
    bond = parts * columns
    part_rows = moved.shape[3]
    line = parts // 2
    group = max(parts // SPLIT, 1)
    steps = SHIFTS * (parts // group)
    block = (group * part_rows, columns)
    anywhere = pl.BlockSpec(memory_space=pl.ANY)
    dma = pltpu.SemaphoreType.DMA
    bf16 = jnp.bfloat16
    return pl.pallas_call(
        rest_kernel,
        in_specs=[anywhere] * 5,
        out_specs=[anywhere] * 4,
        input_output_aliases={1: 3},
        out_shape=[
            jax.ShapeDtypeStruct((width, columns, bond), bf16),
            jax.ShapeDtypeStruct((steps,) + block, bf16),
            jax.ShapeDtypeStruct(carried.shape, bf16),
            jax.ShapeDtypeStruct(moved.shape, bf16),
        ],
        scratch_shapes=[
            pltpu.VMEM(carried.shape[1:], bf16),
            pltpu.VMEM((count * sub, parts * states * depth), bf16),
            pltpu.VMEM((width, columns, bond), bf16),
            pltpu.VMEM((group, width, part_rows, columns), bf16),
            pltpu.VMEM((steps, line) + block, jnp.float32),
            pltpu.VMEM((steps, line) + block, bf16),
            pltpu.VMEM((steps, line) + block, bf16),
            pltpu.VMEM((steps, line) + block, bf16),
            pltpu.VMEM((steps, line + 1) + block, bf16),
            pltpu.VMEM((steps,) + block, bf16),
            dma((CHUNKS, parts)),
            dma((CHUNKS, parts)),
            dma((SHIFTS, line)),
            dma((SHIFTS, line)),
            dma((steps,)),
            dma((steps,)),
            dma((steps, line)),
            dma((steps, line + 1)),
            dma((parts,)),
            dma((HALVES * CHUNKS,)),
            dma((steps,)),
        ],
        compiler_params=pltpu.CompilerParams(
            vmem_limit_bytes=VMEM_LIMIT, collective_id=1, has_side_effects=True
        ),
        cost_estimate=pl.CostEstimate(
            flops=3 * width * columns * parts * states * depth * bond,
            bytes_accessed=128 * 1024 * 1024,
            transcendentals=0,
        ),
    )(gathered, moved, landed, carried, late)


def local(env_left, site_tensor, mpo_tensor, env_right, bond_tensor):
    parts = lax.axis_size("sector")
    _, rows, bond = env_left.shape[1:]
    columns = bond // parts
    site = site_tensor[0].reshape(rows, -1, parts, HALVES, columns // HALVES)
    site = site.transpose(3, 1, 0, 2, 4).reshape(HALVES, -1, rows, bond // HALVES)
    gathered, moved, landed, carried, late = head(
        env_left[0], site, mpo_tensor[0], env_right[0], bond_tensor[0], parts,
    )
    env_new, image, *_ = rest_of(gathered, moved, landed, carried, late)
    image_rows = (
        image.reshape(SHIFTS, parts, rows // SHIFTS, columns)
        .transpose(3, 1, 0, 2)
        .reshape(columns, bond)
    )
    return (env_new[None], image_rows[None])


def plain_local(env_left, site_tensor, mpo_tensor, env_right, bond_tensor):
    width = env_left.shape[1]
    states = site_tensor.shape[2]
    gathered = lax.all_gather(site_tensor, "sector", axis=1, tiled=True)[0]
    half_done = jnp.einsum(
        "wak,ksc->wasc", env_left[0], gathered, preferred_element_type=jnp.float32
    )
    carried = jnp.einsum(
        "vwst,vatc->wsac", mpo_tensor[0], half_done, precision=lax.Precision.HIGHEST
    ).astype(jnp.bfloat16)
    carried = carried.reshape((width * states,) + carried.shape[2:])
    right_next = shifted(env_right, "region", -1)[0]
    bond_right = jnp.einsum(
        "wbc,kc->wbk", right_next, bond_tensor[0], preferred_element_type=jnp.float32
    ).astype(jnp.bfloat16)
    carried_moved = lax.all_to_all(carried, "sector", split_axis=2, concat_axis=1, tiled=True)
    bond_moved = lax.all_to_all(bond_right, "sector", split_axis=2, concat_axis=1, tiled=True)
    carried_moved = carried_moved.reshape((width, states) + carried_moved.shape[1:])
    env_new = jnp.einsum(
        "wsac,asb->wcb", carried_moved, gathered, preferred_element_type=jnp.float32
    ).astype(jnp.bfloat16)
    image_rows = lax.psum_scatter(
        jnp.einsum("wka,wbk->ab", env_new, bond_moved, preferred_element_type=jnp.float32),
        "sector",
        scatter_dimension=0,
        tiled=True,
    )
    return (env_new[None], image_rows.astype(jnp.bfloat16)[None])


def solution(mesh):
    def body(env_left, site_tensor, mpo_tensor, env_right, bond_tensor):
        width, rows, bond = env_left.shape[1:]
        columns = bond // mesh.shape["sector"]
        tiled = rows % LANES == 0 and columns % (HALVES * LANES) == 0 and width % CHUNKS == 0 and rows % (16 * SHIFTS) == 0
        tiled = tiled and mesh.shape["sector"] % 2 == 0 and mesh.shape["region"] > 2
        step = local if tiled else plain_local
        return step(env_left, site_tensor, mpo_tensor, env_right, bond_tensor)

    return jax.shard_map(
        body,
        mesh=mesh,
        in_specs=(
            P("region", None, "sector", None),
            P("region", "sector", None, None),
            P("region", None, None, None, None),
            P("region", None, "sector", None),
            P("region", None, None),
        ),
        out_specs=(P("region", None, "sector", None), P("region", "sector", None)),
        check_vma=False,
    )
```

```python
import functools

import jax
import jax.numpy as jnp
from jax import lax
from jax.experimental import pallas as pl
from jax.experimental.pallas import tpu as pltpu
from jax.sharding import PartitionSpec as P

GROUP = 16
LANES = 128
HALVES = 2
CHUNKS = 4
EDGE_FROM = 2
AHEAD = 4
LATE_AFTER = 7
SHIFTS = 4
CROSS = (4, 6, 11, 12)
PRODUCT = (0, 1, 2, 3)
OWN_LATER = 2
ABSORB = 7
SPLIT = 4
LAG = 2
HOP = 2
VMEM_LIMIT = 60 * 1024 * 1024


def shifted(block, axis, distance):
    devices = range(lax.axis_size(axis))
    route = [((i - distance) % len(devices), i) for i in devices]
    return lax.ppermute(block, axis, route)


MESH = pl.DeviceIdType.MESH


def carried_into(mix_ref, env_ref, site_ref, out_ref):
    width, rows, bond = env_ref.shape
    _, states, _, columns = site_ref.shape
    sub = columns // 2
    tile = min(rows, LANES)
    mix = mix_ref[...]
    mix_high = mix.astype(jnp.bfloat16)
    mix_low = (mix - mix_high.astype(jnp.float32)).astype(jnp.bfloat16)
    dot = functools.partial(jnp.dot, preferred_element_type=jnp.float32)
    step = width // CHUNKS

    def rows_of(i, carry):
        top = pl.multiple_of(i * tile, tile)
        env = env_ref[:, pl.ds(top, tile)].reshape(width * tile, bond)
        half_done = [
            dot(env, site_ref[:, t].reshape(bond, columns)).reshape(width, tile, columns)
            for t in range(states)
        ]
        for g in range(tile // GROUP):
            span = slice(g * GROUP, (g + 1) * GROUP)
            x = jnp.concatenate(
                [h[:, span].reshape(width * GROUP, columns) for h in half_done], axis=0
            )
            high = x.astype(jnp.bfloat16)
            low = (x - high.astype(jnp.float32)).astype(jnp.bfloat16)
            y = dot(mix_high, high) + dot(mix_high, low) + dot(mix_low, high)
            y = y.astype(jnp.bfloat16).reshape(width, states, GROUP, columns)
            for i in range(CHUNKS):
                for j in range(2):
                    out_ref[i, j, :, :, pl.ds(top + g * GROUP, GROUP), :] = y[
                        i * step : (i + 1) * step, :, :, j * sub : (j + 1) * sub
                    ]
        return carry

    lax.fori_loop(0, rows // tile, rows_of, 0)


def inner(parts, device):
    z = device // 2
    return jnp.logical_and(z > 0, z < parts // 2 - 1)


def waits(parts, source, target, q):
    same = lax.rem(source + target, 2) == 0
    return jnp.logical_and(same, jnp.logical_or(inner(parts, source), q >= EDGE_FROM))


def greet(parts):
    me = lax.axis_index("sector")
    barrier = pltpu.get_barrier_semaphore()
    for d in range(1, parts):
        pl.semaphore_signal(
            barrier, inc=1, device_id={"sector": lax.rem(me + d, parts)}, device_id_type=MESH
        )
    return barrier


def remote(src, dst, send, recv, target):
    return pltpu.make_async_remote_copy(
        src_ref=src, dst_ref=dst, send_sem=send, recv_sem=recv,
        device_id=target, device_id_type=MESH,
    )


def head_kernel(
    mix_ref, right_hbm, site_hbm, bond_hbm, left_hbm,
    gathered, moved, landed, carried, late,
    right, bond_ref, blocks, left, tiles, outs,
    shift_send, shift_recv, site_send, site_recv,
    block_send, block_recv, swap_send, swap_recv, out_sem, tile_sem, local_sem,
):

    _, parts, states, _, _ = gathered.shape
    width, rows, bond = right_hbm.shape
    columns = bond // parts
    line = parts // 2
    me = lax.axis_index("sector")
    z, y = me // 2, lax.rem(me, 2)
    regions = lax.axis_size("region")
    region = lax.axis_index("region")
    before = lax.rem(region + regions - 1, regions)
    after = lax.rem(region + 1, regions)
    part_rows = rows // SHIFTS
    twin = 2 * z + 1 - y

    barrier = greet(parts)
    for other in (before, after):
        pl.semaphore_signal(barrier, inc=1, device_id={"region": other}, device_id_type=MESH)
    pl.semaphore_wait(barrier, parts + 1)

    def shift(q):
        span = pl.ds(q * part_rows, part_rows)
        return remote(
            right_hbm.at[:, span], right.at[:, span], shift_send.at[q], shift_recv.at[q],
            {"region": before},
        )

    def hop(way, source, p, t, target, first=False):
        there = gathered.at[p, source, t]
        return remote(
            site_hbm.at[p, t] if first else there, there,
            site_send.at[way, p, source, t], site_recv.at[p, source, t], {"sector": target},
        )

    def outward(source, p, t, first, ways, act):
        for way in ways:
            there = {0: me + 2, 1: me - 2, 2: twin}[way]
            if way == 2:
                act(hop(way, source, p, t, there, first))
            else:
                inside = z + 1 < line if way == 0 else z >= 1

                @pl.when(inside)
                def _():
                    act(hop(way, source, p, t, there, first))

    def target_of(d):
        return lax.rem(me + 1 + d, parts)

    def block(q, d):
        return remote(
            blocks.at[q, d], moved.at[q, me], block_send.at[q, d], block_recv.at[q, me],
            {"sector": target_of(d)},
        )

    def block_in(q, d):
        source = target_of(d)
        return remote(
            blocks.at[q, d], moved.at[q, source], block_send.at[q, d], block_recv.at[q, source],
            {"sector": source},
        )

    def held(q, d):
        return waits(parts, me, target_of(d), q)

    def put_off(q, d):
        return pltpu.make_async_copy(
            blocks.at[q, d], late.at[q, target_of(d) // 2], block_send.at[q, d]
        )

    def own_block(q):
        return pltpu.make_async_copy(
            blocks.at[q, parts - 1], moved.at[q, me], block_send.at[q, parts - 1]
        )

    def start(copy):
        copy.start()

    def settle(copy):
        copy.wait_send()

    for q in range(SHIFTS):
        shift(q).start()
    for t in range(states):
        outward(me, 0, t, True, (0, 1, 2), start)
    load_bond = pltpu.make_async_copy(bond_hbm, bond_ref, local_sem.at[0])
    load_bond.start()
    load_left = pltpu.make_async_copy(left_hbm, left, local_sem.at[1])
    load_left.start()
    keep_site = [
        pltpu.make_async_copy(site_hbm.at[p], gathered.at[p, me], local_sem.at[2 + p])
        for p in range(HALVES)
    ]
    for copy in keep_site:
        copy.start()
    load_bond.wait()

    def product(q):
        shift(q).wait_recv()
        span = pl.ds(q * part_rows, part_rows)
        x = right[:, span].reshape(width * part_rows, bond)

        def step(d, carry):
            j = target_of(d)
            out = lax.dot_general(
                x,
                bond_ref[pl.ds(pl.multiple_of(j * columns, columns), columns), :],
                (((1,), (1,)), ((), ())),
                preferred_element_type=jnp.float32,
            )
            blocks[q, d] = out.astype(jnp.bfloat16).reshape(width, part_rows, columns)
            return carry

        lax.fori_loop(0, parts, step, 0)

    def dispatch(q, cross):
        def step(d, carry):
            same = lax.rem(target_of(d), 2) == y

            @pl.when(jnp.logical_not(same) if cross else jnp.logical_and(same, jnp.logical_not(held(q, d))))
            def _():
                block(q, d).start()

            if not cross:

                @pl.when(held(q, d))
                def _():
                    put_off(q, d).start()

            return carry

        lax.fori_loop(0, parts - 1, step, 0)
        if not cross:
            own_block(q).start()

    hops = (line - 1) * states
    ticks = HALVES * hops

    def relayed(i, act, receive):
        p, distance, t = i // hops, lax.rem(i, hops) // states + 1, lax.rem(i, states)
        for way, source in ((0, me - 2 * distance), (1, me + 2 * distance)):
            there = z >= distance if way == 0 else z + distance < line

            @pl.when(there)
            def _():
                if receive:
                    hop(way, source, p, t, twin).wait_recv()
                outward(source, p, t, False, (way, 2), act)

    def tile_copies(a):
        p, slot = a // line, lax.rem(a, 2)
        m = lax.rem(z + 1 + a, line)
        span = pl.ds(pl.multiple_of(m * columns, columns), columns)
        mine = pltpu.make_async_copy(
            site_hbm.at[p, :, :, span], tiles.at[slot, me], tile_sem.at[slot, parts - 1]
        )
        return mine, lambda d: pltpu.make_async_copy(
            gathered.at[p, target_of(d), :, :, span], tiles.at[slot, target_of(d)],
            tile_sem.at[slot, d],
        )

    def each(count, act):
        def step(d, carry):
            act(d)
            return carry

        lax.fori_loop(0, count, step, 0)

    def load_tile(a):
        mine, other = tile_copies(a)
        mine.start()
        each(parts - 1, lambda d: other(d).start())

    def have_tile(a):
        mine, other = tile_copies(a)
        mine.wait()
        each(parts - 1, lambda d: other(d).wait())

    def swap(a, i, j):
        to = 2 * lax.rem(z + 1 + a, line) + j
        return to, remote(
            outs.at[a, i, j], landed.at[i, me], swap_send.at[i, to], swap_recv.at[i, me],
            {"sector": to},
        ), pltpu.make_async_copy(outs.at[a, i, j], landed.at[i, me], swap_send.at[i, to])

    def store(a, i, j):
        to = 2 * lax.rem(z + 1 + a, line) + j
        slot = lax.rem(a, 2)
        return pltpu.make_async_copy(
            outs.at[line + slot, i, j], carried.at[i, to], out_sem.at[slot, i, j]
        )

    def absorb(a):
        p = a // line

        @pl.when(lax.rem(a, line) == 0)
        def _():
            for other in range(line):
                for t in range(states):
                    hop(2, 2 * other + 1 - y, p, t, twin).wait_recv()
            load_tile(a)

        have_tile(a)

        @pl.when(lax.rem(a, line) < line - 1)
        def _():
            load_tile(a + 1)

        @pl.when(a >= line + 2)
        def _():
            for i in range(CHUNKS):
                for j in range(2):
                    store(a - 2, i, j).wait()

        slot = jnp.where(p == 0, a, line + lax.rem(a, 2))
        carried_into(mix_ref, left, tiles.at[lax.rem(a, 2)], outs.at[slot])
        for i in range(CHUNKS):
            for j in range(2):

                @pl.when(p == 0)
                def _():
                    to, far, near = swap(a, i, j)

                    @pl.when(to == me)
                    def _():
                        near.start()

                    @pl.when(to != me)
                    def _():
                        far.start()

                @pl.when(p > 0)
                def _():
                    store(a, i, j).start()

    def tick(i, carry):
        @pl.when(i < ticks)
        def _():
            relayed(i, start, True)

        @pl.when(i == OWN_LATER)
        def _():
            for p in range(1, HALVES):
                for t in range(states):
                    outward(me, p, t, True, (0, 1, 2), start)

        for q in range(SHIFTS):

            @pl.when(i == PRODUCT[q])
            def _():
                product(q)
                dispatch(q, False)

            @pl.when(i == CROSS[q])
            def _():
                dispatch(q, True)

        @pl.when(i == ABSORB)
        def _():
            load_left.wait()

        early = jnp.logical_and(i >= ABSORB, i < ABSORB + line)

        @pl.when(jnp.logical_or(early, i >= ticks))
        def _():
            absorb(jnp.where(i >= ticks, i - ticks + line, i - ABSORB))

        return carry

    lax.fori_loop(0, ticks + line, tick, 0)

    for copy in keep_site:
        copy.wait()
    for q in range(SHIFTS):
        shift(q).wait_send()
    for p in range(HALVES):
        for t in range(states):
            outward(me, p, t, True, (0, 1, 2), settle)
    each(ticks, lambda i: relayed(i, settle, False))

    def finish(i):
        q, d = i // (parts - 1), lax.rem(i, parts - 1)

        @pl.when(held(q, d))
        def _():
            put_off(q, d).wait()

        @pl.when(jnp.logical_not(held(q, d)))
        def _():
            block(q, d).wait_send()

        @pl.when(jnp.logical_not(waits(parts, target_of(d), me, q)))
        def _():
            block_in(q, d).wait_recv()

    each(SHIFTS * (parts - 1), finish)
    for q in range(SHIFTS):
        own_block(q).wait()

    def swapped(a):
        for i in range(CHUNKS):
            for j in range(2):
                to, far, near = swap(a, i, j)

                @pl.when(to == me)
                def _():
                    near.wait()

                @pl.when(to != me)
                def _():
                    far.wait_send()
                    remote(
                        outs.at[a, i, j], landed.at[i, to], swap_send.at[i, to],
                        swap_recv.at[i, to], {"sector": to},
                    ).wait_recv()

    each(line, swapped)
    for a in range(2 * line - 2, 2 * line):
        for i in range(CHUNKS):
            for j in range(2):
                store(a, i, j).wait()


def head(env_left, site, mpo, env_right, bond_tensor, parts):
    width, rows, bond = env_left.shape
    _, states, depth, _ = site.shape
    columns = bond // parts
    eye = jnp.eye(GROUP, dtype=jnp.float32)
    side = width * states * GROUP
    mix = jnp.einsum("vwst,ij->wsitvj", mpo, eye, precision=lax.Precision.HIGHEST).reshape(side, side)
    part_rows = rows // SHIFTS
    carried = (width // CHUNKS, states, rows, columns // HALVES)
    bf16 = jnp.bfloat16
    anywhere = pl.BlockSpec(memory_space=pl.ANY)
    dma = pltpu.SemaphoreType.DMA
    return pl.pallas_call(
        head_kernel,
        in_specs=[pl.BlockSpec(memory_space=pltpu.VMEM)] + [anywhere] * 4,
        out_specs=[anywhere] * 5,
        out_shape=[
            jax.ShapeDtypeStruct((HALVES, parts, states, depth, bond // HALVES), bf16),
            jax.ShapeDtypeStruct((SHIFTS, parts, width, part_rows, columns), bf16),
            jax.ShapeDtypeStruct((CHUNKS, parts) + carried, bf16),
            jax.ShapeDtypeStruct((CHUNKS, parts) + carried, bf16),
            jax.ShapeDtypeStruct((SHIFTS, parts // 2, width, part_rows, columns), bf16),
        ],
        scratch_shapes=[
            pltpu.VMEM((width, rows, bond), bf16),
            pltpu.VMEM((bond, bond), bf16),
            pltpu.VMEM((SHIFTS, parts, width, part_rows, columns), bf16),
            pltpu.VMEM((width, rows, bond), bf16),
            pltpu.VMEM((2, parts, states, depth, columns), bf16),
            pltpu.VMEM((parts // 2 + 2, CHUNKS, 2) + carried, bf16),
            dma((SHIFTS,)),
            dma((SHIFTS,)),
            dma((3, HALVES, parts, states)),
            dma((HALVES, parts, states)),
            dma((SHIFTS, parts)),
            dma((SHIFTS, parts)),
            dma((CHUNKS, parts)),
            dma((CHUNKS, parts)),
            dma((2, CHUNKS, 2)),
            dma((2, parts)),
            dma((2 + HALVES,)),
        ],
        compiler_params=pltpu.CompilerParams(
            vmem_limit_bytes=VMEM_LIMIT, collective_id=0, has_side_effects=True
        ),
        cost_estimate=pl.CostEstimate(
            flops=3 * width * rows * bond * bond * states,
            bytes_accessed=128 * 1024 * 1024,
            transcendentals=0,
        ),
    )(mix, env_right, site, bond_tensor, env_left)


def rest_kernel(
    gathered, moved_before, landed_first, carried, late,
    env_out, image_out, landed, moved,
    x, turned, env, bond_in, keep, pair_out, pair_in, line_out, line_in, done,
    swap_send, swap_recv, late_send, late_recv, pair_send, pair_recv, line_send, line_recv,
    load_sem, env_sem, out_sem,
):
    _, parts, states, depth, _ = gathered.shape
    _, _, count, _, _, sub = landed.shape
    width, columns, bond = env_out.shape
    part_rows = moved.shape[3]
    line = parts // 2
    group = bond_in.shape[1]
    splits = parts // group
    steps = SHIFTS * splits
    me = lax.axis_index("sector")
    z, y = me // 2, lax.rem(me, 2)
    twin = 2 * z + 1 - y

    pl.semaphore_wait(greet(parts), parts - 1)

    def swap(b, d, receiving=False):
        j = lax.rem(me + 1 + d, parts)
        owner = j if receiving else me
        return remote(
            carried.at[b, j], landed.at[b, owner], swap_send.at[b, d], swap_recv.at[b, owner],
            {"sector": j},
        )

    def dispatch(b):
        def step(d, carry):
            swap(b, d).start()
            return carry

        lax.fori_loop(0, parts - 1, step, 0)

    def fill(b, d, first):
        n = lax.rem(me + 1 + d, parts)
        origin = landed_first if first else landed
        return pltpu.make_async_copy(origin.at[b, n], x.at[n], load_sem.at[d])

    def fill_own(b, first):
        origin = landed_first if first else carried
        return pltpu.make_async_copy(origin.at[b, me], x.at[me], load_sem.at[parts - 1])

    def turn(n, carry):
        for s in range(states):
            at = pl.multiple_of((n * states + s) * depth, depth)
            for v in range(count):
                turned[v * sub : (v + 1) * sub, pl.ds(at, depth)] = x[n, v, s].T
        return carry

    def env_body(*refs):
        out_ref = refs[-1]
        tile = out_ref.shape[-1]
        totals = []
        for site_ref in refs[:-1]:
            site = site_ref[0].reshape(parts * states * depth, site_ref.shape[-1])
            totals.append(
                jnp.dot(turned[...], site, preferred_element_type=jnp.float32)
                .astype(jnp.bfloat16)
                .reshape(count, sub, site_ref.shape[-1])
            )
        for k in range(tile // sub):
            piece = slice(k // HALVES * sub, (k // HALVES + 1) * sub)
            out_ref[:, :, k * sub : (k + 1) * sub] = totals[k % HALVES][:, :, piece]

    def spot(ref, i):
        p, b = i // CHUNKS, lax.rem(i, CHUNKS)
        return ref.at[
            pl.ds(b * count, count), pl.ds(pl.multiple_of(p * sub, sub), sub)
        ]

    def reload(i):
        return pltpu.make_async_copy(spot(env_out, i), spot(env, i), env_sem.at[i])

    def late_block(q, k, receiving=False):
        to = lax.rem(z + 1 + k, line)
        other = 2 * to + y
        owner = other if receiving else me
        return remote(
            late.at[q, to], moved.at[q, owner], late_send.at[q, k],
            late_recv.at[q, owner // 2], {"sector": other},
        )

    def late_blocks(q, act, receiving=False):
        for k in range(line - 1):
            other = 2 * lax.rem(z + 1 + k, line) + y

            @pl.when(waits(parts, other, me, q) if receiving else waits(parts, me, other, q))
            def _():
                act(late_block(q, k, receiving))

    tile = 2 * LANES
    for b in range(min(AHEAD, CHUNKS)):
        dispatch(b)

    def advance(i, carry):
        b = lax.rem(i, CHUNKS)
        for first in (True, False):

            @pl.when(i < CHUNKS if first else i >= CHUNKS)
            def _():
                fill_own(b, first).start()

                def collect(d, carry):
                    if not first:
                        swap(b, d, True).wait_recv()
                    fill(b, d, first).start()
                    return carry

                lax.fori_loop(0, parts - 1, collect, 0)

        @pl.when(jnp.logical_and(i >= CHUNKS, b + AHEAD < CHUNKS))
        def _():
            dispatch(b + AHEAD)

        @pl.when(i == LATE_AFTER)
        def _():
            for q in range(SHIFTS):
                late_blocks(q, lambda copy: copy.start())

        def filled(d, carry):
            fill(b, d, True).wait()
            return carry

        lax.fori_loop(0, parts - 1, filled, 0)
        fill_own(b, True).wait()
        lax.fori_loop(0, parts, turn, 0)
        pltpu.emit_pipeline(
            env_body,
            grid=(bond // (tile * HALVES),),
            in_specs=[
                pl.BlockSpec(
                    (1, parts, states, depth, tile),
                    functools.partial(lambda p, j: (p, 0, 0, 0, j), p),
                )
                for p in range(HALVES)
            ],
            out_specs=[pl.BlockSpec((count, sub, tile * HALVES), lambda j: (0, 0, j))],
        )(*[gathered] * HALVES, spot(env_out, i))
        reload(i).start()
        return carry

    lax.fori_loop(0, HALVES * CHUNKS, advance, 0)
    for i in range(HALVES * CHUNKS):
        reload(i).wait()

    def pair_copy(u):
        return remote(
            pair_out.at[u], pair_in.at[u], pair_send.at[u], pair_recv.at[u], {"sector": twin}
        )

    def line_copy(u, t, way):
        slot = t + 1 if way == 0 else t
        return remote(
            line_out.at[u, t], line_in.at[u, slot], line_send.at[u, t], line_recv.at[u, slot],
            {"sector": me + 2 if way == 0 else me - 2},
        )

    def dot(a, b):
        return jnp.dot(a, b, preferred_element_type=jnp.float32)

    def take(u, i):
        q, n, slot = u // splits, lax.rem(u, splits) * group + i, lax.rem(u, 2)
        return pltpu.make_async_copy(
            moved.at[q, n], bond_in.at[slot, i], load_sem.at[slot * group + i]
        )

    def fetch(u):
        @pl.when(lax.rem(u, splits) == 0)
        def _():
            late_blocks(u // splits, lambda copy: copy.wait_recv(), True)

        for i in range(group):
            take(u, i).start()

    def image(u):
        for i in range(group):
            take(u, i).wait()

        @pl.when(u + 1 < steps)
        def _():
            fetch(u + 1)

        left = jnp.concatenate(
            [
                bond_in[lax.rem(u, 2), :, w].reshape(group * part_rows, columns)
                for w in range(width)
            ],
            axis=1,
        )

        def right(j):
            at = pl.multiple_of(j * columns, columns)
            return env[:, :, pl.ds(at, columns)].reshape(width * columns, columns)

        for t in range(line):
            pair_out[u, t] = dot(left, right(2 * t + 1 - y)).astype(jnp.bfloat16)
        for t in range(line):
            keep[u, t] = dot(left, right(2 * t + y))
        pair_copy(u).start()

    def paired(u):
        pair_copy(u).wait_recv()
        keep[u] = keep[u] + pair_in[u].astype(jnp.float32)

    def relay(s, way):
        first = z if way == 0 else line - 1 - z
        u = s - LAG - HOP * first
        live = jnp.logical_and(u >= 0, u < steps)
        for t in range(line):
            sends = jnp.logical_and(live, t > z if way == 0 else t < z)

            @pl.when(jnp.logical_and(sends, first == 0))
            def _():
                line_out[u, t] = keep[u, t].astype(jnp.bfloat16)

            @pl.when(jnp.logical_and(sends, first > 0))
            def _():
                slot = t + 1 if way == 0 else t
                line_copy(u, t, way).wait_recv()
                line_out[u, t] = (
                    keep[u, t] + line_in[u, slot].astype(jnp.float32)
                ).astype(jnp.bfloat16)

    def send_on(s, way):
        first = z if way == 0 else line - 1 - z
        u = s - LAG - HOP * first
        live = jnp.logical_and(u >= 0, u < steps)
        for t in range(line):

            @pl.when(jnp.logical_and(live, t > z if way == 0 else t < z))
            def _():
                line_copy(u, t, way).start()

    def result(u):
        return pltpu.make_async_copy(done.at[u], image_out.at[u], out_sem.at[u])

    def total(u):
        @pl.when(z > 0)
        def _():
            line_copy(u, z, 0).wait_recv()
            keep[u, z] = keep[u, z] + line_in[u, z + 1].astype(jnp.float32)

        @pl.when(z < line - 1)
        def _():
            line_copy(u, z, 1).wait_recv()
            keep[u, z] = keep[u, z] + line_in[u, z].astype(jnp.float32)

        done[u] = keep[u, z].astype(jnp.bfloat16)

    last = LAG + HOP * (line - 2) + 1

    def pass_on(s, carry):
        @pl.when(s < steps)
        def _():
            image(s)

        @pl.when(jnp.logical_and(s >= LAG, s < steps + LAG))
        def _():
            paired(s - LAG)

        relay(s, 0)
        relay(s, 1)

        @pl.when(s >= last)
        def _():
            total(s - last)

        send_on(s, 0)
        send_on(s, 1)

        @pl.when(s >= last)
        def _():
            result(s - last).start()

        return carry

    fetch(0)
    lax.fori_loop(0, steps + last, pass_on, 0)

    def sent(b, carry):
        def step(d, carry):
            swap(b, d).wait_send()
            return carry

        return lax.fori_loop(0, parts - 1, step, carry)

    lax.fori_loop(0, CHUNKS, sent, 0)

    for q in range(SHIFTS):
        late_blocks(q, lambda copy: copy.wait_send())

    def ended(u, carry):
        pair_copy(u).wait_send()
        result(u).wait()
        for t in range(line):
            @pl.when(t > z)
            def _():
                line_copy(u, t, 0).wait_send()

            @pl.when(t < z)
            def _():
                line_copy(u, t, 1).wait_send()

        return carry

    lax.fori_loop(0, steps, ended, 0)


def rest_of(gathered, moved, landed, carried, late):
    _, parts, states, depth, _ = gathered.shape
    _, _, count, _, _, sub = carried.shape
    width, columns = count * CHUNKS, sub * HALVES
    bond = parts * columns
    part_rows = moved.shape[3]
    line = parts // 2
    group = max(parts // SPLIT, 1)
    steps = SHIFTS * (parts // group)
    block = (group * part_rows, columns)
    anywhere = pl.BlockSpec(memory_space=pl.ANY)
    dma = pltpu.SemaphoreType.DMA
    bf16 = jnp.bfloat16
    return pl.pallas_call(
        rest_kernel,
        in_specs=[anywhere] * 5,
        out_specs=[anywhere] * 4,
        input_output_aliases={1: 3},
        out_shape=[
            jax.ShapeDtypeStruct((width, columns, bond), bf16),
            jax.ShapeDtypeStruct((steps,) + block, bf16),
            jax.ShapeDtypeStruct(carried.shape, bf16),
            jax.ShapeDtypeStruct(moved.shape, bf16),
        ],
        scratch_shapes=[
            pltpu.VMEM(carried.shape[1:], bf16),
            pltpu.VMEM((count * sub, parts * states * depth), bf16),
            pltpu.VMEM((width, columns, bond), bf16),
            pltpu.VMEM((2, group, width, part_rows, columns), bf16),
            pltpu.VMEM((steps, line) + block, jnp.float32),
            pltpu.VMEM((steps, line) + block, bf16),
            pltpu.VMEM((steps, line) + block, bf16),
            pltpu.VMEM((steps, line) + block, bf16),
            pltpu.VMEM((steps, line + 1) + block, bf16),
            pltpu.VMEM((steps,) + block, bf16),
            dma((CHUNKS, parts)),
            dma((CHUNKS, parts)),
            dma((SHIFTS, line)),
            dma((SHIFTS, line)),
            dma((steps,)),
            dma((steps,)),
            dma((steps, line)),
            dma((steps, line + 1)),
            dma((parts,)),
            dma((HALVES * CHUNKS,)),
            dma((steps,)),
        ],
        compiler_params=pltpu.CompilerParams(
            vmem_limit_bytes=VMEM_LIMIT, collective_id=1, has_side_effects=True
        ),
        cost_estimate=pl.CostEstimate(
            flops=3 * width * columns * parts * states * depth * bond,
            bytes_accessed=128 * 1024 * 1024,
            transcendentals=0,
        ),
    )(gathered, moved, landed, carried, late)


def local(env_left, site_tensor, mpo_tensor, env_right, bond_tensor):
    parts = lax.axis_size("sector")
    _, rows, bond = env_left.shape[1:]
    columns = bond // parts
    site = site_tensor[0].reshape(rows, -1, parts, HALVES, columns // HALVES)
    site = site.transpose(3, 1, 0, 2, 4).reshape(HALVES, -1, rows, bond // HALVES)
    gathered, moved, landed, carried, late = head(
        env_left[0], site, mpo_tensor[0], env_right[0], bond_tensor[0], parts,
    )
    env_new, image, *_ = rest_of(gathered, moved, landed, carried, late)
    image_rows = (
        image.reshape(SHIFTS, parts, rows // SHIFTS, columns)
        .transpose(3, 1, 0, 2)
        .reshape(columns, bond)
    )
    return (env_new[None], image_rows[None])


def plain_local(env_left, site_tensor, mpo_tensor, env_right, bond_tensor):
    width = env_left.shape[1]
    states = site_tensor.shape[2]
    gathered = lax.all_gather(site_tensor, "sector", axis=1, tiled=True)[0]
    half_done = jnp.einsum(
        "wak,ksc->wasc", env_left[0], gathered, preferred_element_type=jnp.float32
    )
    carried = jnp.einsum(
        "vwst,vatc->wsac", mpo_tensor[0], half_done, precision=lax.Precision.HIGHEST
    ).astype(jnp.bfloat16)
    carried = carried.reshape((width * states,) + carried.shape[2:])
    right_next = shifted(env_right, "region", -1)[0]
    bond_right = jnp.einsum(
        "wbc,kc->wbk", right_next, bond_tensor[0], preferred_element_type=jnp.float32
    ).astype(jnp.bfloat16)
    carried_moved = lax.all_to_all(carried, "sector", split_axis=2, concat_axis=1, tiled=True)
    bond_moved = lax.all_to_all(bond_right, "sector", split_axis=2, concat_axis=1, tiled=True)
    carried_moved = carried_moved.reshape((width, states) + carried_moved.shape[1:])
    env_new = jnp.einsum(
        "wsac,asb->wcb", carried_moved, gathered, preferred_element_type=jnp.float32
    ).astype(jnp.bfloat16)
    image_rows = lax.psum_scatter(
        jnp.einsum("wka,wbk->ab", env_new, bond_moved, preferred_element_type=jnp.float32),
        "sector",
        scatter_dimension=0,
        tiled=True,
    )
    return (env_new[None], image_rows.astype(jnp.bfloat16)[None])


def solution(mesh):
    def body(env_left, site_tensor, mpo_tensor, env_right, bond_tensor):
        width, rows, bond = env_left.shape[1:]
        columns = bond // mesh.shape["sector"]
        tiled = rows % LANES == 0 and columns % (HALVES * LANES) == 0 and width % CHUNKS == 0 and rows % (16 * SHIFTS) == 0
        tiled = tiled and mesh.shape["sector"] % 2 == 0 and mesh.shape["region"] > 2
        step = local if tiled else plain_local
        return step(env_left, site_tensor, mpo_tensor, env_right, bond_tensor)

    return jax.shard_map(
        body,
        mesh=mesh,
        in_specs=(
            P("region", None, "sector", None),
            P("region", "sector", None, None),
            P("region", None, None, None, None),
            P("region", None, "sector", None),
            P("region", None, None),
        ),
        out_specs=(P("region", None, "sector", None), P("region", "sector", None)),
        check_vma=False,
    )
```

```python
import functools

import jax
import jax.numpy as jnp
from jax import lax
from jax.experimental import pallas as pl
from jax.experimental.pallas import tpu as pltpu
from jax.sharding import PartitionSpec as P

GROUP = 16
LANES = 128
HALVES = 2
CHUNKS = 4
EDGE_FROM = 2
AHEAD = 4
LATE_AFTER = 7
SHIFTS = 4
CROSS = (4, 6, 11, 12)
PRODUCT = (0, 1, 2, 3)
OWN_LATER = 2
ABSORB = 7
SPLIT = 4
LAG = 2
HOP = 2
VMEM_LIMIT = 60 * 1024 * 1024


def shifted(block, axis, distance):
    devices = range(lax.axis_size(axis))
    route = [((i - distance) % len(devices), i) for i in devices]
    return lax.ppermute(block, axis, route)


MESH = pl.DeviceIdType.MESH


def carried_into(mix_ref, env_ref, site_ref, out_ref):
    width, rows, bond = env_ref.shape
    _, states, _, columns = site_ref.shape
    sub = columns // 2
    tile = min(rows, LANES)
    mix = mix_ref[...]
    mix_high = mix.astype(jnp.bfloat16)
    mix_low = (mix - mix_high.astype(jnp.float32)).astype(jnp.bfloat16)
    dot = functools.partial(jnp.dot, preferred_element_type=jnp.float32)
    step = width // CHUNKS

    def rows_of(i, carry):
        top = pl.multiple_of(i * tile, tile)
        env = env_ref[:, pl.ds(top, tile)].reshape(width * tile, bond)
        half_done = [
            dot(env, site_ref[:, t].reshape(bond, columns)).reshape(width, tile, columns)
            for t in range(states)
        ]
        for g in range(tile // GROUP):
            span = slice(g * GROUP, (g + 1) * GROUP)
            x = jnp.concatenate(
                [h[:, span].reshape(width * GROUP, columns) for h in half_done], axis=0
            )
            high = x.astype(jnp.bfloat16)
            low = (x - high.astype(jnp.float32)).astype(jnp.bfloat16)
            y = dot(mix_high, high) + dot(mix_high, low) + dot(mix_low, high)
            y = y.astype(jnp.bfloat16).reshape(width, states, GROUP, columns)
            for i in range(CHUNKS):
                for j in range(2):
                    out_ref[i, j, :, :, pl.ds(top + g * GROUP, GROUP), :] = y[
                        i * step : (i + 1) * step, :, :, j * sub : (j + 1) * sub
                    ]
        return carry

    lax.fori_loop(0, rows // tile, rows_of, 0)


def inner(parts, device):
    z = device // 2
    return jnp.logical_and(z > 0, z < parts // 2 - 1)


def waits(parts, source, target, q):
    same = lax.rem(source + target, 2) == 0
    return jnp.logical_and(same, jnp.logical_or(inner(parts, source), q >= EDGE_FROM))


def greet(parts):
    me = lax.axis_index("sector")
    barrier = pltpu.get_barrier_semaphore()
    for d in range(1, parts):
        pl.semaphore_signal(
            barrier, inc=1, device_id={"sector": lax.rem(me + d, parts)}, device_id_type=MESH
        )
    return barrier


def remote(src, dst, send, recv, target):
    return pltpu.make_async_remote_copy(
        src_ref=src, dst_ref=dst, send_sem=send, recv_sem=recv,
        device_id=target, device_id_type=MESH,
    )


def head_kernel(
    mix_ref, right_hbm, site_hbm, bond_hbm, left_hbm,
    gathered, moved, landed, carried, late,
    right, bond_ref, blocks, left, tiles, outs, own,
    shift_send, shift_recv, site_send, site_recv,
    block_send, block_recv, swap_send, swap_recv, out_sem, tile_sem, local_sem, own_sem,
):

    _, parts, states, _, _ = gathered.shape
    width, rows, bond = right_hbm.shape
    columns = bond // parts
    line = parts // 2
    me = lax.axis_index("sector")
    z, y = me // 2, lax.rem(me, 2)
    regions = lax.axis_size("region")
    region = lax.axis_index("region")
    before = lax.rem(region + regions - 1, regions)
    after = lax.rem(region + 1, regions)
    part_rows = rows // SHIFTS
    twin = 2 * z + 1 - y

    barrier = greet(parts)
    for other in (before, after):
        pl.semaphore_signal(barrier, inc=1, device_id={"region": other}, device_id_type=MESH)

    def shift(q):
        span = pl.ds(q * part_rows, part_rows)
        return remote(
            right_hbm.at[:, span], right.at[:, span], shift_send.at[q], shift_recv.at[q],
            {"region": before},
        )

    def hop(way, source, p, t, target, first=False):
        there = gathered.at[p, source, t]
        return remote(
            own.at[p, t] if first else there, there,
            site_send.at[way, p, source, t], site_recv.at[p, source, t], {"sector": target},
        )

    def outward(source, p, t, first, ways, act):
        for way in ways:
            there = {0: me + 2, 1: me - 2, 2: twin}[way]
            if way == 2:
                act(hop(way, source, p, t, there, first))
            else:
                inside = z + 1 < line if way == 0 else z >= 1

                @pl.when(inside)
                def _():
                    act(hop(way, source, p, t, there, first))

    def target_of(d):
        return lax.rem(me + 1 + d, parts)

    def block(q, d):
        return remote(
            blocks.at[q, d], moved.at[q, me], block_send.at[q, d], block_recv.at[q, me],
            {"sector": target_of(d)},
        )

    def block_in(q, d):
        source = target_of(d)
        return remote(
            blocks.at[q, d], moved.at[q, source], block_send.at[q, d], block_recv.at[q, source],
            {"sector": source},
        )

    def held(q, d):
        return waits(parts, me, target_of(d), q)

    def put_off(q, d):
        return pltpu.make_async_copy(
            blocks.at[q, d], late.at[q, target_of(d) // 2], block_send.at[q, d]
        )

    def own_block(q):
        return pltpu.make_async_copy(
            blocks.at[q, parts - 1], moved.at[q, me], block_send.at[q, parts - 1]
        )

    def start(copy):
        copy.start()

    def settle(copy):
        copy.wait_send()

    sub = columns // HALVES

    def sort_site(p, j):
        return pltpu.make_async_copy(
            site_hbm.at[:, :, pl.ds(j * columns + p * sub, sub)],
            own.at[p, :, :, pl.ds(j * sub, sub)],
            own_sem.at[p, j],
        )

    for p in range(HALVES):
        for j in range(parts):
            sort_site(p, j).start()
    pl.semaphore_wait(barrier, parts + 1)
    for q in range(SHIFTS):
        shift(q).start()
    for j in range(parts):
        sort_site(0, j).wait()
    for t in range(states):
        outward(me, 0, t, True, (0, 1, 2), start)
    for p in range(1, HALVES):
        for j in range(parts):
            sort_site(p, j).wait()
    load_bond = pltpu.make_async_copy(bond_hbm, bond_ref, local_sem.at[0])
    load_bond.start()
    load_left = pltpu.make_async_copy(left_hbm, left, local_sem.at[1])
    load_left.start()
    keep_site = [
        pltpu.make_async_copy(own.at[p], gathered.at[p, me], local_sem.at[2 + p])
        for p in range(HALVES)
    ]
    for copy in keep_site:
        copy.start()
    load_bond.wait()

    def product(q):
        shift(q).wait_recv()
        span = pl.ds(q * part_rows, part_rows)
        x = right[:, span].reshape(width * part_rows, bond)

        def step(d, carry):
            j = target_of(d)
            out = lax.dot_general(
                x,
                bond_ref[pl.ds(pl.multiple_of(j * columns, columns), columns), :],
                (((1,), (1,)), ((), ())),
                preferred_element_type=jnp.float32,
            )
            blocks[q, d] = out.astype(jnp.bfloat16).reshape(width, part_rows, columns)
            return carry

        lax.fori_loop(0, parts, step, 0)

    def dispatch(q, cross):
        def step(d, carry):
            same = lax.rem(target_of(d), 2) == y

            @pl.when(jnp.logical_not(same) if cross else jnp.logical_and(same, jnp.logical_not(held(q, d))))
            def _():
                block(q, d).start()

            if not cross:

                @pl.when(held(q, d))
                def _():
                    put_off(q, d).start()

            return carry

        lax.fori_loop(0, parts - 1, step, 0)
        if not cross:
            own_block(q).start()

    hops = (line - 1) * states
    ticks = HALVES * hops

    def relayed(i, act, receive):
        p, distance, t = i // hops, lax.rem(i, hops) // states + 1, lax.rem(i, states)
        for way, source in ((0, me - 2 * distance), (1, me + 2 * distance)):
            there = z >= distance if way == 0 else z + distance < line

            @pl.when(there)
            def _():
                if receive:
                    hop(way, source, p, t, twin).wait_recv()
                outward(source, p, t, False, (way, 2), act)

    def tile_copies(a):
        p, slot = a // line, lax.rem(a, 2)
        m = lax.rem(z + 1 + a, line)
        span = pl.ds(pl.multiple_of(m * columns, columns), columns)
        mine = pltpu.make_async_copy(
            own.at[p, :, :, span], tiles.at[slot, me], tile_sem.at[slot, parts - 1]
        )
        return mine, lambda d: pltpu.make_async_copy(
            gathered.at[p, target_of(d), :, :, span], tiles.at[slot, target_of(d)],
            tile_sem.at[slot, d],
        )

    def each(count, act):
        def step(d, carry):
            act(d)
            return carry

        lax.fori_loop(0, count, step, 0)

    def load_tile(a):
        mine, other = tile_copies(a)
        mine.start()
        each(parts - 1, lambda d: other(d).start())

    def have_tile(a):
        mine, other = tile_copies(a)
        mine.wait()
        each(parts - 1, lambda d: other(d).wait())

    def swap(a, i, j):
        to = 2 * lax.rem(z + 1 + a, line) + j
        return to, remote(
            outs.at[a, i, j], landed.at[i, me], swap_send.at[i, to], swap_recv.at[i, me],
            {"sector": to},
        ), pltpu.make_async_copy(outs.at[a, i, j], landed.at[i, me], swap_send.at[i, to])

    def store(a, i, j):
        to = 2 * lax.rem(z + 1 + a, line) + j
        slot = lax.rem(a, 2)
        return pltpu.make_async_copy(
            outs.at[line + slot, i, j], carried.at[i, to], out_sem.at[slot, i, j]
        )

    def absorb(a):
        p = a // line

        @pl.when(lax.rem(a, line) == 0)
        def _():
            for other in range(line):
                for t in range(states):
                    hop(2, 2 * other + 1 - y, p, t, twin).wait_recv()
            load_tile(a)

        have_tile(a)

        @pl.when(lax.rem(a, line) < line - 1)
        def _():
            load_tile(a + 1)

        @pl.when(a >= line + 2)
        def _():
            for i in range(CHUNKS):
                for j in range(2):
                    store(a - 2, i, j).wait()

        slot = jnp.where(p == 0, a, line + lax.rem(a, 2))
        carried_into(mix_ref, left, tiles.at[lax.rem(a, 2)], outs.at[slot])
        for i in range(CHUNKS):
            for j in range(2):

                @pl.when(p == 0)
                def _():
                    to, far, near = swap(a, i, j)

                    @pl.when(to == me)
                    def _():
                        near.start()

                    @pl.when(to != me)
                    def _():
                        far.start()

                @pl.when(p > 0)
                def _():
                    store(a, i, j).start()

    def tick(i, carry):
        @pl.when(i < ticks)
        def _():
            relayed(i, start, True)

        @pl.when(i == OWN_LATER)
        def _():
            for p in range(1, HALVES):
                for t in range(states):
                    outward(me, p, t, True, (0, 1, 2), start)

        for q in range(SHIFTS):

            @pl.when(i == PRODUCT[q])
            def _():
                product(q)
                dispatch(q, False)

            @pl.when(i == CROSS[q])
            def _():
                dispatch(q, True)

        @pl.when(i == ABSORB)
        def _():
            load_left.wait()

        early = jnp.logical_and(i >= ABSORB, i < ABSORB + line)

        @pl.when(jnp.logical_or(early, i >= ticks))
        def _():
            absorb(jnp.where(i >= ticks, i - ticks + line, i - ABSORB))

        return carry

    lax.fori_loop(0, ticks + line, tick, 0)

    for copy in keep_site:
        copy.wait()
    for q in range(SHIFTS):
        shift(q).wait_send()
    for p in range(HALVES):
        for t in range(states):
            outward(me, p, t, True, (0, 1, 2), settle)
    each(ticks, lambda i: relayed(i, settle, False))

    def finish(i):
        q, d = i // (parts - 1), lax.rem(i, parts - 1)

        @pl.when(held(q, d))
        def _():
            put_off(q, d).wait()

        @pl.when(jnp.logical_not(held(q, d)))
        def _():
            block(q, d).wait_send()

        @pl.when(jnp.logical_not(waits(parts, target_of(d), me, q)))
        def _():
            block_in(q, d).wait_recv()

    each(SHIFTS * (parts - 1), finish)
    for q in range(SHIFTS):
        own_block(q).wait()

    def swapped(a):
        for i in range(CHUNKS):
            for j in range(2):
                to, far, near = swap(a, i, j)

                @pl.when(to == me)
                def _():
                    near.wait()

                @pl.when(to != me)
                def _():
                    far.wait_send()
                    remote(
                        outs.at[a, i, j], landed.at[i, to], swap_send.at[i, to],
                        swap_recv.at[i, to], {"sector": to},
                    ).wait_recv()

    each(line, swapped)
    for a in range(2 * line - 2, 2 * line):
        for i in range(CHUNKS):
            for j in range(2):
                store(a, i, j).wait()


def head(env_left, site, mpo, env_right, bond_tensor, parts):
    width, rows, bond = env_left.shape
    states, depth, _ = site.shape
    columns = bond // parts
    eye = jnp.eye(GROUP, dtype=jnp.float32)
    side = width * states * GROUP
    mix = jnp.einsum("vwst,ij->wsitvj", mpo, eye, precision=lax.Precision.HIGHEST).reshape(side, side)
    part_rows = rows // SHIFTS
    carried = (width // CHUNKS, states, rows, columns // HALVES)
    bf16 = jnp.bfloat16
    anywhere = pl.BlockSpec(memory_space=pl.ANY)
    dma = pltpu.SemaphoreType.DMA
    return pl.pallas_call(
        head_kernel,
        in_specs=[pl.BlockSpec(memory_space=pltpu.VMEM)] + [anywhere] * 4,
        out_specs=[anywhere] * 5,
        out_shape=[
            jax.ShapeDtypeStruct((HALVES, parts, states, depth, bond // HALVES), bf16),
            jax.ShapeDtypeStruct((SHIFTS, parts, width, part_rows, columns), bf16),
            jax.ShapeDtypeStruct((CHUNKS, parts) + carried, bf16),
            jax.ShapeDtypeStruct((CHUNKS, parts) + carried, bf16),
            jax.ShapeDtypeStruct((SHIFTS, parts // 2, width, part_rows, columns), bf16),
        ],
        scratch_shapes=[
            pltpu.VMEM((width, rows, bond), bf16),
            pltpu.VMEM((bond, bond), bf16),
            pltpu.VMEM((SHIFTS, parts, width, part_rows, columns), bf16),
            pltpu.VMEM((width, rows, bond), bf16),
            pltpu.VMEM((2, parts, states, depth, columns), bf16),
            pltpu.VMEM((parts // 2 + 2, CHUNKS, 2) + carried, bf16),
            pltpu.VMEM((HALVES, states, depth, bond // HALVES), bf16),
            dma((SHIFTS,)),
            dma((SHIFTS,)),
            dma((3, HALVES, parts, states)),
            dma((HALVES, parts, states)),
            dma((SHIFTS, parts)),
            dma((SHIFTS, parts)),
            dma((CHUNKS, parts)),
            dma((CHUNKS, parts)),
            dma((2, CHUNKS, 2)),
            dma((2, parts)),
            dma((2 + HALVES,)),
            dma((HALVES, parts)),
        ],
        compiler_params=pltpu.CompilerParams(
            vmem_limit_bytes=VMEM_LIMIT, collective_id=0, has_side_effects=True
        ),
        cost_estimate=pl.CostEstimate(
            flops=3 * width * rows * bond * bond * states,
            bytes_accessed=128 * 1024 * 1024,
            transcendentals=0,
        ),
    )(mix, env_right, site, bond_tensor, env_left)


def rest_kernel(
    gathered, moved_before, landed_first, carried, late,
    env_out, image_out, landed, moved,
    x, turned, env, bond_in, keep, pair_out, pair_in, line_out, line_in, done,
    swap_send, swap_recv, late_send, late_recv, pair_send, pair_recv, line_send, line_recv,
    load_sem, env_sem, out_sem,
):
    _, parts, states, depth, _ = gathered.shape
    _, _, count, _, _, sub = landed.shape
    width, columns, bond = env_out.shape
    part_rows = moved.shape[3]
    line = parts // 2
    group = bond_in.shape[1]
    splits = parts // group
    steps = SHIFTS * splits
    me = lax.axis_index("sector")
    z, y = me // 2, lax.rem(me, 2)
    twin = 2 * z + 1 - y

    pl.semaphore_wait(greet(parts), parts - 1)

    def swap(b, d, receiving=False):
        j = lax.rem(me + 1 + d, parts)
        owner = j if receiving else me
        return remote(
            carried.at[b, j], landed.at[b, owner], swap_send.at[b, d], swap_recv.at[b, owner],
            {"sector": j},
        )

    def dispatch(b):
        def step(d, carry):
            swap(b, d).start()
            return carry

        lax.fori_loop(0, parts - 1, step, 0)

    def fill(b, d, first):
        n = lax.rem(me + 1 + d, parts)
        origin = landed_first if first else landed
        return pltpu.make_async_copy(origin.at[b, n], x.at[n], load_sem.at[d])

    def fill_own(b, first):
        origin = landed_first if first else carried
        return pltpu.make_async_copy(origin.at[b, me], x.at[me], load_sem.at[parts - 1])

    def turn(n, carry):
        for s in range(states):
            at = pl.multiple_of((n * states + s) * depth, depth)
            for v in range(count):
                turned[v * sub : (v + 1) * sub, pl.ds(at, depth)] = x[n, v, s].T
        return carry

    def env_body(*refs):
        out_ref = refs[-1]
        tile = out_ref.shape[-1]
        totals = []
        for site_ref in refs[:-1]:
            site = site_ref[0].reshape(parts * states * depth, site_ref.shape[-1])
            totals.append(
                jnp.dot(turned[...], site, preferred_element_type=jnp.float32)
                .astype(jnp.bfloat16)
                .reshape(count, sub, site_ref.shape[-1])
            )
        for k in range(tile // sub):
            piece = slice(k // HALVES * sub, (k // HALVES + 1) * sub)
            out_ref[:, :, k * sub : (k + 1) * sub] = totals[k % HALVES][:, :, piece]

    def spot(ref, i):
        p, b = i // CHUNKS, lax.rem(i, CHUNKS)
        return ref.at[
            pl.ds(b * count, count), pl.ds(pl.multiple_of(p * sub, sub), sub)
        ]

    def reload(i):
        return pltpu.make_async_copy(spot(env_out, i), spot(env, i), env_sem.at[i])

    def late_block(q, k, receiving=False):
        to = lax.rem(z + 1 + k, line)
        other = 2 * to + y
        owner = other if receiving else me
        return remote(
            late.at[q, to], moved.at[q, owner], late_send.at[q, k],
            late_recv.at[q, owner // 2], {"sector": other},
        )

    def late_blocks(q, act, receiving=False):
        for k in range(line - 1):
            other = 2 * lax.rem(z + 1 + k, line) + y

            @pl.when(waits(parts, other, me, q) if receiving else waits(parts, me, other, q))
            def _():
                act(late_block(q, k, receiving))

    tile = 2 * LANES
    for b in range(min(AHEAD, CHUNKS)):
        dispatch(b)

    def advance(i, carry):
        b = lax.rem(i, CHUNKS)
        for first in (True, False):

            @pl.when(i < CHUNKS if first else i >= CHUNKS)
            def _():
                fill_own(b, first).start()

                def collect(d, carry):
                    if not first:
                        swap(b, d, True).wait_recv()
                    fill(b, d, first).start()
                    return carry

                lax.fori_loop(0, parts - 1, collect, 0)

        @pl.when(jnp.logical_and(i >= CHUNKS, b + AHEAD < CHUNKS))
        def _():
            dispatch(b + AHEAD)

        @pl.when(i == LATE_AFTER)
        def _():
            for q in range(SHIFTS):
                late_blocks(q, lambda copy: copy.start())

        def filled(d, carry):
            fill(b, d, True).wait()
            return carry

        lax.fori_loop(0, parts - 1, filled, 0)
        fill_own(b, True).wait()
        lax.fori_loop(0, parts, turn, 0)
        pltpu.emit_pipeline(
            env_body,
            grid=(bond // (tile * HALVES),),
            in_specs=[
                pl.BlockSpec(
                    (1, parts, states, depth, tile),
                    functools.partial(lambda p, j: (p, 0, 0, 0, j), p),
                )
                for p in range(HALVES)
            ],
            out_specs=[pl.BlockSpec((count, sub, tile * HALVES), lambda j: (0, 0, j))],
        )(*[gathered] * HALVES, spot(env_out, i))
        reload(i).start()
        return carry

    lax.fori_loop(0, HALVES * CHUNKS, advance, 0)
    for i in range(HALVES * CHUNKS):
        reload(i).wait()

    def pair_copy(u):
        return remote(
            pair_out.at[u], pair_in.at[u], pair_send.at[u], pair_recv.at[u], {"sector": twin}
        )

    def line_copy(u, t, way):
        slot = t + 1 if way == 0 else t
        return remote(
            line_out.at[u, t], line_in.at[u, slot], line_send.at[u, t], line_recv.at[u, slot],
            {"sector": me + 2 if way == 0 else me - 2},
        )

    def dot(a, b):
        return jnp.dot(a, b, preferred_element_type=jnp.float32)

    def take(u, i):
        q, n, slot = u // splits, lax.rem(u, splits) * group + i, lax.rem(u, 2)
        return pltpu.make_async_copy(
            moved.at[q, n], bond_in.at[slot, i], load_sem.at[slot * group + i]
        )

    def fetch(u):
        @pl.when(lax.rem(u, splits) == 0)
        def _():
            late_blocks(u // splits, lambda copy: copy.wait_recv(), True)

        for i in range(group):
            take(u, i).start()

    def image(u):
        for i in range(group):
            take(u, i).wait()

        @pl.when(u + 1 < steps)
        def _():
            fetch(u + 1)

        left = jnp.concatenate(
            [
                bond_in[lax.rem(u, 2), :, w].reshape(group * part_rows, columns)
                for w in range(width)
            ],
            axis=1,
        )

        def right(j):
            at = pl.multiple_of(j * columns, columns)
            return env[:, :, pl.ds(at, columns)].reshape(width * columns, columns)

        for t in range(line):
            pair_out[u, t] = dot(left, right(2 * t + 1 - y)).astype(jnp.bfloat16)
        for t in range(line):
            keep[u, t] = dot(left, right(2 * t + y))
        pair_copy(u).start()

    def paired(u):
        pair_copy(u).wait_recv()
        keep[u] = keep[u] + pair_in[u].astype(jnp.float32)

    def relay(s, way):
        first = z if way == 0 else line - 1 - z
        u = s - LAG - HOP * first
        live = jnp.logical_and(u >= 0, u < steps)
        for t in range(line):
            sends = jnp.logical_and(live, t > z if way == 0 else t < z)

            @pl.when(jnp.logical_and(sends, first == 0))
            def _():
                line_out[u, t] = keep[u, t].astype(jnp.bfloat16)

            @pl.when(jnp.logical_and(sends, first > 0))
            def _():
                slot = t + 1 if way == 0 else t
                line_copy(u, t, way).wait_recv()
                line_out[u, t] = (
                    keep[u, t] + line_in[u, slot].astype(jnp.float32)
                ).astype(jnp.bfloat16)

    def send_on(s, way):
        first = z if way == 0 else line - 1 - z
        u = s - LAG - HOP * first
        live = jnp.logical_and(u >= 0, u < steps)
        for t in range(line):

            @pl.when(jnp.logical_and(live, t > z if way == 0 else t < z))
            def _():
                line_copy(u, t, way).start()

    def result(u):
        return pltpu.make_async_copy(done.at[u], image_out.at[u], out_sem.at[u])

    def total(u):
        @pl.when(z > 0)
        def _():
            line_copy(u, z, 0).wait_recv()
            keep[u, z] = keep[u, z] + line_in[u, z + 1].astype(jnp.float32)

        @pl.when(z < line - 1)
        def _():
            line_copy(u, z, 1).wait_recv()
            keep[u, z] = keep[u, z] + line_in[u, z].astype(jnp.float32)

        done[u] = keep[u, z].astype(jnp.bfloat16)

    last = LAG + HOP * (line - 2) + 1

    def pass_on(s, carry):
        @pl.when(s < steps)
        def _():
            image(s)

        @pl.when(jnp.logical_and(s >= LAG, s < steps + LAG))
        def _():
            paired(s - LAG)

        relay(s, 0)
        relay(s, 1)

        @pl.when(s >= last)
        def _():
            total(s - last)

        send_on(s, 0)
        send_on(s, 1)

        @pl.when(s >= last)
        def _():
            result(s - last).start()

        return carry

    fetch(0)
    lax.fori_loop(0, steps + last, pass_on, 0)

    def sent(b, carry):
        def step(d, carry):
            swap(b, d).wait_send()
            return carry

        return lax.fori_loop(0, parts - 1, step, carry)

    lax.fori_loop(0, CHUNKS, sent, 0)

    for q in range(SHIFTS):
        late_blocks(q, lambda copy: copy.wait_send())

    def ended(u, carry):
        pair_copy(u).wait_send()
        result(u).wait()
        for t in range(line):
            @pl.when(t > z)
            def _():
                line_copy(u, t, 0).wait_send()

            @pl.when(t < z)
            def _():
                line_copy(u, t, 1).wait_send()

        return carry

    lax.fori_loop(0, steps, ended, 0)


def rest_of(gathered, moved, landed, carried, late):
    _, parts, states, depth, _ = gathered.shape
    _, _, count, _, _, sub = carried.shape
    width, columns = count * CHUNKS, sub * HALVES
    bond = parts * columns
    part_rows = moved.shape[3]
    line = parts // 2
    group = max(parts // SPLIT, 1)
    steps = SHIFTS * (parts // group)
    block = (group * part_rows, columns)
    anywhere = pl.BlockSpec(memory_space=pl.ANY)
    dma = pltpu.SemaphoreType.DMA
    bf16 = jnp.bfloat16
    return pl.pallas_call(
        rest_kernel,
        in_specs=[anywhere] * 5,
        out_specs=[anywhere] * 4,
        input_output_aliases={1: 3},
        out_shape=[
            jax.ShapeDtypeStruct((width, columns, bond), bf16),
            jax.ShapeDtypeStruct((steps,) + block, bf16),
            jax.ShapeDtypeStruct(carried.shape, bf16),
            jax.ShapeDtypeStruct(moved.shape, bf16),
        ],
        scratch_shapes=[
            pltpu.VMEM(carried.shape[1:], bf16),
            pltpu.VMEM((count * sub, parts * states * depth), bf16),
            pltpu.VMEM((width, columns, bond), bf16),
            pltpu.VMEM((2, group, width, part_rows, columns), bf16),
            pltpu.VMEM((steps, line) + block, jnp.float32),
            pltpu.VMEM((steps, line) + block, bf16),
            pltpu.VMEM((steps, line) + block, bf16),
            pltpu.VMEM((steps, line) + block, bf16),
            pltpu.VMEM((steps, line + 1) + block, bf16),
            pltpu.VMEM((steps,) + block, bf16),
            dma((CHUNKS, parts)),
            dma((CHUNKS, parts)),
            dma((SHIFTS, line)),
            dma((SHIFTS, line)),
            dma((steps,)),
            dma((steps,)),
            dma((steps, line)),
            dma((steps, line + 1)),
            dma((parts,)),
            dma((HALVES * CHUNKS,)),
            dma((steps,)),
        ],
        compiler_params=pltpu.CompilerParams(
            vmem_limit_bytes=VMEM_LIMIT, collective_id=1, has_side_effects=True
        ),
        cost_estimate=pl.CostEstimate(
            flops=3 * width * columns * parts * states * depth * bond,
            bytes_accessed=128 * 1024 * 1024,
            transcendentals=0,
        ),
    )(gathered, moved, landed, carried, late)


def local(env_left, site_tensor, mpo_tensor, env_right, bond_tensor):
    parts = lax.axis_size("sector")
    _, rows, bond = env_left.shape[1:]
    columns = bond // parts
    site = site_tensor[0].transpose(1, 0, 2)
    gathered, moved, landed, carried, late = head(
        env_left[0], site, mpo_tensor[0], env_right[0], bond_tensor[0], parts,
    )
    env_new, image, *_ = rest_of(gathered, moved, landed, carried, late)
    image_rows = (
        image.reshape(SHIFTS, parts, rows // SHIFTS, columns)
        .transpose(3, 1, 0, 2)
        .reshape(columns, bond)
    )
    return (env_new[None], image_rows[None])


def plain_local(env_left, site_tensor, mpo_tensor, env_right, bond_tensor):
    width = env_left.shape[1]
    states = site_tensor.shape[2]
    gathered = lax.all_gather(site_tensor, "sector", axis=1, tiled=True)[0]
    half_done = jnp.einsum(
        "wak,ksc->wasc", env_left[0], gathered, preferred_element_type=jnp.float32
    )
    carried = jnp.einsum(
        "vwst,vatc->wsac", mpo_tensor[0], half_done, precision=lax.Precision.HIGHEST
    ).astype(jnp.bfloat16)
    carried = carried.reshape((width * states,) + carried.shape[2:])
    right_next = shifted(env_right, "region", -1)[0]
    bond_right = jnp.einsum(
        "wbc,kc->wbk", right_next, bond_tensor[0], preferred_element_type=jnp.float32
    ).astype(jnp.bfloat16)
    carried_moved = lax.all_to_all(carried, "sector", split_axis=2, concat_axis=1, tiled=True)
    bond_moved = lax.all_to_all(bond_right, "sector", split_axis=2, concat_axis=1, tiled=True)
    carried_moved = carried_moved.reshape((width, states) + carried_moved.shape[1:])
    env_new = jnp.einsum(
        "wsac,asb->wcb", carried_moved, gathered, preferred_element_type=jnp.float32
    ).astype(jnp.bfloat16)
    image_rows = lax.psum_scatter(
        jnp.einsum("wka,wbk->ab", env_new, bond_moved, preferred_element_type=jnp.float32),
        "sector",
        scatter_dimension=0,
        tiled=True,
    )
    return (env_new[None], image_rows.astype(jnp.bfloat16)[None])


def solution(mesh):
    def body(env_left, site_tensor, mpo_tensor, env_right, bond_tensor):
        width, rows, bond = env_left.shape[1:]
        columns = bond // mesh.shape["sector"]
        tiled = rows % LANES == 0 and columns % (HALVES * LANES) == 0 and width % CHUNKS == 0 and rows % (16 * SHIFTS) == 0
        tiled = tiled and mesh.shape["sector"] % 2 == 0 and mesh.shape["region"] > 2
        step = local if tiled else plain_local
        return step(env_left, site_tensor, mpo_tensor, env_right, bond_tensor)

    return jax.shard_map(
        body,
        mesh=mesh,
        in_specs=(
            P("region", None, "sector", None),
            P("region", "sector", None, None),
            P("region", None, None, None, None),
            P("region", None, "sector", None),
            P("region", None, None),
        ),
        out_specs=(P("region", None, "sector", None), P("region", "sector", None)),
        check_vma=False,
    )
```

```python
import functools

import jax
import jax.numpy as jnp
from jax import lax
from jax.experimental import pallas as pl
from jax.experimental.pallas import tpu as pltpu
from jax.sharding import PartitionSpec as P

GROUP = 16
LANES = 128
HALVES = 2
CHUNKS = 4
EDGE_FROM = 2
AHEAD = 4
LATE_AFTER = 7
SHIFTS = 4
CROSS = (4, 6, 11, 12)
PRODUCT = (0, 1, 2, 3)
OWN_LATER = 2
ABSORB = 7
SPLIT = 4
LAG = 2
HOP = 2
VMEM_LIMIT = 60 * 1024 * 1024


def shifted(block, axis, distance):
    devices = range(lax.axis_size(axis))
    route = [((i - distance) % len(devices), i) for i in devices]
    return lax.ppermute(block, axis, route)


MESH = pl.DeviceIdType.MESH


def carried_into(mix_ref, env_ref, site_ref, out_ref):
    width, rows, bond = env_ref.shape
    _, states, _, columns = site_ref.shape
    sub = columns // 2
    tile = min(rows, LANES)
    mix = mix_ref[...]
    mix_high = mix.astype(jnp.bfloat16)
    mix_low = (mix - mix_high.astype(jnp.float32)).astype(jnp.bfloat16)
    dot = functools.partial(jnp.dot, preferred_element_type=jnp.float32)
    step = width // CHUNKS

    def rows_of(i, carry):
        top = pl.multiple_of(i * tile, tile)
        env = env_ref[:, pl.ds(top, tile)].reshape(width * tile, bond)
        half_done = [
            dot(env, site_ref[:, t].reshape(bond, columns)).reshape(width, tile, columns)
            for t in range(states)
        ]
        for g in range(tile // GROUP):
            span = slice(g * GROUP, (g + 1) * GROUP)
            x = jnp.concatenate(
                [h[:, span].reshape(width * GROUP, columns) for h in half_done], axis=0
            )
            high = x.astype(jnp.bfloat16)
            low = (x - high.astype(jnp.float32)).astype(jnp.bfloat16)
            y = dot(mix_high, high) + dot(mix_high, low) + dot(mix_low, high)
            y = y.astype(jnp.bfloat16).reshape(width, states, GROUP, columns)
            for i in range(CHUNKS):
                for j in range(2):
                    out_ref[i, j, :, :, pl.ds(top + g * GROUP, GROUP), :] = y[
                        i * step : (i + 1) * step, :, :, j * sub : (j + 1) * sub
                    ]
        return carry

    lax.fori_loop(0, rows // tile, rows_of, 0)


def inner(parts, device):
    z = device // 2
    return jnp.logical_and(z > 0, z < parts // 2 - 1)


def waits(parts, source, target, q):
    same = lax.rem(source + target, 2) == 0
    return jnp.logical_and(same, jnp.logical_or(inner(parts, source), q >= EDGE_FROM))


def greet(parts):
    me = lax.axis_index("sector")
    barrier = pltpu.get_barrier_semaphore()
    for d in range(1, parts):
        pl.semaphore_signal(
            barrier, inc=1, device_id={"sector": lax.rem(me + d, parts)}, device_id_type=MESH
        )
    return barrier


def remote(src, dst, send, recv, target):
    return pltpu.make_async_remote_copy(
        src_ref=src, dst_ref=dst, send_sem=send, recv_sem=recv,
        device_id=target, device_id_type=MESH,
    )


def head_kernel(
    mix_ref, right_hbm, site_hbm, bond_hbm, left_hbm,
    gathered, moved, landed, carried, late,
    right, bond_ref, blocks, left, tiles, outs, own,
    shift_send, shift_recv, site_send, site_recv,
    block_send, block_recv, swap_send, swap_recv, out_sem, tile_sem, local_sem, own_sem,
):

    _, parts, states, _, _ = gathered.shape
    width, rows, bond = right_hbm.shape
    columns = bond // parts
    line = parts // 2
    me = lax.axis_index("sector")
    z, y = me // 2, lax.rem(me, 2)
    regions = lax.axis_size("region")
    region = lax.axis_index("region")
    before = lax.rem(region + regions - 1, regions)
    after = lax.rem(region + 1, regions)
    part_rows = rows // SHIFTS
    twin = 2 * z + 1 - y

    barrier = greet(parts)
    for other in (before, after):
        pl.semaphore_signal(barrier, inc=1, device_id={"region": other}, device_id_type=MESH)

    def shift(q):
        span = pl.ds(q * part_rows, part_rows)
        return remote(
            right_hbm.at[:, span], right.at[:, span], shift_send.at[q], shift_recv.at[q],
            {"region": before},
        )

    def hop(way, source, p, t, target, first=False):
        there = gathered.at[p, source, t]
        return remote(
            own.at[p, t] if first else there, there,
            site_send.at[way, p, source, t], site_recv.at[p, source, t], {"sector": target},
        )

    def outward(source, p, t, first, ways, act):
        for way in ways:
            there = {0: me + 2, 1: me - 2, 2: twin}[way]
            if way == 2:
                act(hop(way, source, p, t, there, first))
            else:
                inside = z + 1 < line if way == 0 else z >= 1

                @pl.when(inside)
                def _():
                    act(hop(way, source, p, t, there, first))

    def target_of(d):
        return lax.rem(me + 1 + d, parts)

    def block(q, d):
        return remote(
            blocks.at[q, d], moved.at[q, me], block_send.at[q, d], block_recv.at[q, me],
            {"sector": target_of(d)},
        )

    def block_in(q, d):
        source = target_of(d)
        return remote(
            blocks.at[q, d], moved.at[q, source], block_send.at[q, d], block_recv.at[q, source],
            {"sector": source},
        )

    def held(q, d):
        return waits(parts, me, target_of(d), q)

    def put_off(q, d):
        return pltpu.make_async_copy(
            blocks.at[q, d], late.at[q, target_of(d) // 2], block_send.at[q, d]
        )

    def own_block(q):
        return pltpu.make_async_copy(
            blocks.at[q, parts - 1], moved.at[q, me], block_send.at[q, parts - 1]
        )

    def start(copy):
        copy.start()

    def settle(copy):
        copy.wait_send()

    sub = columns // HALVES

    def sort_site(p, j):
        return pltpu.make_async_copy(
            site_hbm.at[:, :, pl.ds(j * columns + p * sub, sub)],
            own.at[p, :, :, pl.ds(j * sub, sub)],
            own_sem.at[p, j],
        )

    for p in range(HALVES):
        for j in range(parts):
            sort_site(p, j).start()
    pl.semaphore_wait(barrier, parts + 1)
    for q in range(SHIFTS):
        shift(q).start()
    for j in range(parts):
        sort_site(0, j).wait()
    for t in range(states):
        outward(me, 0, t, True, (0, 1, 2), start)
    for p in range(1, HALVES):
        for j in range(parts):
            sort_site(p, j).wait()
    load_bond = pltpu.make_async_copy(bond_hbm, bond_ref, local_sem.at[0])
    load_bond.start()
    load_left = pltpu.make_async_copy(left_hbm, left, local_sem.at[1])
    load_left.start()
    keep_site = [
        pltpu.make_async_copy(own.at[p], gathered.at[p, me], local_sem.at[2 + p])
        for p in range(HALVES)
    ]
    for copy in keep_site:
        copy.start()
    load_bond.wait()

    def product(q):
        shift(q).wait_recv()
        span = pl.ds(q * part_rows, part_rows)
        x = right[:, span].reshape(width * part_rows, bond)

        def step(d, carry):
            j = target_of(d)
            out = lax.dot_general(
                x,
                bond_ref[pl.ds(pl.multiple_of(j * columns, columns), columns), :],
                (((1,), (1,)), ((), ())),
                preferred_element_type=jnp.float32,
            )
            blocks[q, d] = out.astype(jnp.bfloat16).reshape(width, part_rows, columns)
            return carry

        lax.fori_loop(0, parts, step, 0)

    def dispatch(q, cross):
        def step(d, carry):
            same = lax.rem(target_of(d), 2) == y

            @pl.when(jnp.logical_not(same) if cross else jnp.logical_and(same, jnp.logical_not(held(q, d))))
            def _():
                block(q, d).start()

            if not cross:

                @pl.when(held(q, d))
                def _():
                    put_off(q, d).start()

            return carry

        lax.fori_loop(0, parts - 1, step, 0)
        if not cross:
            own_block(q).start()

    hops = (line - 1) * states
    ticks = HALVES * hops

    def relayed(i, act, receive):
        p, distance, t = i // hops, lax.rem(i, hops) // states + 1, lax.rem(i, states)
        for way, source in ((0, me - 2 * distance), (1, me + 2 * distance)):
            there = z >= distance if way == 0 else z + distance < line

            @pl.when(there)
            def _():
                if receive:
                    hop(way, source, p, t, twin).wait_recv()
                outward(source, p, t, False, (way, 2), act)

    def tile_copies(a):
        p, slot = a // line, lax.rem(a, 2)
        m = lax.rem(z + 1 + a, line)
        span = pl.ds(pl.multiple_of(m * columns, columns), columns)
        mine = pltpu.make_async_copy(
            own.at[p, :, :, span], tiles.at[slot, me], tile_sem.at[slot, parts - 1]
        )
        return mine, lambda d: pltpu.make_async_copy(
            gathered.at[p, target_of(d), :, :, span], tiles.at[slot, target_of(d)],
            tile_sem.at[slot, d],
        )

    def each(count, act):
        def step(d, carry):
            act(d)
            return carry

        lax.fori_loop(0, count, step, 0)

    def load_tile(a):
        mine, other = tile_copies(a)
        mine.start()
        each(parts - 1, lambda d: other(d).start())

    def have_tile(a):
        mine, other = tile_copies(a)
        mine.wait()
        each(parts - 1, lambda d: other(d).wait())

    def swap(a, i, j):
        to = 2 * lax.rem(z + 1 + a, line) + j
        return to, remote(
            outs.at[a, i, j], landed.at[i, me], swap_send.at[i, to], swap_recv.at[i, me],
            {"sector": to},
        ), pltpu.make_async_copy(outs.at[a, i, j], landed.at[i, me], swap_send.at[i, to])

    def store(a, i, j):
        to = 2 * lax.rem(z + 1 + a, line) + j
        slot = lax.rem(a, 2)
        return pltpu.make_async_copy(
            outs.at[line + slot, i, j], carried.at[i, to], out_sem.at[slot, i, j]
        )

    def absorb(a):
        p = a // line

        @pl.when(lax.rem(a, line) == 0)
        def _():
            for other in range(line):
                for t in range(states):
                    hop(2, 2 * other + 1 - y, p, t, twin).wait_recv()
            load_tile(a)

        have_tile(a)

        @pl.when(lax.rem(a, line) < line - 1)
        def _():
            load_tile(a + 1)

        @pl.when(a >= line + 2)
        def _():
            for i in range(CHUNKS):
                for j in range(2):
                    store(a - 2, i, j).wait()

        slot = jnp.where(p == 0, a, line + lax.rem(a, 2))
        carried_into(mix_ref, left, tiles.at[lax.rem(a, 2)], outs.at[slot])
        for i in range(CHUNKS):
            for j in range(2):

                @pl.when(p == 0)
                def _():
                    to, far, near = swap(a, i, j)

                    @pl.when(to == me)
                    def _():
                        near.start()

                    @pl.when(to != me)
                    def _():
                        far.start()

                @pl.when(p > 0)
                def _():
                    store(a, i, j).start()

    def tick(i, carry):
        @pl.when(i < ticks)
        def _():
            relayed(i, start, True)

        @pl.when(i == OWN_LATER)
        def _():
            for p in range(1, HALVES):
                for t in range(states):
                    outward(me, p, t, True, (0, 1, 2), start)

        for q in range(SHIFTS):

            @pl.when(i == PRODUCT[q])
            def _():
                product(q)
                dispatch(q, False)

            @pl.when(i == CROSS[q])
            def _():
                dispatch(q, True)

        @pl.when(i == ABSORB)
        def _():
            load_left.wait()

        early = jnp.logical_and(i >= ABSORB, i < ABSORB + line)

        @pl.when(jnp.logical_or(early, i >= ticks))
        def _():
            absorb(jnp.where(i >= ticks, i - ticks + line, i - ABSORB))

        return carry

    lax.fori_loop(0, ticks + line, tick, 0)

    for copy in keep_site:
        copy.wait()
    for q in range(SHIFTS):
        shift(q).wait_send()
    for p in range(HALVES):
        for t in range(states):
            outward(me, p, t, True, (0, 1, 2), settle)
    each(ticks, lambda i: relayed(i, settle, False))

    def finish(i):
        q, d = i // (parts - 1), lax.rem(i, parts - 1)

        @pl.when(held(q, d))
        def _():
            put_off(q, d).wait()

        @pl.when(jnp.logical_not(held(q, d)))
        def _():
            block(q, d).wait_send()

        @pl.when(jnp.logical_not(waits(parts, target_of(d), me, q)))
        def _():
            block_in(q, d).wait_recv()

    each(SHIFTS * (parts - 1), finish)
    for q in range(SHIFTS):
        own_block(q).wait()

    def swapped(a):
        for i in range(CHUNKS):
            for j in range(2):
                to, far, near = swap(a, i, j)

                @pl.when(to == me)
                def _():
                    near.wait()

                @pl.when(to != me)
                def _():
                    far.wait_send()
                    remote(
                        outs.at[a, i, j], landed.at[i, to], swap_send.at[i, to],
                        swap_recv.at[i, to], {"sector": to},
                    ).wait_recv()

    each(line, swapped)
    for a in range(2 * line - 2, 2 * line):
        for i in range(CHUNKS):
            for j in range(2):
                store(a, i, j).wait()


def head(env_left, site, mpo, env_right, bond_tensor, parts):
    width, rows, bond = env_left.shape
    states, depth, _ = site.shape
    columns = bond // parts
    eye = jnp.eye(GROUP, dtype=jnp.float32)
    side = width * states * GROUP
    mix = jnp.einsum("vwst,ij->wsitvj", mpo, eye, precision=lax.Precision.HIGHEST).reshape(side, side)
    part_rows = rows // SHIFTS
    carried = (width // CHUNKS, states, rows, columns // HALVES)
    bf16 = jnp.bfloat16
    anywhere = pl.BlockSpec(memory_space=pl.ANY)
    dma = pltpu.SemaphoreType.DMA
    return pl.pallas_call(
        head_kernel,
        in_specs=[pl.BlockSpec(memory_space=pltpu.VMEM)] + [anywhere] * 4,
        out_specs=[anywhere] * 5,
        out_shape=[
            jax.ShapeDtypeStruct((HALVES, parts, states, depth, bond // HALVES), bf16),
            jax.ShapeDtypeStruct((SHIFTS, parts, width, part_rows, columns), bf16),
            jax.ShapeDtypeStruct((CHUNKS, parts) + carried, bf16),
            jax.ShapeDtypeStruct((CHUNKS, parts) + carried, bf16),
            jax.ShapeDtypeStruct((SHIFTS, parts // 2, width, part_rows, columns), bf16),
        ],
        scratch_shapes=[
            pltpu.VMEM((width, rows, bond), bf16),
            pltpu.VMEM((bond, bond), bf16),
            pltpu.VMEM((SHIFTS, parts, width, part_rows, columns), bf16),
            pltpu.VMEM((width, rows, bond), bf16),
            pltpu.VMEM((2, parts, states, depth, columns), bf16),
            pltpu.VMEM((parts // 2 + 2, CHUNKS, 2) + carried, bf16),
            pltpu.VMEM((HALVES, states, depth, bond // HALVES), bf16),
            dma((SHIFTS,)),
            dma((SHIFTS,)),
            dma((3, HALVES, parts, states)),
            dma((HALVES, parts, states)),
            dma((SHIFTS, parts)),
            dma((SHIFTS, parts)),
            dma((CHUNKS, parts)),
            dma((CHUNKS, parts)),
            dma((2, CHUNKS, 2)),
            dma((2, parts)),
            dma((2 + HALVES,)),
            dma((HALVES, parts)),
        ],
        compiler_params=pltpu.CompilerParams(
            vmem_limit_bytes=VMEM_LIMIT, collective_id=0, has_side_effects=True
        ),
        cost_estimate=pl.CostEstimate(
            flops=3 * width * rows * bond * bond * states,
            bytes_accessed=128 * 1024 * 1024,
            transcendentals=0,
        ),
    )(mix, env_right, site, bond_tensor, env_left)


def rest_kernel(
    gathered, moved_before, landed_first, carried, late,
    env_out, image_out, landed, moved,
    x, turned, env, bond_in, keep, pair_out, pair_in, line_out, line_in, done,
    swap_send, swap_recv, late_send, late_recv, pair_send, pair_recv, line_send, line_recv,
    load_sem, env_sem, out_sem,
):
    _, parts, states, depth, _ = gathered.shape
    _, _, count, _, _, sub = landed.shape
    width, columns, bond = env_out.shape
    part_rows = moved.shape[3]
    line = parts // 2
    group = bond_in.shape[1]
    splits = parts // group
    steps = SHIFTS * splits
    me = lax.axis_index("sector")
    z, y = me // 2, lax.rem(me, 2)
    twin = 2 * z + 1 - y

    pl.semaphore_wait(greet(parts), parts - 1)

    def swap(b, d, receiving=False):
        j = lax.rem(me + 1 + d, parts)
        owner = j if receiving else me
        return remote(
            carried.at[b, j], landed.at[b, owner], swap_send.at[b, d], swap_recv.at[b, owner],
            {"sector": j},
        )

    def dispatch(b):
        def step(d, carry):
            swap(b, d).start()
            return carry

        lax.fori_loop(0, parts - 1, step, 0)

    def fill(b, d, first):
        n = lax.rem(me + 1 + d, parts)
        origin = landed_first if first else landed
        return pltpu.make_async_copy(origin.at[b, n], x.at[n], load_sem.at[d])

    def fill_own(b, first):
        origin = landed_first if first else carried
        return pltpu.make_async_copy(origin.at[b, me], x.at[me], load_sem.at[parts - 1])

    def turn(n, carry):
        for s in range(states):
            at = pl.multiple_of((n * states + s) * depth, depth)
            for v in range(count):
                turned[v * sub : (v + 1) * sub, pl.ds(at, depth)] = x[n, v, s].T
        return carry

    def env_body(*refs):
        out_ref = refs[-1]
        tile = out_ref.shape[-1]
        totals = []
        for site_ref in refs[:-1]:
            site = site_ref[0].reshape(parts * states * depth, site_ref.shape[-1])
            totals.append(
                jnp.dot(turned[...], site, preferred_element_type=jnp.float32)
                .astype(jnp.bfloat16)
                .reshape(count, sub, site_ref.shape[-1])
            )
        for k in range(tile // sub):
            piece = slice(k // HALVES * sub, (k // HALVES + 1) * sub)
            out_ref[:, :, k * sub : (k + 1) * sub] = totals[k % HALVES][:, :, piece]

    def spot(ref, i):
        p, b = i // CHUNKS, lax.rem(i, CHUNKS)
        return ref.at[
            pl.ds(b * count, count), pl.ds(pl.multiple_of(p * sub, sub), sub)
        ]

    def reload(i):
        return pltpu.make_async_copy(spot(env_out, i), spot(env, i), env_sem.at[i])

    def late_block(q, k, receiving=False):
        to = lax.rem(z + 1 + k, line)
        other = 2 * to + y
        owner = other if receiving else me
        return remote(
            late.at[q, to], moved.at[q, owner], late_send.at[q, k],
            late_recv.at[q, owner // 2], {"sector": other},
        )

    def late_blocks(q, act, receiving=False):
        for k in range(line - 1):
            other = 2 * lax.rem(z + 1 + k, line) + y

            @pl.when(waits(parts, other, me, q) if receiving else waits(parts, me, other, q))
            def _():
                act(late_block(q, k, receiving))

    tile = 2 * LANES
    for b in range(min(AHEAD, CHUNKS)):
        dispatch(b)

    def advance(i, carry):
        b = lax.rem(i, CHUNKS)
        for first in (True, False):

            @pl.when(i < CHUNKS if first else i >= CHUNKS)
            def _():
                fill_own(b, first).start()

                def collect(d, carry):
                    if not first:
                        swap(b, d, True).wait_recv()
                    fill(b, d, first).start()
                    return carry

                lax.fori_loop(0, parts - 1, collect, 0)

        @pl.when(jnp.logical_and(i >= CHUNKS, b + AHEAD < CHUNKS))
        def _():
            dispatch(b + AHEAD)

        @pl.when(i == LATE_AFTER)
        def _():
            for q in range(2):
                late_blocks(q, lambda copy: copy.start())

        def filled(d, carry):
            fill(b, d, True).wait()
            return carry

        lax.fori_loop(0, parts - 1, filled, 0)
        fill_own(b, True).wait()
        lax.fori_loop(0, parts, turn, 0)
        pltpu.emit_pipeline(
            env_body,
            grid=(bond // (tile * HALVES),),
            in_specs=[
                pl.BlockSpec(
                    (1, parts, states, depth, tile),
                    functools.partial(lambda p, j: (p, 0, 0, 0, j), p),
                )
                for p in range(HALVES)
            ],
            out_specs=[pl.BlockSpec((count, sub, tile * HALVES), lambda j: (0, 0, j))],
        )(*[gathered] * HALVES, spot(env_out, i))
        reload(i).start()
        return carry

    lax.fori_loop(0, HALVES * CHUNKS, advance, 0)
    for i in range(HALVES * CHUNKS):
        reload(i).wait()

    def pair_copy(u):
        return remote(
            pair_out.at[u], pair_in.at[u], pair_send.at[u], pair_recv.at[u], {"sector": twin}
        )

    def line_copy(u, t, way):
        slot = t + 1 if way == 0 else t
        return remote(
            line_out.at[u, t], line_in.at[u, slot], line_send.at[u, t], line_recv.at[u, slot],
            {"sector": me + 2 if way == 0 else me - 2},
        )

    def dot(a, b):
        return jnp.dot(a, b, preferred_element_type=jnp.float32)

    def take(u, i):
        q, n, slot = u // splits, lax.rem(u, splits) * group + i, lax.rem(u, 2)
        return pltpu.make_async_copy(
            moved.at[q, n], bond_in.at[slot, i], load_sem.at[slot * group + i]
        )

    def fetch(u):
        @pl.when(lax.rem(u, splits) == 0)
        def _():
            late_blocks(u // splits, lambda copy: copy.wait_recv(), True)

        for i in range(group):
            take(u, i).start()

    def image(u):
        for i in range(group):
            take(u, i).wait()

        @pl.when(u + 1 < steps)
        def _():
            fetch(u + 1)

        left = jnp.concatenate(
            [
                bond_in[lax.rem(u, 2), :, w].reshape(group * part_rows, columns)
                for w in range(width)
            ],
            axis=1,
        )

        def right(j):
            at = pl.multiple_of(j * columns, columns)
            return env[:, :, pl.ds(at, columns)].reshape(width * columns, columns)

        for t in range(line):
            pair_out[u, t] = dot(left, right(2 * t + 1 - y)).astype(jnp.bfloat16)
        for t in range(line):
            keep[u, t] = dot(left, right(2 * t + y))
        pair_copy(u).start()

    def paired(u):
        pair_copy(u).wait_recv()
        keep[u] = keep[u] + pair_in[u].astype(jnp.float32)

    def relay(s, way):
        first = z if way == 0 else line - 1 - z
        u = s - LAG - HOP * first
        live = jnp.logical_and(u >= 0, u < steps)
        for t in range(line):
            sends = jnp.logical_and(live, t > z if way == 0 else t < z)

            @pl.when(jnp.logical_and(sends, first == 0))
            def _():
                line_out[u, t] = keep[u, t].astype(jnp.bfloat16)

            @pl.when(jnp.logical_and(sends, first > 0))
            def _():
                slot = t + 1 if way == 0 else t
                line_copy(u, t, way).wait_recv()
                line_out[u, t] = (
                    keep[u, t] + line_in[u, slot].astype(jnp.float32)
                ).astype(jnp.bfloat16)

    def send_on(s, way):
        first = z if way == 0 else line - 1 - z
        u = s - LAG - HOP * first
        live = jnp.logical_and(u >= 0, u < steps)
        for t in range(line):

            @pl.when(jnp.logical_and(live, t > z if way == 0 else t < z))
            def _():
                line_copy(u, t, way).start()

    def result(u):
        return pltpu.make_async_copy(done.at[u], image_out.at[u], out_sem.at[u])

    def total(u):
        @pl.when(z > 0)
        def _():
            line_copy(u, z, 0).wait_recv()
            keep[u, z] = keep[u, z] + line_in[u, z + 1].astype(jnp.float32)

        @pl.when(z < line - 1)
        def _():
            line_copy(u, z, 1).wait_recv()
            keep[u, z] = keep[u, z] + line_in[u, z].astype(jnp.float32)

        done[u] = keep[u, z].astype(jnp.bfloat16)

    last = LAG + HOP * (line - 2) + 1

    def pass_on(s, carry):
        for q in range(2, SHIFTS):

            @pl.when(s == (q - 2) * splits + 1)
            def _():
                late_blocks(q, lambda copy: copy.start())

        @pl.when(s < steps)
        def _():
            image(s)

        @pl.when(jnp.logical_and(s >= LAG, s < steps + LAG))
        def _():
            paired(s - LAG)

        relay(s, 0)
        relay(s, 1)

        @pl.when(s >= last)
        def _():
            total(s - last)

        send_on(s, 0)
        send_on(s, 1)

        @pl.when(s >= last)
        def _():
            result(s - last).start()

        return carry

    fetch(0)
    lax.fori_loop(0, steps + last, pass_on, 0)

    def sent(b, carry):
        def step(d, carry):
            swap(b, d).wait_send()
            return carry

        return lax.fori_loop(0, parts - 1, step, carry)

    lax.fori_loop(0, CHUNKS, sent, 0)

    for q in range(SHIFTS):
        late_blocks(q, lambda copy: copy.wait_send())

    def ended(u, carry):
        pair_copy(u).wait_send()
        result(u).wait()
        for t in range(line):
            @pl.when(t > z)
            def _():
                line_copy(u, t, 0).wait_send()

            @pl.when(t < z)
            def _():
                line_copy(u, t, 1).wait_send()

        return carry

    lax.fori_loop(0, steps, ended, 0)


def rest_of(gathered, moved, landed, carried, late):
    _, parts, states, depth, _ = gathered.shape
    _, _, count, _, _, sub = carried.shape
    width, columns = count * CHUNKS, sub * HALVES
    bond = parts * columns
    part_rows = moved.shape[3]
    line = parts // 2
    group = max(parts // SPLIT, 1)
    steps = SHIFTS * (parts // group)
    block = (group * part_rows, columns)
    anywhere = pl.BlockSpec(memory_space=pl.ANY)
    dma = pltpu.SemaphoreType.DMA
    bf16 = jnp.bfloat16
    return pl.pallas_call(
        rest_kernel,
        in_specs=[anywhere] * 5,
        out_specs=[anywhere] * 4,
        input_output_aliases={1: 3},
        out_shape=[
            jax.ShapeDtypeStruct((width, columns, bond), bf16),
            jax.ShapeDtypeStruct((steps,) + block, bf16),
            jax.ShapeDtypeStruct(carried.shape, bf16),
            jax.ShapeDtypeStruct(moved.shape, bf16),
        ],
        scratch_shapes=[
            pltpu.VMEM(carried.shape[1:], bf16),
            pltpu.VMEM((count * sub, parts * states * depth), bf16),
            pltpu.VMEM((width, columns, bond), bf16),
            pltpu.VMEM((2, group, width, part_rows, columns), bf16),
            pltpu.VMEM((steps, line) + block, jnp.float32),
            pltpu.VMEM((steps, line) + block, bf16),
            pltpu.VMEM((steps, line) + block, bf16),
            pltpu.VMEM((steps, line) + block, bf16),
            pltpu.VMEM((steps, line + 1) + block, bf16),
            pltpu.VMEM((steps,) + block, bf16),
            dma((CHUNKS, parts)),
            dma((CHUNKS, parts)),
            dma((SHIFTS, line)),
            dma((SHIFTS, line)),
            dma((steps,)),
            dma((steps,)),
            dma((steps, line)),
            dma((steps, line + 1)),
            dma((parts,)),
            dma((HALVES * CHUNKS,)),
            dma((steps,)),
        ],
        compiler_params=pltpu.CompilerParams(
            vmem_limit_bytes=VMEM_LIMIT, collective_id=1, has_side_effects=True
        ),
        cost_estimate=pl.CostEstimate(
            flops=3 * width * columns * parts * states * depth * bond,
            bytes_accessed=128 * 1024 * 1024,
            transcendentals=0,
        ),
    )(gathered, moved, landed, carried, late)


def local(env_left, site_tensor, mpo_tensor, env_right, bond_tensor):
    parts = lax.axis_size("sector")
    _, rows, bond = env_left.shape[1:]
    columns = bond // parts
    site = site_tensor[0].transpose(1, 0, 2)
    gathered, moved, landed, carried, late = head(
        env_left[0], site, mpo_tensor[0], env_right[0], bond_tensor[0], parts,
    )
    env_new, image, *_ = rest_of(gathered, moved, landed, carried, late)
    image_rows = (
        image.reshape(SHIFTS, parts, rows // SHIFTS, columns)
        .transpose(3, 1, 0, 2)
        .reshape(columns, bond)
    )
    return (env_new[None], image_rows[None])


def plain_local(env_left, site_tensor, mpo_tensor, env_right, bond_tensor):
    width = env_left.shape[1]
    states = site_tensor.shape[2]
    gathered = lax.all_gather(site_tensor, "sector", axis=1, tiled=True)[0]
    half_done = jnp.einsum(
        "wak,ksc->wasc", env_left[0], gathered, preferred_element_type=jnp.float32
    )
    carried = jnp.einsum(
        "vwst,vatc->wsac", mpo_tensor[0], half_done, precision=lax.Precision.HIGHEST
    ).astype(jnp.bfloat16)
    carried = carried.reshape((width * states,) + carried.shape[2:])
    right_next = shifted(env_right, "region", -1)[0]
    bond_right = jnp.einsum(
        "wbc,kc->wbk", right_next, bond_tensor[0], preferred_element_type=jnp.float32
    ).astype(jnp.bfloat16)
    carried_moved = lax.all_to_all(carried, "sector", split_axis=2, concat_axis=1, tiled=True)
    bond_moved = lax.all_to_all(bond_right, "sector", split_axis=2, concat_axis=1, tiled=True)
    carried_moved = carried_moved.reshape((width, states) + carried_moved.shape[1:])
    env_new = jnp.einsum(
        "wsac,asb->wcb", carried_moved, gathered, preferred_element_type=jnp.float32
    ).astype(jnp.bfloat16)
    image_rows = lax.psum_scatter(
        jnp.einsum("wka,wbk->ab", env_new, bond_moved, preferred_element_type=jnp.float32),
        "sector",
        scatter_dimension=0,
        tiled=True,
    )
    return (env_new[None], image_rows.astype(jnp.bfloat16)[None])


def solution(mesh):
    def body(env_left, site_tensor, mpo_tensor, env_right, bond_tensor):
        width, rows, bond = env_left.shape[1:]
        columns = bond // mesh.shape["sector"]
        tiled = rows % LANES == 0 and columns % (HALVES * LANES) == 0 and width % CHUNKS == 0 and rows % (16 * SHIFTS) == 0
        tiled = tiled and mesh.shape["sector"] % 2 == 0 and mesh.shape["region"] > 2
        step = local if tiled else plain_local
        return step(env_left, site_tensor, mpo_tensor, env_right, bond_tensor)

    return jax.shard_map(
        body,
        mesh=mesh,
        in_specs=(
            P("region", None, "sector", None),
            P("region", "sector", None, None),
            P("region", None, None, None, None),
            P("region", None, "sector", None),
            P("region", None, None),
        ),
        out_specs=(P("region", None, "sector", None), P("region", "sector", None)),
        check_vma=False,
    )
```
